32 devices in a mesh: dp: 8 (over z, y), mp: 4 (over x, core).
Axes of the slice: x: 2, y: 2, z: 4, core: 2. Of those that a mesh axis runs over, the one named last changes fastest.
Arguments:
- tokens: bfloat16 [16384, 1024], P(('dp', 'mp')), may hold values from -6 to 6
- cotangent: bfloat16 [16384, 1024], P(('dp', 'mp')), may hold values from -6 to 6
- lengths: int32 [8, 4], P('dp'), may hold values from 1 to 1024, 2048 in all within a row
- key_mask: int32 [8, 2048], P('dp'), may hold values 0 or 1
- w_query: bfloat16 [1024, 1024], P('dp', 'mp'), may hold values from -0.1875 to 0.1875
- w_key: bfloat16 [1024, 1024], P('dp', 'mp'), may hold values from -0.1875 to 0.1875
- w_value: bfloat16 [1024, 1024], P('dp', 'mp'), may hold values from -0.1875 to 0.1875
- w_out: bfloat16 [1024, 1024], P('mp', 'dp'), may hold values from -0.1875 to 0.1875
- w_up: bfloat16 [1024, 4096], P('dp', 'mp'), may hold values from -0.1875 to 0.1875
- w_gate: bfloat16 [1024, 4096], P('dp', 'mp'), may hold values from -0.1875 to 0.1875
- w_down: bfloat16 [4096, 1024], P('mp', 'dp'), may hold values from -0.09375 to 0.09375
- s_qk: float32 [1024], P(('dp', 'mp')), may hold values from 0.7 to 1.4
- s_up: float32 [4096], P(('dp', 'mp')), may hold values from 0.5 to 1.5
- s_gate: float32 [4096], P(('dp', 'mp')), may hold values from 0.5 to 1.5
- alpha_attn: float32 [1024], P(('dp', 'mp')), may hold values from 0.1 to 0.6
- alpha_mlp: float32 [1024], P(('dp', 'mp')), may hold values from 0.1 to 0.6
Outputs:
- out_tokens: bfloat16 [16384, 1024], P(('dp', 'mp'))
- grad_tokens: float32 [16384, 1024], P(('dp', 'mp'))
- grad_query: float32 [1024, 1024], P('dp', 'mp')
- grad_key: float32 [1024, 1024], P('dp', 'mp')
- grad_value: float32 [1024, 1024], P('dp', 'mp')
- grad_out: float32 [1024, 1024], P('mp', 'dp')
- grad_up: float32 [1024, 4096], P('dp', 'mp')
- grad_gate: float32 [1024, 4096], P('dp', 'mp')
- grad_down: float32 [4096, 1024], P('mp', 'dp')
- grad_sqk: float32 [1024], P(('dp', 'mp'))
- grad_s_up: float32 [4096], P(('dp', 'mp'))
- grad_s_gate: float32 [4096], P(('dp', 'mp'))
- grad_alpha_attn: float32 [1024], P(('dp', 'mp'))
- grad_alpha_mlp: float32 [1024], P(('dp', 'mp'))
- grad_norm: float32 [], replicated
- mean_alphas: float32 [2], replicated
The draws below stay inside these ranges and needn't reach their ends.
Inputs may be any that keep to these rules, and one draw needn't show every extreme that they name: `lengths`: each row's 4 documents fill its 2048 slots in order; in each row the longest is exactly 1024.
All inputs are finite; a program needn't handle non-finite values. No bound on the sum of `key_mask` on one device may be relied on, other than what follows from the above.
Results may differ from the reference program's by a relative error of at most 0.018.
Values may be sent and summed in bfloat16 or wider, within the bound.
No kernel may reach another device: no remote copies, remote signals or barrier semaphores. Data moves between devices by JAX's collectives and lax.ppermute only.
A program may use at most 256 MiB of HBM per device.

```python
import math
import jax
import jax.numpy as jnp
import numpy as np
from jax import lax

D = 1024
HEADS = 16
FF = 4096
ROW = 2048
MOST_LEN = 1024
DOCS = 4
ROWS = 8
TOKENS = 16384


def with_ends(values, stream_key, low, high):
    place = [jax.random.randint(jax.random.fold_in(stream_key, axis), (), 0, length) for axis, length in enumerate(values.shape)]
    longest = values.shape.index(max(values.shape))
    beside = place[:longest] + [(place[longest] + 1) % values.shape[longest]] + place[longest + 1:]
    return values.at[tuple(place)].set(low).at[tuple(beside)].set(high)


def block_levels(own_key, dims, cuts, least, largest):
    level = 1.0
    for dim, parts in cuts:
        steps = jax.random.uniform(jax.random.fold_in(jax.random.fold_in(own_key, 6), dim), (parts,), jnp.float32, least / len(cuts), largest / len(cuts))
        level = level * jnp.repeat(jnp.exp(steps), dims[dim] // parts).reshape((-1,) + (1,) * (len(dims) - 1 - dim))
    return level


def split_up(number_of, total, limit, slope):
    weights = [(1 << 20) // math.isqrt(standing ** slope) + 1 for standing in range(2, number_of + 1)]
    surplus, given = total - limit - (number_of - 1), [1] * (number_of - 1)
    while surplus > 0:
        candidates = [i for i in range(number_of - 1) if given[i] < limit]
        pool, left = sum([weights[i] for i in candidates]), surplus
        for i in candidates:
            extra = min(limit - given[i], max(1, left * weights[i] // pool), surplus)
            given[i] = given[i] + extra
            surplus = surplus - extra
    return np.array([limit] + given)


def uneven_parts(stream_key, amount, total, most, skew):
    if amount == 2:
        one = jax.random.randint(stream_key, (), max(1, total - most), min(most, total - 1) + 1)
        return jnp.stack([one, total - one])
    sizes = jnp.asarray(split_up(amount, total, most, skew), jnp.int32)
    pairs = (amount - 1) // 2
    giver, sink = sizes[1:1 + 2 * pairs:2], sizes[2:2 + 2 * pairs:2]
    room = jnp.minimum(giver - 1, most - sink)
    moved = jax.random.randint(jax.random.fold_in(stream_key, 1), (pairs,), 0, 1 << 20) % (room + 1)
    sizes = sizes.at[1:1 + 2 * pairs:2].set(giver - moved).at[2:2 + 2 * pairs:2].set(sink + moved)
    return sizes[jax.random.permutation(jax.random.fold_in(stream_key, 2), amount)]


def gaussian(own_key, shape, width, bound, shards=(), kind=jnp.bfloat16):
    factor_of = block_levels(own_key, shape, shards, -0.22, 0.18) if shards else 1.0
    entries = jax.random.normal(own_key, shape, jnp.float32) * width * factor_of
    return jnp.minimum(jnp.maximum(entries, -bound), bound).astype(kind)


def setup_inputs(seed: int = 0) -> dict:
    seeds = jax.random.split(jax.random.key(seed), 17)
    return {
        "tokens": gaussian(seeds[0], (TOKENS, D), 1.0, 6.0, ((0, 32),)),
        "cotangent": gaussian(seeds[1], (TOKENS, D), 1.0, 6.0, ((0, 32),)),
        "lengths": jax.vmap(lambda own: uneven_parts(own, DOCS, ROW, MOST_LEN, 2))(jax.random.split(seeds[2], ROWS)).reshape((ROWS, DOCS)).astype(jnp.int32),
        "key_mask": with_ends((jax.random.randint(seeds[3], (ROWS, ROW), 0, 8) < 7).astype(jnp.int32), jax.random.fold_in(seeds[3], 1), 0, 1),
        "w_query": gaussian(seeds[4], (D, D), D ** -0.5, 0.1875, ((0, 8), (1, 4))),
        "w_key": gaussian(seeds[5], (D, D), D ** -0.5, 0.1875, ((0, 8), (1, 4))),
        "w_value": gaussian(seeds[6], (D, D), D ** -0.5, 0.1875, ((0, 8), (1, 4))),
        "w_out": gaussian(seeds[7], (D, D), D ** -0.5, 0.1875, ((0, 4), (1, 8))),
        "w_up": gaussian(seeds[8], (D, FF), D ** -0.5, 0.1875, ((0, 8), (1, 4))),
        "w_gate": gaussian(seeds[9], (D, FF), D ** -0.5, 0.1875, ((0, 8), (1, 4))),
        "w_down": gaussian(seeds[10], (FF, D), FF ** -0.5, 0.09375, ((0, 4), (1, 8))),
        "s_qk": jnp.clip(0.7 + 0.7 * jax.random.uniform(seeds[11], (D,), jnp.float32) ** block_levels(seeds[11], (D,), ((0, 32),), -0.2, 0.2), 0.7, 1.4),
        "s_up": jnp.clip(0.5 + 1.0 * jax.random.uniform(seeds[12], (FF,), jnp.float32) ** block_levels(seeds[12], (FF,), ((0, 32),), -0.2, 0.2), 0.5, 1.5),
        "s_gate": jnp.clip(0.5 + 1.0 * jax.random.uniform(seeds[13], (FF,), jnp.float32) ** block_levels(seeds[13], (FF,), ((0, 32),), -0.2, 0.2), 0.5, 1.5),
        "alpha_attn": jnp.clip(jnp.exp(math.log(0.6) - 1.7917595 * jax.random.uniform(seeds[14], (D,), jnp.float32) ** block_levels(seeds[14], (D,), ((0, 32),), -0.2, 0.2)), 0.1, 0.6),
        "alpha_mlp": jnp.clip(jnp.exp(math.log(0.6) - 1.7917595 * jax.random.uniform(seeds[15], (D,), jnp.float32) ** block_levels(seeds[15], (D,), ((0, 32),), -0.2, 0.2)), 0.1, 0.6),
    }


EPS = 1e-06
NEG = -1e+30

@jax.custom_vjp
def low(v):
    return lax.optimization_barrier(v.astype(jnp.bfloat16)).astype(jnp.float32)

@jax.custom_vjp
def low_back(v):
    return v

def low_keep(v):
    return (low(v), None)

def low_pass(kept, grad):
    return (grad,)

def back_keep(v):
    return (v, None)

def back_low(kept, grad):
    return (low(grad),)
low.defvjp(low_keep, low_pass)
low_back.defvjp(back_keep, back_low)

def matmul(left, right):
    return jnp.dot(left, right, precision=lax.Precision.HIGHEST)

def rms_rows(tensor):
    return tensor * lax.rsqrt(lax.optimization_barrier(jnp.mean(tensor * tensor, axis=-1, keepdims=True)) + EPS)

def rotate_half(tensor):
    middle = tensor.shape[-1] // 2
    return jnp.concatenate([-tensor[..., middle:], tensor[..., :middle]], axis=-1)

def rope_tables(positions, length):
    steps_even = jnp.arange(0, length, 2).astype(jnp.float32)
    inverse = jnp.power(jnp.float32(10000.0), -steps_even / length)
    angles = positions.astype(jnp.float32)[:, None] * inverse[None, :]
    angles = jnp.concatenate([angles, angles], axis=-1)
    return (jnp.cos(angles)[:, None, :], jnp.sin(angles)[:, None, :])

def row_layout(length_row, length):
    doc_ends = jnp.cumsum(length_row)
    slot_ids = jnp.arange(length, dtype=jnp.int32)
    passed = (slot_ids[:, None] >= doc_ends[None, :]).astype(jnp.int32)
    documents = lax.optimization_barrier(jnp.sum(passed, axis=1)).astype(jnp.int32)
    starts = lax.optimization_barrier(jnp.sum(passed * length_row[None, :], axis=1)).astype(jnp.int32)
    return (documents, slot_ids - starts)

def layer(x_row, params, documents, positions, mask_row):
    w_query, w_key, w_value, w_out, w_up, w_gate, w_down, s_qk, s_up, s_gate, alpha_attn, alpha_mlp = params
    length = x_row.shape[0]
    head_size = D // HEADS
    cosine, sine_vals = rope_tables(positions, head_size)

    def project(weight):
        raw_proj = low_back(matmul(x_row, weight)).reshape(length, HEADS, head_size)
        turned = raw_proj * cosine + rotate_half(raw_proj) * sine_vals
        return low(rms_rows(turned) * s_qk.reshape(HEADS, head_size))
    queries = project(w_query)
    keys_all = project(w_key)
    values_all = low_back(low(matmul(x_row, w_value))).reshape(length, HEADS, head_size)
    slot_ids = jnp.arange(length)
    allowed = (documents[:, None] == documents[None, :]) & (slot_ids[None, :] <= slot_ids[:, None])
    allowed = allowed & ((mask_row[None, :] == 1) | (slot_ids[None, :] == slot_ids[:, None]))
    scaling = head_size ** (-0.5)

    def one_head(head_items):
        query_head, key_head, value_head = head_items
        scores = low_back(matmul(query_head, key_head.T) * scaling)
        scores = jnp.where(allowed, scores, NEG)
        highest = lax.optimization_barrier(jnp.max(scores, axis=-1, keepdims=True))
        expo_vals = jnp.exp(scores - highest)
        probs = low(expo_vals / lax.optimization_barrier(jnp.sum(expo_vals, axis=-1, keepdims=True)))
        return matmul(probs, value_head)
    mixed = lax.map(jax.checkpoint(one_head), (queries.transpose(1, 0, 2), keys_all.transpose(1, 0, 2), values_all.transpose(1, 0, 2)))
    attended = low_back(low(mixed.transpose(1, 0, 2).reshape(length, D)))
    branch_attn = low_back(matmul(attended, w_out))
    h_attn = rms_rows(branch_attn)
    hidden_one = rms_rows(x_row + alpha_attn * (h_attn - x_row))
    hidden_low = low(hidden_one)
    up_proj = low_back(matmul(hidden_low, w_up))
    gate_proj = low_back(matmul(hidden_low, w_gate))
    inner_act = s_up * up_proj
    outer_act = s_gate * gate_proj
    activation = low(inner_act * (outer_act * jax.nn.sigmoid(outer_act)))
    branch_mlp = low_back(matmul(activation, w_down))
    h_mlp = rms_rows(branch_mlp)
    return rms_rows(hidden_one + alpha_mlp * (h_mlp - hidden_one))

def reference(tokens, cotangent, lengths, key_mask, w_query, w_key, w_value, w_out, w_up, w_gate, w_down, s_qk, s_up, s_gate, alpha_attn, alpha_mlp):
    params = (w_query.astype(jnp.float32), w_key.astype(jnp.float32), w_value.astype(jnp.float32), w_out.astype(jnp.float32), w_up.astype(jnp.float32), w_gate.astype(jnp.float32), w_down.astype(jnp.float32), s_qk.astype(jnp.float32), s_up.astype(jnp.float32), s_gate.astype(jnp.float32), alpha_attn.astype(jnp.float32), alpha_mlp.astype(jnp.float32))
    inputs = tokens.astype(jnp.float32).reshape(ROWS, ROW, D)
    cotangents = cotangent.astype(jnp.float32).reshape(ROWS, ROW, D)

    def one_row(carry, row_items):
        x_row, grad_row, length_row, mask_row = row_items
        documents, positions = row_layout(length_row, ROW)

        def forward(x_value, weights):
            return layer(x_value, weights, documents, positions, mask_row)
        result, pullback = jax.vjp(forward, x_row, params)
        grad_x, grad_weights = pullback(grad_row)
        summed = tuple((running + part for running, part in zip(carry, grad_weights)))
        return (summed, (result.astype(jnp.bfloat16), grad_x))
    start_sums = tuple((jnp.zeros_like(item) for item in params))
    totals, (outputs, grad_inputs) = lax.scan(one_row, start_sums, (inputs, cotangents, lengths, key_mask))
    squares = jnp.float32(0.0)
    for item in totals:
        squares = squares + jnp.sum(item * item)
    grad_norm = jnp.sqrt(squares)
    mean_alphas = jnp.stack([jnp.mean(params[10]), jnp.mean(params[11])])
    return (outputs.reshape(TOKENS, D), grad_inputs.reshape(TOKENS, D), totals[0], totals[1], totals[2], totals[3], totals[4], totals[5], totals[6], totals[7], totals[8], totals[9], totals[10], totals[11], grad_norm, mean_alphas)
```

```python
import functools

import jax
import jax.numpy as jnp
from jax import lax
from jax.experimental import pallas as pl
from jax.experimental.pallas import tpu as pltpu
from jax.sharding import PartitionSpec as P

D = 1024
HEADS = 16
HEAD = D // HEADS
EPS = 1e-06
BLOCK = 256
F32 = jnp.float32
BF16 = jnp.bfloat16


def rms_rows(tensor):
    factor = lax.rsqrt(jnp.mean(tensor * tensor, axis=-1, keepdims=True) + EPS)
    return (tensor * factor, factor)


def rms_back(incoming, normed, factor):
    return factor * (incoming - normed * jnp.mean(incoming * normed, axis=-1, keepdims=True))


def dot(left, right, left_dim=1, right_dim=0):
    return lax.dot_general(
        left, right, (((left_dim,), (right_dim,)), ((), ())), preferred_element_type=F32
    )


def swap(array, axis, bit):
    size = lax.axis_size(axis)
    return lax.ppermute(array, axis, [(i, i ^ bit) for i in range(size)])


def from_z(array, step):
    return lax.ppermute(
        array, "dp", [(((z + step) % 4) * 2 + y, z * 2 + y) for z in range(4) for y in range(2)]
    )


def to_z(array, step):
    return lax.ppermute(
        array, "dp", [(z * 2 + y, ((z + step) % 4) * 2 + y) for z in range(4) for y in range(2)]
    )


def gather(weight, axis, after):
    if lax.axis_size("dp") != 8:
        return lax.all_gather(weight, "dp", axis=axis, tiled=True), ()
    if after:
        weight = lax.optimization_barrier((weight,) + tuple(after))[0]
    parts = [from_z(weight, step) for step in (1, 2, 3)]
    half = jnp.concatenate([weight] + parts, axis=axis)
    other = swap(half, "dp", 1)
    return jnp.concatenate([half, other], axis=axis), tuple(parts)


def scatter(grad, axis):
    if lax.axis_size("dp") != 8:
        return lax.psum_scatter(grad.astype(F32), "dp", scatter_dimension=axis, tiled=True)
    size = grad.shape[axis] // 8
    mine = lax.slice_in_dim(grad, 0, 4 * size, axis=axis)
    theirs = lax.slice_in_dim(grad, 4 * size, 8 * size, axis=axis)
    half = mine.astype(F32) + swap(theirs.astype(BF16), "dp", 1).astype(F32)
    total = lax.slice_in_dim(half, 0, size, axis=axis)
    for step in (1, 2, 3):
        part = lax.slice_in_dim(half, step * size, (step + 1) * size, axis=axis)
        total = total + to_z(part.astype(BF16), step).astype(F32)
    return total


def reduce_pair(remote, local):
    rows = local.shape[0] // 2
    for_x = remote[:rows].astype(F32) + swap(remote[rows:].astype(BF16), "mp", 1).astype(F32)
    from_x = swap(for_x.astype(BF16), "mp", 2)
    mine = local[:rows].astype(F32) + swap(local[rows:].astype(BF16), "mp", 1).astype(F32)
    return mine + from_x.astype(F32)


def spread(own):
    local = jnp.concatenate([own, swap(own, "mp", 1)], axis=0)
    over_x = swap(own, "mp", 2)
    remote = jnp.concatenate([over_x, swap(over_x, "mp", 1)], axis=0)
    return local, remote


def pick_cols(array, table):
    rows, cols = array.shape

    def body(table_ref, in_ref, out_ref):
        out_ref[...] = in_ref[...]

    return pl.pallas_call(
        body,
        out_shape=jax.ShapeDtypeStruct(array.shape, array.dtype),
        grid_spec=pltpu.PrefetchScalarGridSpec(
            num_scalar_prefetch=1,
            grid=(8,),
            in_specs=[pl.BlockSpec((rows, cols // 8), lambda i, t: (0, t[i]))],
            out_specs=pl.BlockSpec((rows, cols // 8), lambda i, t: (0, i)),
        ),
        cost_estimate=pl.CostEstimate(
            flops=0, bytes_accessed=2 * array.size * array.dtype.itemsize, transcendentals=0
        ),
        name="pick_cols",
    )(table, array)


def rotate_half(tensor):
    width = tensor.shape[-1]
    lane = lax.broadcasted_iota(jnp.int32, tensor.shape, 1)
    ahead = pltpu.roll(tensor, width - HEAD // 2, 1)
    behind = pltpu.roll(tensor, HEAD // 2, 1)
    return jnp.where((lane & (HEAD - 1)) < HEAD // 2, -ahead, behind)


def head_mean(tensor):
    width = tensor.shape[-1]
    row = lax.broadcasted_iota(jnp.int32, (width, width), 0) // HEAD
    col = lax.broadcasted_iota(jnp.int32, (width, width), 1) // HEAD
    ones = jnp.where(row == col, 1.0 / HEAD, 0.0).astype(F32)
    return jnp.dot(tensor, ones, precision=lax.Precision.HIGHEST, preferred_element_type=F32)


def wide(table):
    return jnp.concatenate([table, table], axis=1)


def project_body(m_ref, x_ref, wq_ref, wk_ref, wv_ref, cos_ref, sin_ref, sqk_ref, *refs):
    q_ref, k_ref, v_ref, qr_ref, kr_ref = refs[-5:]
    rows = x_ref[...]
    cosine, sine = wide(cos_ref[...]), wide(sin_ref[...])
    scale = sqk_ref[0:1, :]
    for weight_ref, out_ref, rot_ref in ((wq_ref, q_ref, qr_ref), (wk_ref, k_ref, kr_ref)):
        raw = jnp.dot(rows, weight_ref[...], preferred_element_type=F32)
        turned = raw * cosine + rotate_half(raw) * sine
        rot_ref[...] = turned
        unit = turned * lax.rsqrt(head_mean(turned * turned) + EPS)
        out_ref[...] = (unit * scale).astype(BF16)
    v_ref[...] = jnp.dot(rows, wv_ref[...], preferred_element_type=F32).astype(BF16)


def project(place, x_rows, weights, cosine, sine, sqk, previous, first):
    rows, width = x_rows.shape[0], weights[0].shape[1]
    total = cosine.shape[0]
    per = total // 4 // BLOCK

    def row_block(i, m):
        return ((m[0] ^ (first + i // per)) * per + i % per, 0)

    any_spec = pl.BlockSpec(memory_space=pl.ANY)
    whole = pl.BlockSpec((x_rows.shape[1], width), lambda i, m: (0, 0))
    table = pl.BlockSpec((BLOCK, cosine.shape[1]), row_block)
    out = pl.BlockSpec((BLOCK, width), row_block)
    shapes = [jax.ShapeDtypeStruct((total, width), t) for t in (BF16, BF16, BF16, F32, F32)]
    extra = list(previous) if previous is not None else []
    return pl.pallas_call(
        project_body,
        out_shape=shapes,
        grid_spec=pltpu.PrefetchScalarGridSpec(
            num_scalar_prefetch=1,
            grid=(rows // BLOCK,),
            in_specs=[
                pl.BlockSpec((BLOCK, x_rows.shape[1]), lambda i, m: (i, 0)),
                whole,
                whole,
                whole,
                table,
                table,
                pl.BlockSpec((8, width), lambda i, m: (0, 0)),
            ]
            + [any_spec] * len(extra),
            out_specs=[out] * 5,
        ),
        input_output_aliases={8 + i: i for i in range(len(extra))},
        cost_estimate=pl.CostEstimate(
            flops=6 * rows * D * width, bytes_accessed=8 * rows * D, transcendentals=rows
        ),
        name="project",
    )(place, x_rows, *weights, cosine, sine, sqk, *extra)


def head_lanes(array, head):
    lane = lax.broadcasted_iota(jnp.int32, array.shape, 1)
    return jnp.where(lane // HEAD == head, array, jnp.zeros_like(array))


def stack_heads(array):
    heads = array.shape[1] // HEAD
    return jnp.concatenate([head_lanes(array, h) for h in range(heads)], axis=0)


def doc_start(meta_ref, docs, slots):
    start = jnp.zeros_like(slots)
    end = 0
    for i in range(docs):
        length = meta_ref[1 + i]
        end = end + length
        start = start + jnp.where(slots >= end, length, 0)
    return start


def attend_body(docs, meta_ref, q_ref, k_ref, v_ref, kpos_ref, o_ref, inv_ref, acc_ref, sum_ref):
    step = pl.program_id(0)
    heads = q_ref.shape[1] // HEAD
    base = step * BLOCK
    low = doc_start(meta_ref, docs, base) // BLOCK
    queries = stack_heads(q_ref[...] * jnp.bfloat16(HEAD**-0.5))
    rows = lax.broadcasted_iota(jnp.int32, (BLOCK, BLOCK), 0) + base
    starts = doc_start(meta_ref, docs, rows)
    acc_ref[...] = jnp.zeros_like(acc_ref)
    sum_ref[...] = jnp.zeros_like(sum_ref)

    def visit(block, allowed):
        at = pl.ds(pl.multiple_of(block * BLOCK, BLOCK), BLOCK)
        keys, vals = k_ref[at, :], v_ref[at, :]
        scores = dot(queries, keys, 1, 1)
        total = acc_ref[...]
        for h in range(heads):
            part = slice(h * BLOCK, (h + 1) * BLOCK)
            expo = jnp.where(allowed, jnp.exp(scores[part]), 0.0)
            sum_ref[part, :] += expo[:, :128] + expo[:, 128:]
            total = total + dot(expo.astype(BF16), head_lanes(vals, h))
        acc_ref[...] = total

    def off_diagonal(block, carry):
        at = pl.ds(pl.multiple_of(block * BLOCK, BLOCK), BLOCK)
        visit(block, kpos_ref[0:1, at] >= starts)
        return carry

    lax.fori_loop(low, step, off_diagonal, 0)
    cols = lax.broadcasted_iota(jnp.int32, (BLOCK, BLOCK), 1) + base
    at = pl.ds(pl.multiple_of(base, BLOCK), BLOCK)
    visit(step, ((kpos_ref[0:1, at] >= starts) & (cols <= rows)) | (cols == rows))
    lane = lax.broadcasted_iota(jnp.int32, (BLOCK, q_ref.shape[1]), 1) // HEAD
    inverse = jnp.zeros((BLOCK, q_ref.shape[1]), F32)
    for h in range(heads):
        mass = jnp.sum(sum_ref[h * BLOCK : (h + 1) * BLOCK, :], axis=1, keepdims=True)
        inverse = jnp.where(lane == h, 1.0 / mass, inverse)
    inv_ref[...] = inverse
    o_ref[...] = (acc_ref[...] * inverse).astype(BF16)


def attend(meta, queries, keys, vals, kpos, docs):
    total, width = queries.shape
    per = total // 4 // BLOCK
    heads = width // HEAD
    whole = pl.BlockSpec((total, width), lambda i, m: (0, 0))
    block = pl.BlockSpec((BLOCK, width), lambda i, m: (i, 0))

    def rel(i, m):
        return ((m[0] ^ (i // per)) * per + i % per, 0)

    return pl.pallas_call(
        functools.partial(attend_body, docs),
        out_shape=[
            jax.ShapeDtypeStruct((total, width), BF16),
            jax.ShapeDtypeStruct((total, width), F32),
        ],
        grid_spec=pltpu.PrefetchScalarGridSpec(
            num_scalar_prefetch=1,
            grid=(total // BLOCK,),
            in_specs=[block, whole, whole, pl.BlockSpec((8, total), lambda i, m: (0, 0))],
            out_specs=[pl.BlockSpec((BLOCK, width), rel), block],
            scratch_shapes=[
                pltpu.VMEM((BLOCK, width), F32),
                pltpu.VMEM((heads * BLOCK, 128), F32),
            ],
        ),
        cost_estimate=pl.CostEstimate(
            flops=12_000_000_000, bytes_accessed=8 * total * width, transcendentals=6_000_000
        ),
        name="attend",
    )(meta, queries, keys, vals, kpos)


def finish(grad, turned, cosine, sine, scale):
    factor = lax.rsqrt(head_mean(turned * turned) + EPS)
    unit = turned * factor
    by_scale = jnp.sum(grad * unit, axis=0, keepdims=True)
    scaled = grad * scale
    back = factor * (scaled - unit * head_mean(scaled * unit))
    raw = back * cosine - rotate_half(back) * sine
    return raw.astype(BF16), by_scale


def back_body(
    docs,
    meta_ref,
    q_ref,
    qr_ref,
    o_ref,
    inv_ref,
    do_ref,
    k_ref,
    v_ref,
    kr_ref,
    kpos_ref,
    cos_ref,
    sin_ref,
    sqk_ref,
    gq_ref,
    gk_ref,
    gv_ref,
    gs_ref,
    dq_ref,
    dk_ref,
    dv_ref,
):
    step = pl.program_id(0)
    width = q_ref.shape[1]
    heads = width // HEAD
    per = k_ref.shape[0] // 4 // BLOCK
    base = step * BLOCK
    low = doc_start(meta_ref, docs, base) // BLOCK

    @pl.when(step == 0)
    def _():
        dk_ref[...] = jnp.zeros_like(dk_ref)
        dv_ref[...] = jnp.zeros_like(dv_ref)
        gs_ref[...] = jnp.zeros_like(gs_ref)

    dq_ref[...] = jnp.zeros_like(dq_ref)
    queries = stack_heads(q_ref[...] * jnp.bfloat16(HEAD**-0.5))
    upward = do_ref[...].astype(F32) * inv_ref[...]
    ups = stack_heads(upward.astype(BF16))
    picks = lax.broadcasted_iota(jnp.int32, (8, width), 0)
    lanes = lax.broadcasted_iota(jnp.int32, (8, width), 1) // HEAD
    delta = lax.dot_general(
        jnp.where(picks == lanes, 1.0, 0.0).astype(F32),
        upward * o_ref[...].astype(F32),
        (((1,), (1,)), ((), ())),
        precision=lax.Precision.HIGHEST,
        preferred_element_type=F32,
    )
    cols = lax.broadcasted_iota(jnp.int32, (BLOCK, BLOCK), 1) + base
    starts = doc_start(meta_ref, docs, cols)

    def visit(block, allowed):
        at = pl.ds(pl.multiple_of(block * BLOCK, BLOCK), BLOCK)
        keys, vals = k_ref[at, :], v_ref[at, :]
        scores = dot(keys, queries, 1, 1)
        grads = dot(vals, ups, 1, 1)
        expos, slopes = [], []
        total = dq_ref[...]
        for h in range(heads):
            part = slice(h * BLOCK, (h + 1) * BLOCK)
            expo = jnp.where(allowed, jnp.exp(scores[:, part]), 0.0)
            slope = (expo * (grads[:, part] - delta[h : h + 1, :])).astype(BF16)
            expos.append(expo.astype(BF16))
            slopes.append(slope)
            total = total + dot(slope, head_lanes(keys, h), 0, 0)
        dq_ref[...] = total
        dv_ref[at, :] += dot(jnp.concatenate(expos, axis=1), ups)
        dk_ref[at, :] += dot(jnp.concatenate(slopes, axis=1), queries)

    def key_slots(block):
        at = pl.ds(pl.multiple_of(block * BLOCK, BLOCK), BLOCK)
        return wide(kpos_ref[at, :])

    def off_diagonal(block, carry):
        visit(block, key_slots(block) >= starts)
        return carry

    lax.fori_loop(low, step, off_diagonal, 0)
    rows = lax.broadcasted_iota(jnp.int32, (BLOCK, BLOCK), 0) + base
    visit(step, ((key_slots(step) >= starts) & (rows <= cols)) | (rows == cols))

    scale = sqk_ref[0:1, :]
    here = pl.ds(pl.multiple_of(base, BLOCK), BLOCK)
    raw, by_scale = finish(
        dq_ref[...] * (HEAD**-0.5),
        qr_ref[...],
        wide(cos_ref[here, :]),
        wide(sin_ref[here, :]),
        scale,
    )
    gq_ref[...] = raw
    gs_ref[0:1, :] += by_scale

    @pl.when(step == pl.num_programs(0) - 1)
    def _():
        def one(block, carry):
            at = pl.ds(pl.multiple_of(block * BLOCK, BLOCK), BLOCK)
            slot = (meta_ref[0] ^ (block // per)) * per + block % per
            to = pl.ds(pl.multiple_of(slot * BLOCK, BLOCK), BLOCK)
            raw, by_scale = finish(
                dk_ref[at, :], kr_ref[at, :], wide(cos_ref[at, :]), wide(sin_ref[at, :]), scale
            )
            gk_ref[to, :] = raw
            gs_ref[0:1, :] += by_scale
            gv_ref[to, :] = dv_ref[at, :].astype(BF16)
            return carry

        lax.fori_loop(0, pl.num_programs(0), one, 0)


def attend_back(meta, queries, qrot, out, inverse, grad, keys, vals, krot, kpos, cosine, sine, sqk, docs):
    total, width = queries.shape
    per = total // 4 // BLOCK

    def rel(i, m):
        return ((m[0] ^ (i // per)) * per + i % per, 0)

    whole = pl.BlockSpec((total, width), lambda i, m: (0, 0))
    half = pl.BlockSpec((total, 128), lambda i, m: (0, 0))
    block = pl.BlockSpec((BLOCK, width), lambda i, m: (i, 0))
    moved = pl.BlockSpec((BLOCK, width), rel)
    small = pl.BlockSpec((8, width), lambda i, m: (0, 0))
    return pl.pallas_call(
        functools.partial(back_body, docs),
        out_shape=[jax.ShapeDtypeStruct((total, width), BF16)] * 3
        + [jax.ShapeDtypeStruct((8, width), F32)],
        grid_spec=pltpu.PrefetchScalarGridSpec(
            num_scalar_prefetch=1,
            grid=(total // BLOCK,),
            in_specs=[block, block, moved, block, moved, whole, whole, whole, half, half, half, small],
            out_specs=[moved, whole, whole, small],
            scratch_shapes=[
                pltpu.VMEM((BLOCK, width), F32),
                pltpu.VMEM((total, width), F32),
                pltpu.VMEM((total, width), F32),
            ],
        ),
        cost_estimate=pl.CostEstimate(
            flops=30_000_000_000, bytes_accessed=24 * total * width, transcendentals=6_000_000
        ),
        name="attend_back",
    )(meta, queries, qrot, out, inverse, grad, keys, vals, krot, kpos, cosine, sine, sqk)


def both(own, axis, bit, index):
    other = swap(own, axis, bit)
    stacked = jnp.stack([own, other])
    return jnp.where((index & bit) == 0, stacked, jnp.stack([other, own]))


def gather_small(vectors, d, m):
    s_qk, s_up, s_gate, alpha_attn, alpha_mlp = vectors
    if lax.axis_size("dp") != 8:
        whole = [lax.all_gather(v, ("dp", "mp"), axis=0, tiled=True) for v in vectors]
        cut = [
            lax.dynamic_slice_in_dim(v, m * (v.shape[0] // 4), v.shape[0] // 4) for v in whole[:3]
        ]
        return cut[0], cut[1], cut[2], whole[3], whole[4]
    packed = jnp.concatenate([s_up, s_gate, s_qk, alpha_attn, alpha_mlp, s_qk])
    packed = packed.reshape(3, 128)
    pair = both(packed, "mp", 1, m)
    quad = both(pair, "mp", 2, m).reshape(4, 3, 128)
    near = jnp.stack([quad] + [from_z(quad, step) for step in (1, 2, 3)])
    every = jnp.stack([near, swap(near, "dp", 1)]).reshape(2, 4, 4, 384)
    z, y = d >> 1, d & 1
    mine = lax.dynamic_slice_in_dim(every, (m - z) & 3, 1, axis=1)[:, 0]
    mine = jnp.where(y == 0, mine, mine[::-1])
    return (
        mine[..., 256:288].reshape(-1),
        mine[..., :128].reshape(-1),
        mine[..., 128:256].reshape(-1),
        every[..., 288:320].reshape(-1),
        every[..., 320:352].reshape(-1),
    )


def scatter_small(g_sqk, g_up, g_gate, g_alpha_attn, g_alpha_mlp, d, m):
    if lax.axis_size("dp") != 8:
        def place(part):
            whole = jnp.zeros((part.shape[0] * 4,), F32)
            return lax.dynamic_update_slice_in_dim(whole, part, m * part.shape[0], 0)

        whole = (place(g_sqk), place(g_up), place(g_gate), g_alpha_attn, g_alpha_mlp)
        return tuple(
            lax.psum_scatter(
                lax.psum_scatter(v, "dp", scatter_dimension=0, tiled=True),
                "mp",
                scatter_dimension=0,
                tiled=True,
            )
            for v in whole
        )
    z, y = d >> 1, d & 1
    mine = jnp.concatenate(
        [g_up.reshape(2, 4, 128), g_gate.reshape(2, 4, 128), g_sqk.reshape(2, 4, 32)], axis=-1
    )
    mine = jnp.where(y == 0, mine, mine[::-1])
    slot = lax.broadcasted_iota(jnp.int32, (1, 4, 1, 1), 1)
    mine = jnp.where(slot == ((m - z) & 3), mine[:, None], 0.0)
    total = jnp.concatenate(
        [
            mine,
            g_alpha_attn.reshape(2, 4, 4, 32),
            g_alpha_mlp.reshape(2, 4, 4, 32),
            jnp.zeros((2, 4, 4, 32), F32),
        ],
        axis=-1,
    ).reshape(2, 4, 12, 128)
    total = total + swap(total, "mp", 1)
    total = total + swap(total, "mp", 2)
    half = total[0] + swap(total[1], "dp", 1)
    rest = half[0]
    for step in (1, 2, 3):
        rest = rest + to_z(half[step], step)
    rest = lax.dynamic_slice_in_dim(rest.reshape(4, 384), m, 1, axis=0)[0]
    return rest[256:288], rest[:128], rest[128:256], rest[288:320], rest[320:352]


def sum_everywhere(value):
    if lax.axis_size("dp") != 8:
        return lax.psum(value, ("dp", "mp"))
    value = jnp.broadcast_to(value, (8, 128))
    value = value + swap(value, "mp", 1) + swap(value, "mp", 2) + swap(value, "mp", 3)
    value = value + to_z(value, 1) + to_z(value, 2) + to_z(value, 3)
    value = value + swap(value, "dp", 1)
    return value[0, 0]


def shards(
    tokens,
    cotangent,
    lengths,
    key_mask,
    w_query,
    w_key,
    w_value,
    w_out,
    w_up,
    w_gate,
    w_down,
    s_qk,
    s_up,
    s_gate,
    alpha_attn,
    alpha_mlp,
):
    m = lax.axis_index("mp").astype(jnp.int32)
    d = lax.axis_index("dp").astype(jnp.int32)
    direct = lax.axis_size("dp") == 8
    local = tokens.shape[0]
    row_len = key_mask.shape[1]
    docs = lengths.shape[1]

    if direct:
        slots = jnp.arange(8, dtype=jnp.int32)
        z, y = d >> 1, d & 1
        natural = 2 * ((z + (slots & 3)) & 3) + (y ^ (slots >> 2))
        inverse = ((slots & 1) ^ y) * 4 + (((slots >> 1) - z) & 3)
        tokens = pick_cols(tokens, natural)
        cotangent = pick_cols(cotangent, natural)

    x_near, x_far = spread(tokens)
    full_query, after = gather(w_query, 0, ())
    full_key, after = gather(w_key, 0, after)
    full_value, after = gather(w_value, 0, after)
    full_out, after = gather(w_out, 1, after)
    full_up, after = gather(w_up, 0, after)
    full_gate, after = gather(w_gate, 0, after)
    full_down, after = gather(w_down, 1, after)
    sqk, sup, sgate, alpha_one, alpha_two = gather_small(
        (s_qk, s_up, s_gate, alpha_attn, alpha_mlp), d, m
    )
    sqk = jnp.broadcast_to(sqk[None], (8, sqk.shape[0]))

    place = m.reshape(1)
    meta = jnp.concatenate([place, lengths[0]])
    slot_ids = jnp.arange(row_len, dtype=jnp.int32)
    ends = jnp.cumsum(lengths[0])
    passed = (slot_ids[:, None] >= ends[None, :]).astype(jnp.int32)
    positions = slot_ids - jnp.sum(passed * lengths, axis=1)
    steps_even = jnp.arange(0, HEAD, 2).astype(F32)
    frequencies = jnp.power(jnp.float32(10000.0), -steps_even / HEAD)
    angles = positions.astype(F32)[:, None] * jnp.tile(frequencies, 4)[None, :]
    cosine, sine = jnp.cos(angles), jnp.sin(angles)
    kpos = jnp.where(key_mask[0] == 1, slot_ids, -1)
    kpos_rows = jnp.broadcast_to(kpos[None, :], (8, row_len))
    kpos_cols = jnp.broadcast_to(kpos[:, None], (row_len, 128))

    weights = (full_query, full_key, full_value)
    half = project(place, x_near, weights, cosine, sine, sqk, None, 0)
    queries, keys, vals, qrot, krot = project(place, x_far, weights, cosine, sine, sqk, half, 2)
    attended, inverse_mass = attend(meta, queries, keys, vals, kpos_rows, docs)

    near, far = attended[: 2 * local], attended[2 * local :]
    branch_attn = reduce_pair(dot(far, full_out).astype(BF16), dot(near, full_out))
    x_local = tokens.astype(F32)
    h_attn, attn_factor = rms_rows(branch_attn)
    hidden_one, one_factor = rms_rows(x_local + alpha_one * (h_attn - x_local))
    h_near, h_far = spread(hidden_one.astype(BF16))

    def forward(rows):
        up_proj = dot(rows, full_up)
        gate_proj = dot(rows, full_gate)
        outer = sgate * gate_proj
        active = (sup * up_proj * (outer * jax.nn.sigmoid(outer))).astype(BF16)
        return up_proj, gate_proj, active

    up_near, gate_near, act_near = forward(h_near)
    up_far, gate_far, act_far = forward(h_far)
    branch_mlp = reduce_pair(dot(act_far, full_down).astype(BF16), dot(act_near, full_down))
    h_mlp, mlp_factor = rms_rows(branch_mlp)
    result, two_factor = rms_rows(hidden_one + alpha_two * (h_mlp - hidden_one))
    grad_two = rms_back(cotangent.astype(F32), result, two_factor)
    g_alpha_two = jnp.sum(grad_two * (h_mlp - hidden_one), axis=0)
    grad_branch = rms_back(grad_two * alpha_two, h_mlp, mlp_factor).astype(BF16)
    gm_near, gm_far = spread(grad_branch)

    def backward(rows, up_proj, gate_proj):
        g_act = dot(rows, full_down, 1, 1)
        outer = sgate * gate_proj
        sigma = jax.nn.sigmoid(outer)
        g_inner = g_act * (outer * sigma)
        g_outer = g_act * (sup * up_proj) * (sigma * (1.0 + outer * (1.0 - sigma)))
        by_up = jnp.sum(g_inner * up_proj, axis=0)
        by_gate = jnp.sum(g_outer * gate_proj, axis=0)
        g_up = (g_inner * sup).astype(BF16)
        g_gate = (g_outer * sgate).astype(BF16)
        g_hidden = dot(g_up, full_up, 1, 1) + dot(g_gate, full_gate, 1, 1)
        return g_up, g_gate, g_hidden, by_up, by_gate

    gu_near, gg_near, gh_near, bu_near, bg_near = backward(gm_near, up_near, gate_near)
    gu_far, gg_far, gh_far, bu_far, bg_far = backward(gm_far, up_far, gate_far)
    grad_hidden = grad_two * (1.0 - alpha_two) + reduce_pair(gh_far.astype(BF16), gh_near)
    grad_down = scatter(dot(act_near, gm_near, 0, 0) + dot(act_far, gm_far, 0, 0), 1)
    grad_up = scatter(dot(h_near, gu_near, 0, 0) + dot(h_far, gu_far, 0, 0), 0)
    grad_gate = scatter(dot(h_near, gg_near, 0, 0) + dot(h_far, gg_far, 0, 0), 0)

    grad_one = rms_back(grad_hidden, hidden_one, one_factor)
    g_alpha_one = jnp.sum(grad_one * (h_attn - x_local), axis=0)
    grad_attn = rms_back(grad_one * alpha_one, h_attn, attn_factor).astype(BF16)
    ga_near, ga_far = spread(grad_attn)
    g_att = jnp.concatenate(
        [dot(ga_near, full_out, 1, 1).astype(BF16), dot(ga_far, full_out, 1, 1).astype(BF16)]
    )
    grad_out = scatter(dot(near, ga_near, 0, 0) + dot(far, ga_far, 0, 0), 1)

    g_query, g_key, g_val, g_sqk = attend_back(
        meta, queries, qrot, attended, inverse_mass, g_att, keys, vals, krot, kpos_cols, cosine, sine, sqk, docs
    )

    def to_tokens(rows):
        return (
            dot(g_query[rows], full_query, 1, 1)
            + dot(g_key[rows], full_key, 1, 1)
            + dot(g_val[rows], full_value, 1, 1)
        )

    first, second = slice(0, 2 * local), slice(2 * local, 4 * local)
    grad_tokens = grad_one * (1.0 - alpha_one) + reduce_pair(
        to_tokens(second).astype(BF16), to_tokens(first)
    )

    def by_weight(grad):
        return scatter(dot(x_near, grad[first], 0, 0) + dot(x_far, grad[second], 0, 0), 0)

    small = scatter_small(
        g_sqk[0], bu_near + bu_far, bg_near + bg_far, g_alpha_one, g_alpha_two, d, m
    )
    pieces = (
        by_weight(g_query),
        by_weight(g_key),
        by_weight(g_val),
        grad_out,
        grad_up,
        grad_gate,
        grad_down,
    ) + small
    squares = jnp.float32(0.0)
    for piece in pieces:
        squares = squares + jnp.sum(piece * piece)
    grad_norm = jnp.sqrt(sum_everywhere(squares))
    mean_alphas = jnp.stack([jnp.mean(alpha_one), jnp.mean(alpha_two)])
    result = result.astype(BF16)
    if direct:
        result = pick_cols(result, inverse)
        grad_tokens = pick_cols(grad_tokens, inverse)
    return (result, grad_tokens) + pieces + (grad_norm, mean_alphas)


def solution(mesh):
    both_axes = P(("dp", "mp"))
    rows = P(("dp", "mp"), None)
    in_specs = (
        (rows, rows, P("dp", None), P("dp", None))
        + (P("dp", "mp"),) * 3
        + (P("mp", "dp"),)
        + (P("dp", "mp"),) * 2
        + (P("mp", "dp"),)
        + (both_axes,) * 5
    )
    out_specs = (
        (rows, rows)
        + (P("dp", "mp"),) * 3
        + (P("mp", "dp"),)
        + (P("dp", "mp"),) * 2
        + (P("mp", "dp"),)
        + (both_axes,) * 5
        + (P(), P())
    )
    return jax.shard_map(shards, mesh=mesh, in_specs=in_specs, out_specs=out_specs, check_vma=False)
```

```python
import functools

import jax
import jax.numpy as jnp
from jax import lax
from jax.experimental import pallas as pl
from jax.experimental.pallas import tpu as pltpu
from jax.sharding import PartitionSpec as P

D = 1024
HEADS = 16
HEAD = D // HEADS
EPS = 1e-06
NEG = -1e30
BLOCK = 256
F32 = jnp.float32
BF16 = jnp.bfloat16


def mean_rows(tensor):
    return jnp.mean(tensor, axis=-1, keepdims=True)


def normed(tensor):
    factor = lax.rsqrt(mean_rows(tensor * tensor) + EPS)
    return tensor * factor, factor


def normed_back(incoming, unit, factor):
    return factor * (incoming - unit * mean_rows(incoming * unit))


def dot(left, right, left_dim=1, right_dim=0):
    return lax.dot_general(
        left, right, (((left_dim,), (right_dim,)), ((), ())), preferred_element_type=F32
    )


RING = (0, 2, 4, 6, 7, 5, 3, 1)


def swap(array, axis, bit):
    size = lax.axis_size(axis)
    return lax.ppermute(array, axis, [(i, i ^ bit) for i in range(size)])


def to_z(array, step):
    return lax.ppermute(
        array, "dp", [(z * 2 + y, ((z + step) % 4) * 2 + y) for z in range(4) for y in range(2)]
    )


def around(array, step):
    return lax.ppermute(array, "dp", [(RING[p], RING[(p + step) % 8]) for p in range(8)])


def gather(shard, before_last=()):
    if lax.axis_size("dp") != 8:
        return lax.all_gather(shard, "dp", axis=0, tiled=True)
    d = lax.axis_index("dp")
    rows, width = shard.shape
    place = jnp.where((d & 1) == 0, d >> 1, 7 - (d >> 1))

    def put(full, part, step):
        q = (place + step) & 7
        index = jnp.where(q < 4, 2 * q, 2 * (7 - q) + 1)
        return lax.dynamic_update_slice(full, part, (index * rows, jnp.int32(0)))

    full = put(jnp.zeros((8 * rows, width), shard.dtype), shard, 0)
    ahead = behind = shard
    for step in (1, 2, 3):
        ahead, behind = around(ahead, 1), around(behind, -1)
        full = put(put(full, ahead, -step), behind, step)
    if before_last:
        ahead = lax.optimization_barrier((ahead,) + tuple(before_last))[0]
    return put(full, around(ahead, 1), 4)


def chip_groups():
    return [
        [d * 4 + 2 * x + core for d in range(lax.axis_size("dp")) for core in range(2)]
        for x in range(2)
    ]


def scatter(grad):
    if lax.axis_size("dp") != 8:
        return lax.psum_scatter(grad.astype(F32), "dp", scatter_dimension=0, tiled=True)
    d = lax.axis_index("dp")
    z, y = d >> 1, d & 1
    rows, width = grad.shape[0] // 8, grad.shape[1]
    grad = grad.reshape(4, 2, rows, width)
    theirs = lax.dynamic_index_in_dim(grad, 1 - y, axis=1, keepdims=False)
    mine = lax.dynamic_index_in_dim(grad, y, axis=1, keepdims=False)
    half = mine.astype(F32) + swap(theirs.astype(BF16), "dp", 1).astype(F32)
    total = lax.dynamic_index_in_dim(half, z, axis=0, keepdims=False)
    for step in (1, 2, 3):
        part = lax.dynamic_index_in_dim(half, (z + step) & 3, axis=0, keepdims=False)
        total = total + to_z(part.astype(BF16), step).astype(F32)
    return total


def to_all(rows):
    return lax.all_to_all(rows, ("dp", "mp"), 0, 0, tiled=True)


def rotate_half(tensor):
    width = tensor.shape[-1]
    lane = lax.broadcasted_iota(jnp.int32, tensor.shape, 1)
    ahead = pltpu.roll(tensor, width - HEAD // 2, 1)
    behind = pltpu.roll(tensor, HEAD // 2, 1)
    return jnp.where((lane & (HEAD - 1)) < HEAD // 2, -ahead, behind)


def head_mean(tensor):
    width = tensor.shape[-1]
    row = lax.broadcasted_iota(jnp.int32, (width, width), 0) // HEAD
    col = lax.broadcasted_iota(jnp.int32, (width, width), 1) // HEAD
    ones = jnp.where(row == col, 1.0 / HEAD, 0.0).astype(BF16)
    high = tensor.astype(BF16)
    rest = (tensor - high.astype(F32)).astype(BF16)
    return dot(high, ones) + dot(rest, ones)


def wide(table):
    return jnp.concatenate([table, table], axis=1)


def project_body(m_ref, x_ref, wq_ref, wk_ref, wv_ref, cos_ref, sin_ref, sqk_ref, *refs):
    q_ref, k_ref, v_ref, qr_ref, kr_ref = refs[-5:]
    rows = x_ref[...]
    cosine, sine = wide(cos_ref[...]), wide(sin_ref[...])
    scale = sqk_ref[0:1, :]
    for weight_ref, out_ref, rot_ref in ((wq_ref, q_ref, qr_ref), (wk_ref, k_ref, kr_ref)):
        raw = jnp.dot(rows, weight_ref[...], preferred_element_type=F32)
        turned = raw * cosine + rotate_half(raw) * sine
        rot_ref[...] = turned
        unit = turned * lax.rsqrt(head_mean(turned * turned) + EPS)
        out_ref[...] = (unit * scale).astype(BF16)
    v_ref[...] = jnp.dot(rows, wv_ref[...], preferred_element_type=F32).astype(BF16)


def project(place, x_rows, weight, cosine, sine, sqk, previous, first):
    rows, width = x_rows.shape[0], weight.shape[1] // 4
    total = cosine.shape[0]
    per = total // 4 // BLOCK

    def row_block(i, m):
        return ((m[0] ^ (first + 2 * (i // per))) * per + i % per, 0)

    any_spec = pl.BlockSpec(memory_space=pl.ANY)

    def column(index):
        return pl.BlockSpec((x_rows.shape[1], width), lambda i, m: (0, index))

    table = pl.BlockSpec((BLOCK, cosine.shape[1]), row_block)
    out = pl.BlockSpec((BLOCK, width), row_block)
    shapes = [jax.ShapeDtypeStruct((total, width), t) for t in (BF16, BF16, BF16, F32, F32)]
    extra = list(previous) if previous is not None else []
    return pl.pallas_call(
        project_body,
        out_shape=shapes,
        grid_spec=pltpu.PrefetchScalarGridSpec(
            num_scalar_prefetch=1,
            grid=(rows // BLOCK,),
            in_specs=[
                pl.BlockSpec((BLOCK, x_rows.shape[1]), lambda i, m: (i, 0)),
                column(0),
                column(1),
                column(2),
                table,
                table,
                pl.BlockSpec((8, width), lambda i, m: (0, 0)),
            ]
            + [any_spec] * len(extra),
            out_specs=[out] * 5,
        ),
        input_output_aliases={8 + i: i for i in range(len(extra))},
        cost_estimate=pl.CostEstimate(
            flops=6 * rows * D * width, bytes_accessed=8 * rows * D, transcendentals=rows
        ),
        name="project",
    )(place, x_rows, weight, weight, weight, cosine, sine, sqk, *extra)


def head_lanes(array, head):
    lane = lax.broadcasted_iota(jnp.int32, array.shape, 1)
    return jnp.where(lane // HEAD == head, array, jnp.zeros_like(array))


def stack_heads(array):
    heads = array.shape[1] // HEAD
    return jnp.concatenate([head_lanes(array, h) for h in range(heads)], axis=0)


def doc_start(meta_ref, docs, slots):
    start = jnp.zeros_like(slots)
    end = 0
    for i in range(docs):
        length = meta_ref[1 + i]
        end = end + length
        start = start + jnp.where(slots >= end, length, 0)
    return start


def slot_place(rel):
    return (rel >> 1) + 2 * (rel & 1)


def block_at(block):
    return pl.ds(pl.multiple_of(block * BLOCK, BLOCK), BLOCK)


def split_heads(source_ref, split_ref):
    def one(block, carry):
        split_ref[block] = stack_heads(source_ref[block_at(block), :])
        return carry

    lax.fori_loop(0, source_ref.shape[0] // BLOCK, one, 0)


def attend_body(docs, meta_ref, q_ref, k_ref, v_ref, kpos_ref, o_ref, inv_ref, acc_ref, sum_ref, vs_ref):
    step = pl.program_id(0)
    heads = q_ref.shape[1] // HEAD
    base = step * BLOCK
    low = doc_start(meta_ref, docs, base) // BLOCK

    @pl.when(step == 0)
    def _():
        split_heads(v_ref, vs_ref)

    scaled = q_ref[...] * jnp.bfloat16(HEAD**-0.5)
    queries = [head_lanes(scaled, h) for h in range(heads)]
    rows = lax.broadcasted_iota(jnp.int32, (BLOCK, BLOCK), 0) + base
    starts = doc_start(meta_ref, docs, rows)
    acc_ref[...] = jnp.zeros_like(acc_ref)
    sum_ref[...] = jnp.zeros_like(sum_ref)

    def visit(block, allowed):
        keys = k_ref[block_at(block), :]
        bias = jnp.where(allowed, 0.0, NEG)
        expos = []
        for h in range(heads):
            expo = jnp.exp(dot(queries[h], keys, 1, 1) + bias)
            sum_ref[h * BLOCK : (h + 1) * BLOCK, :] += expo[:, :128] + expo[:, 128:]
            expos.append(expo.astype(BF16))
        acc_ref[...] += dot(jnp.concatenate(expos, axis=1), vs_ref[block])

    def off_diagonal(block, carry):
        visit(block, kpos_ref[0:1, block_at(block)] >= starts)
        return carry

    lax.fori_loop(low, step, off_diagonal, 0)
    cols = lax.broadcasted_iota(jnp.int32, (BLOCK, BLOCK), 1) + base
    visit(step, ((kpos_ref[0:1, block_at(step)] >= starts) & (cols <= rows)) | (cols == rows))
    lane = lax.broadcasted_iota(jnp.int32, (BLOCK, q_ref.shape[1]), 1) // HEAD
    inverse = jnp.zeros((BLOCK, q_ref.shape[1]), F32)
    for h in range(heads):
        mass = jnp.sum(sum_ref[h * BLOCK : (h + 1) * BLOCK, :], axis=1, keepdims=True)
        inverse = jnp.where(lane == h, 1.0 / mass, inverse)
    inv_ref[...] = inverse
    o_ref[...] = (acc_ref[...] * inverse).astype(BF16)


def attend(meta, queries, keys, vals, kpos, docs):
    total, width = queries.shape
    per = total // 4 // BLOCK
    heads = width // HEAD
    whole = pl.BlockSpec((total, width), lambda i, m: (0, 0))
    block = pl.BlockSpec((BLOCK, width), lambda i, m: (i, 0))

    def rel(i, m):
        return (slot_place(m[0] ^ (i // per)) * per + i % per, 0)

    return pl.pallas_call(
        functools.partial(attend_body, docs),
        out_shape=[
            jax.ShapeDtypeStruct((total, width), BF16),
            jax.ShapeDtypeStruct((total, width), F32),
        ],
        grid_spec=pltpu.PrefetchScalarGridSpec(
            num_scalar_prefetch=1,
            grid=(total // BLOCK,),
            in_specs=[block, whole, whole, pl.BlockSpec((8, total), lambda i, m: (0, 0))],
            out_specs=[pl.BlockSpec((BLOCK, width), rel), block],
            scratch_shapes=[
                pltpu.VMEM((BLOCK, width), F32),
                pltpu.VMEM((heads * BLOCK, 128), F32),
                pltpu.VMEM((total // BLOCK, heads * BLOCK, width), BF16),
            ],
        ),
        cost_estimate=pl.CostEstimate(
            flops=12_000_000_000, bytes_accessed=8 * total * width, transcendentals=6_000_000
        ),
        name="attend",
    )(meta, queries, keys, vals, kpos)


def finish(grad, turned, cosine, sine, scale):
    factor = lax.rsqrt(head_mean(turned * turned) + EPS)
    unit = turned * factor
    by_scale = jnp.sum(grad * unit, axis=0, keepdims=True)
    scaled = grad * scale
    back = factor * (scaled - unit * head_mean(scaled * unit))
    raw = back * cosine - rotate_half(back) * sine
    return raw.astype(BF16), by_scale


def back_body(
    docs,
    meta_ref,
    q_ref,
    qr_ref,
    o_ref,
    inv_ref,
    do_ref,
    k_ref,
    v_ref,
    kr_ref,
    kpos_ref,
    cos_ref,
    sin_ref,
    sqk_ref,
    g_ref,
    gs_ref,
    dq_ref,
    dk_ref,
    dv_ref,
    ks_ref,
):
    step = pl.program_id(0)
    width = q_ref.shape[1]
    heads = width // HEAD
    per = k_ref.shape[0] // 4 // BLOCK
    base = step * BLOCK
    low = doc_start(meta_ref, docs, base) // BLOCK

    @pl.when(step == 0)
    def _():
        dk_ref[...] = jnp.zeros_like(dk_ref)
        dv_ref[...] = jnp.zeros_like(dv_ref)
        gs_ref[...] = jnp.zeros_like(gs_ref)
        split_heads(k_ref, ks_ref)

    dq_ref[...] = jnp.zeros_like(dq_ref)
    scaled = q_ref[...] * jnp.bfloat16(HEAD**-0.5)
    queries = [head_lanes(scaled, h) for h in range(heads)]
    all_queries = jnp.concatenate(queries, axis=0)
    upward = do_ref[...].astype(F32) * inv_ref[...]
    ups = [head_lanes(upward.astype(BF16), h) for h in range(heads)]
    all_ups = jnp.concatenate(ups, axis=0)
    picks = lax.broadcasted_iota(jnp.int32, (8, width), 0)
    lanes = lax.broadcasted_iota(jnp.int32, (8, width), 1) // HEAD
    delta = lax.dot_general(
        jnp.where(picks == lanes, 1.0, 0.0).astype(F32),
        upward * o_ref[...].astype(F32),
        (((1,), (1,)), ((), ())),
        precision=lax.Precision.HIGHEST,
        preferred_element_type=F32,
    )
    cols = lax.broadcasted_iota(jnp.int32, (BLOCK, BLOCK), 1) + base
    starts = doc_start(meta_ref, docs, cols)

    def visit(block, allowed):
        at = block_at(block)
        keys, vals = k_ref[at, :], v_ref[at, :]
        bias = jnp.where(allowed, 0.0, NEG)
        expos, slopes = [], []
        for h in range(heads):
            expo = jnp.exp(dot(keys, queries[h], 1, 1) + bias)
            expos.append(expo.astype(BF16))
            slope = expo * (dot(vals, ups[h], 1, 1) - delta[h : h + 1, :])
            slopes.append(slope.astype(BF16))
        dv_ref[at, :] += dot(jnp.concatenate(expos, axis=1), all_ups)
        dk_ref[at, :] += dot(jnp.concatenate(slopes, axis=1), all_queries)
        dq_ref[...] += dot(jnp.concatenate(slopes, axis=0), ks_ref[block], 0, 0)

    def key_slots(block):
        return wide(kpos_ref[block_at(block), :])

    def off_diagonal(block, carry):
        visit(block, key_slots(block) >= starts)
        return carry

    lax.fori_loop(low, step, off_diagonal, 0)
    rows = lax.broadcasted_iota(jnp.int32, (BLOCK, BLOCK), 0) + base
    visit(step, ((key_slots(step) >= starts) & (rows <= cols)) | (rows == cols))

    scale = sqk_ref[0:1, :]
    here = pl.ds(pl.multiple_of(base, BLOCK), BLOCK)
    raw, by_scale = finish(
        dq_ref[...] * (HEAD**-0.5),
        qr_ref[...],
        wide(cos_ref[here, :]),
        wide(sin_ref[here, :]),
        scale,
    )
    slot = slot_place(meta_ref[0] ^ (step // per)) * per + step % per
    g_ref[pl.ds(pl.multiple_of(slot * BLOCK, BLOCK), BLOCK), :width] = raw
    gs_ref[0:1, :] += by_scale

    @pl.when(step == pl.num_programs(0) - 1)
    def _():
        def one(block, carry):
            at = pl.ds(pl.multiple_of(block * BLOCK, BLOCK), BLOCK)
            slot = slot_place(meta_ref[0] ^ (block // per)) * per + block % per
            to = pl.ds(pl.multiple_of(slot * BLOCK, BLOCK), BLOCK)
            raw, by_scale = finish(
                dk_ref[at, :], kr_ref[at, :], wide(cos_ref[at, :]), wide(sin_ref[at, :]), scale
            )
            g_ref[to, width : 2 * width] = raw
            gs_ref[0:1, :] += by_scale
            g_ref[to, 2 * width :] = dv_ref[at, :].astype(BF16)
            return carry

        lax.fori_loop(0, pl.num_programs(0), one, 0)


def attend_back(meta, queries, qrot, out, inverse, grad, keys, vals, krot, kpos, cosine, sine, sqk, docs):
    total, width = queries.shape
    per = total // 4 // BLOCK

    def rel(i, m):
        return (slot_place(m[0] ^ (i // per)) * per + i % per, 0)

    whole = pl.BlockSpec((total, width), lambda i, m: (0, 0))
    half = pl.BlockSpec((total, 128), lambda i, m: (0, 0))
    block = pl.BlockSpec((BLOCK, width), lambda i, m: (i, 0))
    moved = pl.BlockSpec((BLOCK, width), rel)
    small = pl.BlockSpec((8, width), lambda i, m: (0, 0))
    return pl.pallas_call(
        functools.partial(back_body, docs),
        out_shape=[
            jax.ShapeDtypeStruct((total, 3 * width), BF16),
            jax.ShapeDtypeStruct((8, width), F32),
        ],
        grid_spec=pltpu.PrefetchScalarGridSpec(
            num_scalar_prefetch=1,
            grid=(total // BLOCK,),
            in_specs=[block, block, moved, block, moved, whole, whole, whole, half, half, half, small],
            out_specs=[pl.BlockSpec((total, 3 * width), lambda i, m: (0, 0)), small],
            scratch_shapes=[
                pltpu.VMEM((BLOCK, width), F32),
                pltpu.VMEM((total, width), F32),
                pltpu.VMEM((total, width), F32),
                pltpu.VMEM((total // BLOCK, width // HEAD * BLOCK, width), BF16),
            ],
        ),
        cost_estimate=pl.CostEstimate(
            flops=30_000_000_000, bytes_accessed=24 * total * width, transcendentals=6_000_000
        ),
        name="attend_back",
    )(meta, queries, qrot, out, inverse, grad, keys, vals, krot, kpos, cosine, sine, sqk)


TILE = 256


def weight_tile(weight_ref, part, index):
    return weight_ref[:, part, index].reshape(D, TILE)


def weight_spec(weights):
    return pl.BlockSpec(weights.shape[:4] + (TILE,), lambda t: (0, 0, 0, 0, t))


def forward_body(
    h_ref, w_ref, sup_ref, sgate_ref, gate_ref, act_ref, by_up_ref, by_gate_ref, out_ref, acc_ref
):
    t = pl.program_id(0)
    rows = h_ref[...]
    acts = []
    for part in range(2):
        sup, sgate = sup_ref[part, 0:1, :], sgate_ref[part, 0:1, :]
        scaled = sup * dot(rows, weight_tile(w_ref, part, 0))
        gate_proj = dot(rows, weight_tile(w_ref, part, 1))
        outer = sgate * gate_proj
        sigma = jax.nn.sigmoid(outer)
        silu = outer * sigma
        acts.append((scaled * silu).astype(BF16))
        gate_ref[part] = gate_proj.astype(BF16)
        act_ref[part] = acts[part]
        by_up_ref[part] = (sup * silu).astype(BF16)
        by_gate_ref[part] = ((sgate * scaled) * (sigma + silu * (1.0 - sigma))).astype(BF16)
    total = dot(
        jnp.concatenate(acts, axis=1),
        jnp.concatenate([weight_tile(w_ref, part, 2) for part in range(2)], axis=1),
        1,
        1,
    )
    add_up(t, total, acc_ref, out_ref)


def add_up(t, total, acc_ref, out_ref):
    @pl.when(t == 0)
    def _():
        acc_ref[...] = total

    @pl.when((t > 0) & (t < pl.num_programs(0) - 1))
    def _():
        acc_ref[...] += total

    @pl.when(t == pl.num_programs(0) - 1)
    def _():
        out_ref[...] = (acc_ref[...] + total).astype(out_ref.dtype)


def ffn_specs(count):
    whole = pl.BlockSpec((count, D), lambda t: (0, 0))
    tile = pl.BlockSpec((2, count, TILE), lambda t: (0, 0, t))
    scale = pl.BlockSpec((2, 8, TILE), lambda t: (0, 0, t))
    return whole, tile, scale


def ffn_forward(rows, weights, sup, sgate, kind):
    count, hidden = rows.shape[0], sup.shape[2]
    whole, tile, scale = ffn_specs(count)
    return pl.pallas_call(
        forward_body,
        out_shape=[jax.ShapeDtypeStruct((2, count, hidden), BF16)] * 4
        + [jax.ShapeDtypeStruct((count, D), kind)],
        grid=(hidden // TILE,),
        in_specs=[whole, weight_spec(weights), scale, scale],
        out_specs=[tile] * 4 + [whole],
        scratch_shapes=[pltpu.VMEM((count, D), F32)],
        cost_estimate=pl.CostEstimate(
            flops=12 * count * D * hidden,
            bytes_accessed=12 * D * hidden + 12 * count * hidden,
            transcendentals=2 * count * hidden,
        ),
        name="ffn_forward",
    )(rows, weights, sup, sgate)


def backward_body(
    gm_ref, w_ref, gate_ref, act_ref, by_up_ref, by_gate_ref, sup_ref, sgate_ref, gu_ref, gg_ref, bu_ref, bg_ref, out_ref, acc_ref
):
    t = pl.program_id(0)
    rows = gm_ref[...]
    lefts, rights = [], []
    for part in range(2):
        g_act = dot(rows, weight_tile(w_ref, part, 2))
        g_up = (g_act * by_up_ref[part].astype(F32)).astype(BF16)
        g_gate = g_act * by_gate_ref[part].astype(F32)
        up_sum = jnp.sum(g_act * act_ref[part].astype(F32), axis=0, keepdims=True)
        gate_sum = jnp.sum(g_gate * gate_ref[part].astype(F32), axis=0, keepdims=True)
        g_gate = g_gate.astype(BF16)
        bu_ref[part, 0:1, :] = up_sum / sup_ref[part, 0:1, :]
        bg_ref[part, 0:1, :] = gate_sum / sgate_ref[part, 0:1, :]
        gu_ref[part] = g_up
        gg_ref[part] = g_gate
        lefts += [g_up, g_gate]
        rights += [weight_tile(w_ref, part, 0), weight_tile(w_ref, part, 1)]
    total = dot(jnp.concatenate(lefts, axis=1), jnp.concatenate(rights, axis=1), 1, 1)
    add_up(t, total, acc_ref, out_ref)


def ffn_backward(grads, weights, saved, sup, sgate, kind):
    count, hidden = grads.shape[0], sup.shape[2]
    whole, tile, scale = ffn_specs(count)
    return pl.pallas_call(
        backward_body,
        out_shape=[jax.ShapeDtypeStruct((2, count, hidden), BF16)] * 2
        + [jax.ShapeDtypeStruct((2, 8, hidden), F32)] * 2
        + [jax.ShapeDtypeStruct((count, D), kind)],
        grid=(hidden // TILE,),
        in_specs=[whole, weight_spec(weights)] + [tile] * 4 + [scale, scale],
        out_specs=[tile, tile, scale, scale, whole],
        scratch_shapes=[pltpu.VMEM((count, D), F32)],
        cost_estimate=pl.CostEstimate(
            flops=12 * count * D * hidden,
            bytes_accessed=12 * D * hidden + 24 * count * hidden,
            transcendentals=0,
        ),
        name="ffn_backward",
    )(grads, weights, *saved, sup, sgate)


def turn_rows(own_ref, far_ref, turned_ref):
    count = own_ref.shape[0]

    @pl.when(pl.program_id(0) == 0)
    def _():
        turned_ref[:, :count] = own_ref[...].T
        turned_ref[:, count:] = far_ref[...].T


def down_grad_body(m_ref, lo_ref, lr_ref, ro_ref, rr_ref, mine_ref, other_ref, turned_ref):
    turn_rows(lo_ref, lr_ref, turned_ref)
    core = m_ref[0] & 1
    for part, out_ref in ((core, mine_ref), (1 - core, other_ref)):
        right = jnp.concatenate([ro_ref[part], rr_ref[part]], axis=0)
        out_ref[...] = dot(turned_ref[...], right).astype(BF16)


def up_grad_body(m_ref, lo_ref, lr_ref, uo_ref, ur_ref, go_ref, gr_ref, out_ref, turned_ref):
    turn_rows(lo_ref, lr_ref, turned_ref)
    for index, (own_ref, far_ref) in enumerate(((uo_ref, ur_ref), (go_ref, gr_ref))):
        for part in range(2):
            right = jnp.concatenate([own_ref[part], far_ref[part]], axis=0)
            total = dot(turned_ref[...], right).astype(BF16)
            out_ref[:, part, index] = total.reshape(out_ref.shape[0], out_ref.shape[3], TILE)


def weight_grad(body, place, lefts, rights, out_shape, out_specs):
    _, count, hidden = rights[0].shape
    whole = pl.BlockSpec((count, D), lambda t, m: (0, 0))
    tile = pl.BlockSpec((2, count, TILE), lambda t, m: (0, 0, t))
    pairs = len(rights) // 2
    return pl.pallas_call(
        body,
        out_shape=out_shape,
        grid_spec=pltpu.PrefetchScalarGridSpec(
            num_scalar_prefetch=1,
            grid=(hidden // TILE,),
            in_specs=[whole, whole] + [tile] * len(rights),
            out_specs=out_specs,
            scratch_shapes=[pltpu.VMEM((D, 2 * count), BF16)],
        ),
        cost_estimate=pl.CostEstimate(
            flops=8 * pairs * count * D * hidden,
            bytes_accessed=pairs * (4 * D * hidden + 8 * count * hidden),
            transcendentals=0,
        ),
        name="weight_grad",
    )(place, *lefts, *rights)


def own_call(body, name, rows_in, vectors, wholes, outs, sums, flops):
    count = outs[0][0]
    blocks = count // BLOCK

    def rows_spec(width, skip, column):
        return pl.BlockSpec((BLOCK, width), lambda i: (skip // BLOCK + i, column))

    in_specs = [rows_spec(w, s, c) for _, w, s, c in rows_in]
    in_specs += [pl.BlockSpec((8, v.shape[1]), lambda i: (0, 0)) for v in vectors]
    in_specs += [pl.BlockSpec((D, w), lambda i, c=c: (0, c)) for _, w, c in wholes]
    shapes = [jax.ShapeDtypeStruct((count, w), t) for count, w, t in outs]
    shapes += [jax.ShapeDtypeStruct((8, D), F32)] * sums
    out_specs = [pl.BlockSpec((BLOCK, w), lambda i: (i, 0)) for _, w, _ in outs]
    out_specs += [pl.BlockSpec((8, D), lambda i: (0, 0))] * sums
    return pl.pallas_call(
        body,
        out_shape=shapes,
        grid=(blocks,),
        in_specs=in_specs,
        out_specs=out_specs,
        cost_estimate=pl.CostEstimate(
            flops=flops, bytes_accessed=20 * count * D, transcendentals=count
        ),
        name=name,
    )(*[a for a, *_ in rows_in], *vectors, *[a for a, *_ in wholes])


def first_update(branch, x_rows, alpha):
    h_attn, attn_factor = normed(branch)
    hidden, one_factor = normed(x_rows + alpha * (h_attn - x_rows))
    return h_attn, attn_factor, hidden, one_factor


def attn_body(a0, a1, a2, a3, x_ref, alpha_ref, w0, w1, w2, w3, branch_ref, low_ref):
    branch = dot(a0[...], w0[...], 1, 1) + dot(a1[...], w1[...], 1, 1)
    branch = branch + dot(a2[...], w2[...], 1, 1) + dot(a3[...], w3[...], 1, 1)
    branch_ref[...] = branch
    hidden = first_update(branch, x_ref[...].astype(F32), alpha_ref[0:1, :])[2]
    low_ref[...] = hidden.astype(BF16)


def turn_body(own_ref, far_ref, branch_ref, x_ref, cot_ref, one_ref, two_ref, out_ref, gm_ref, keep_ref, sum_ref):
    hidden = first_update(branch_ref[...], x_ref[...].astype(F32), one_ref[0:1, :])[2]
    alpha = two_ref[0:1, :]
    h_mlp, mlp_factor = normed(own_ref[...] + far_ref[...].astype(F32))
    step = h_mlp - hidden
    result, two_factor = normed(hidden + alpha * step)
    out_ref[...] = result.astype(BF16)
    grad_two = normed_back(cot_ref[...].astype(F32), result, two_factor)
    keep_ref[...] = grad_two * (1.0 - alpha)
    gm_ref[...] = normed_back(grad_two * alpha, h_mlp, mlp_factor).astype(BF16)

    @pl.when(pl.program_id(0) == 0)
    def _():
        sum_ref[...] = jnp.zeros_like(sum_ref)

    sum_ref[0:1, :] += jnp.sum(grad_two * step, axis=0, keepdims=True)


def attn_back_body(
    own_ref, far_ref, keep_ref, branch_ref, x_ref, one_ref, w0, w1, w2, w3, ga_ref, gt_ref, o0, o1, o2, o3, sum_ref
):
    x_rows, alpha = x_ref[...].astype(F32), one_ref[0:1, :]
    h_attn, attn_factor, hidden, one_factor = first_update(branch_ref[...], x_rows, alpha)
    incoming = keep_ref[...] + own_ref[...] + far_ref[...].astype(F32)
    grad_one = normed_back(incoming, hidden, one_factor)
    gt_ref[...] = grad_one * (1.0 - alpha)
    grad_attn = normed_back(grad_one * alpha, h_attn, attn_factor).astype(BF16)
    ga_ref[...] = grad_attn
    for weight_ref, out_ref in ((w0, o0), (w1, o1), (w2, o2), (w3, o3)):
        out_ref[...] = dot(grad_attn, weight_ref[...]).astype(BF16)

    @pl.when(pl.program_id(0) == 0)
    def _():
        sum_ref[...] = jnp.zeros_like(sum_ref)

    sum_ref[0:1, :] += jnp.sum(grad_one * (h_attn - x_rows), axis=0, keepdims=True)


def shards(
    tokens,
    cotangent,
    lengths,
    key_mask,
    w_query,
    w_key,
    w_value,
    w_out,
    w_up,
    w_gate,
    w_down,
    s_qk,
    s_up,
    s_gate,
    alpha_attn,
    alpha_mlp,
):
    m = lax.axis_index("mp").astype(jnp.int32)
    devices = lax.axis_size("dp") * lax.axis_size("mp")
    local = tokens.shape[0]
    row_len = key_mask.shape[1]
    docs = lengths.shape[1]
    part = w_up.shape[1]
    width = w_query.shape[1]

    shard = jnp.concatenate([w_up, w_gate, w_down.T], axis=0)
    weights = lax.all_gather(
        shard, ("dp", "mp"), axis=0, tiled=True, axis_index_groups=chip_groups()
    ).reshape(-1, 2, 3, shard.shape[0] // 3, part)
    x_over = swap(tokens, "mp", 2)
    vector = jnp.concatenate([s_up, s_gate, s_qk, alpha_attn, alpha_mlp])[None]
    every = to_all(jnp.broadcast_to(vector, (devices, vector.shape[1])))
    attn = gather(jnp.concatenate([w_query, w_key, w_value, w_out.T], axis=1), (x_over, every))
    cuts, start = [], 0
    for piece in (s_up, s_gate, s_qk, alpha_attn, alpha_mlp):
        cuts.append(every[:, start : start + piece.shape[0]].reshape(-1))
        start += piece.shape[0]
    sup_all, sgate_all, sqk_all, alpha_one, alpha_two = cuts

    def quarter(array, index):
        size = array.shape[0] // 4
        return lax.dynamic_slice_in_dim(array, index * size, size)

    def eight(array):
        return jnp.broadcast_to(array[None], (8, array.shape[0]))

    sqk = eight(quarter(sqk_all, m))
    low = m & 2
    sup = jnp.stack([eight(quarter(sup_all, low)), eight(quarter(sup_all, low + 1))])
    sgate = jnp.stack([eight(quarter(sgate_all, low)), eight(quarter(sgate_all, low + 1))])
    one, two = eight(alpha_one), eight(alpha_two)
    x_first = jnp.concatenate([tokens, x_over], axis=0)
    x_second = swap(x_first, "mp", 1)
    out_mine = attn[:, 3 * width :]
    out_core = swap(out_mine, "mp", 1)
    out_over = swap(out_mine, "mp", 2)
    out_cross = swap(out_over, "mp", 1)
    out_parts = [(w, width, 0) for w in (out_mine, out_core, out_over, out_cross)]

    place = m.reshape(1)
    meta = jnp.concatenate([place, lengths[0]])
    slot_ids = jnp.arange(row_len, dtype=jnp.int32)
    positions, end = slot_ids, 0
    for i in range(docs):
        end = end + lengths[0, i]
        positions = positions - jnp.where(slot_ids >= end, lengths[0, i], 0)
    steps_even = jnp.arange(0, HEAD, 2).astype(F32)
    frequencies = jnp.power(jnp.float32(10000.0), -steps_even / HEAD)
    angles = positions.astype(F32)[:, None] * jnp.tile(frequencies, 4)[None, :]
    cosine, sine = jnp.cos(angles), jnp.sin(angles)
    kpos = jnp.where(key_mask[0] == 1, slot_ids, -1)
    kpos_rows = jnp.broadcast_to(kpos[None, :], (8, row_len))
    kpos_cols = jnp.broadcast_to(kpos[:, None], (row_len, 128))

    half = project(place, x_first, attn, cosine, sine, sqk, None, 0)
    queries, keys, vals, qrot, krot = project(place, x_second, attn, cosine, sine, sqk, half, 1)
    attended, inverse_mass = attend(meta, queries, keys, vals, kpos_rows, docs)
    near = attended[: 2 * local]
    by_core = swap(attended[2 * local :], "mp", 1)
    by_x = swap(jnp.concatenate([near[local:], by_core[local:]]), "mp", 2)
    heads_in = [(near, width, 0, 0), (by_core, width, 0, 0), (by_x, width, 0, 0), (by_x, width, local, 0)]
    branch, h_own = own_call(
        attn_body,
        "attn_out",
        heads_in + [(tokens, D, 0, 0)],
        [one],
        out_parts,
        [(local, D, F32), (local, D, BF16)],
        0,
        2 * local * D * D,
    )

    h_far = swap(h_own, "mp", 2)
    *saved_own, sum_own = ffn_forward(h_own, weights, sup, sgate, F32)
    *saved_far, sum_far = ffn_forward(h_far, weights, sup, sgate, BF16)
    result, gm_own, keep_two, by_two = own_call(
        turn_body,
        "turn",
        [(sum_own, D, 0, 0), (swap(sum_far, "mp", 2), D, 0, 0), (branch, D, 0, 0), (tokens, D, 0, 0), (cotangent, D, 0, 0)],
        [one, two],
        [],
        [(local, D, BF16), (local, D, BF16), (local, D, F32)],
        1,
        60 * local * D,
    )
    gm_far = swap(gm_own, "mp", 2)
    gu_own, gg_own, bu_own, bg_own, gh_own = ffn_backward(gm_own, weights, saved_own, sup, sgate, F32)
    gu_far, gg_far, bu_far, bg_far, gh_far = ffn_backward(gm_far, weights, saved_far, sup, sgate, BF16)
    gh_over = swap(gh_far, "mp", 2)

    down_mine, down_other = weight_grad(
        down_grad_body,
        place,
        (gm_own, gm_far),
        (saved_own[1], saved_far[1]),
        [jax.ShapeDtypeStruct((D, part), BF16)] * 2,
        [pl.BlockSpec((D, TILE), lambda t, m: (0, t))] * 2,
    )
    ups = weights.shape[:2] + (2,) + weights.shape[3:]
    ups = weight_grad(
        up_grad_body,
        place,
        (h_own, h_far),
        (gu_own, gu_far, gg_own, gg_far),
        jax.ShapeDtypeStruct(ups, BF16),
        pl.BlockSpec(ups[:4] + (TILE,), lambda t, m: (0, 0, 0, 0, t)),
    )
    grad_ups = lax.psum_scatter(
        ups.reshape(-1, part), ("dp", "mp"), scatter_dimension=0, tiled=True, axis_index_groups=chip_groups()
    ).astype(F32)
    grad_up, grad_gate = jnp.split(grad_ups, 2, axis=0)
    grad_down = scatter(down_mine.astype(F32) + swap(down_other, "mp", 1).astype(F32)).T

    grad_attn, grad_x, att0, att1, att2, att3, by_one = own_call(
        attn_back_body,
        "attn_back_out",
        [(gh_own, D, 0, 0), (gh_over, D, 0, 0), (keep_two, D, 0, 0), (branch, D, 0, 0), (tokens, D, 0, 0)],
        [one],
        out_parts,
        [(local, D, BF16), (local, D, F32)] + [(local, width, BF16)] * 4,
        1,
        2 * local * D * D,
    )
    back_x = swap(jnp.concatenate([att2, att3]), "mp", 2)
    back_core = swap(jnp.concatenate([att1, back_x[local:]]), "mp", 1)
    g_att = jnp.concatenate([att0, back_x[:local], back_core])
    outs = [dot(grad_attn, a[s : s + local], 0, 0) for a, _, s, _ in heads_in]
    core_out = swap(jnp.concatenate([outs[1], outs[3]], axis=1).astype(BF16), "mp", 1)
    over_out = swap((outs[2] + core_out[:, width:].astype(F32)).astype(BF16), "mp", 2)
    grad_out = scatter(outs[0] + core_out[:, :width].astype(F32) + over_out.astype(F32)).T

    grads, g_sqk = attend_back(
        meta, queries, qrot, attended, inverse_mass, g_att, keys, vals, krot, kpos_cols, cosine, sine, sqk, docs
    )
    g_first, g_second = grads[: 2 * local], grads[2 * local :]
    qkv = attn[:, : 3 * width]
    to_core = swap(dot(g_second, qkv, 1, 1).astype(BF16), "mp", 1)
    partial = dot(g_first, qkv, 1, 1)
    to_x = swap((partial[local:] + to_core[local:].astype(F32)).astype(BF16), "mp", 2)
    grad_tokens = grad_x + partial[:local] + to_core[:local].astype(F32) + to_x.astype(F32)
    grad_qkv = scatter(dot(x_first, g_first, 0, 0) + dot(x_second, g_second, 0, 0))
    g_qkv = [grad_qkv[:, i * width : (i + 1) * width] for i in range(3)]

    def placed(array, index):
        slots = lax.broadcasted_iota(jnp.int32, (4, 1), 0)
        return jnp.where(slots == index, array[None], 0.0)

    def quarters(own, far):
        by = own[:, 0] + far[:, 0]
        return (placed(by[0], m & 2) + placed(by[1], (m & 2) + 1)).reshape(devices, -1)

    rows = [
        quarters(bu_own, bu_far),
        quarters(bg_own, bg_far),
        placed(g_sqk[0], m).reshape(devices, -1),
        by_one[0].reshape(devices, -1),
        by_two[0].reshape(devices, -1),
    ]
    small = jnp.sum(to_all(jnp.concatenate(rows, axis=1)), axis=0)
    cuts, start = [], 0
    for piece in rows:
        cuts.append(small[start : start + piece.shape[1]])
        start += piece.shape[1]
    g_sup, g_sgate, g_sqk, g_alpha_one, g_alpha_two = cuts

    pieces = tuple(g_qkv) + (grad_out, grad_up, grad_gate, grad_down)
    pieces = pieces + (g_sqk, g_sup, g_sgate, g_alpha_one, g_alpha_two)
    squares = jnp.float32(0.0)
    for piece in pieces:
        squares = squares + jnp.sum(piece * piece)
    squares = jnp.sum(to_all(jnp.broadcast_to(squares, (devices, 128))), axis=0)
    grad_norm = jnp.sqrt(squares[0])
    mean_alphas = jnp.stack([jnp.mean(alpha_one), jnp.mean(alpha_two)])
    return (result, grad_tokens) + pieces + (grad_norm, mean_alphas)


def solution(mesh):
    both_axes = P(("dp", "mp"))
    rows = P(("dp", "mp"), None)
    in_specs = (
        (rows, rows, P("dp", None), P("dp", None))
        + (P("dp", "mp"),) * 3
        + (P("mp", "dp"),)
        + (P("dp", "mp"),) * 2
        + (P("mp", "dp"),)
        + (both_axes,) * 5
    )
    out_specs = (
        (rows, rows)
        + (P("dp", "mp"),) * 3
        + (P("mp", "dp"),)
        + (P("dp", "mp"),) * 2
        + (P("mp", "dp"),)
        + (both_axes,) * 5
        + (P(), P())
    )
    return jax.shard_map(shards, mesh=mesh, in_specs=in_specs, out_specs=out_specs, check_vma=False)
```

```python
import functools

import jax
import jax.numpy as jnp
from jax import lax
from jax.experimental import pallas as pl
from jax.experimental.layout import Layout, with_layout_constraint
from jax.experimental.pallas import tpu as pltpu
from jax.sharding import PartitionSpec as P

D = 1024
HEADS = 16
HEAD = D // HEADS
EPS = 1e-06
NEG = -1e30
BLOCK = 256
F32 = jnp.float32
BF16 = jnp.bfloat16


def mean_rows(tensor):
    return jnp.mean(tensor, axis=-1, keepdims=True)


def normed(tensor):
    factor = lax.rsqrt(mean_rows(tensor * tensor) + EPS)
    return tensor * factor, factor


def normed_back(incoming, unit, factor):
    return factor * (incoming - unit * mean_rows(incoming * unit))


def dot(left, right, left_dim=1, right_dim=0):
    return lax.dot_general(
        left, right, (((left_dim,), (right_dim,)), ((), ())), preferred_element_type=F32
    )


RING = (0, 2, 4, 6, 7, 5, 3, 1)


def swap(array, axis, bit):
    size = lax.axis_size(axis)
    return lax.ppermute(array, axis, [(i, i ^ bit) for i in range(size)])


def to_z(array, step):
    return lax.ppermute(
        array, "dp", [(z * 2 + y, ((z + step) % 4) * 2 + y) for z in range(4) for y in range(2)]
    )


def around(array, step):
    return lax.ppermute(array, "dp", [(RING[p], RING[(p + step) % 8]) for p in range(8)])


def after(array, *others):
    if not others:
        return array
    return lax.optimization_barrier((array,) + others)[0]


def gather(shard, before):
    if lax.axis_size("dp") != 8:
        return lax.all_gather(shard, "dp", axis=0, tiled=True)
    d = lax.axis_index("dp")
    rows, width = shard.shape
    place = jnp.where((d & 1) == 0, d >> 1, 7 - (d >> 1))

    def put(full, part, step):
        q = (place + step) & 7
        index = jnp.where(q < 4, 2 * q, 2 * (7 - q) + 1)
        return lax.dynamic_update_slice(full, part, (index * rows, jnp.int32(0)))

    full = put(jnp.zeros((8 * rows, width), shard.dtype), shard, 0)
    ahead = behind = shard
    for step in (1, 2, 3, 4):
        if step > 1:
            ahead, behind = lax.optimization_barrier((ahead, behind) + tuple(before[step - 1]))[:2]
        ahead = around(ahead, 1)
        full = put(full, ahead, -step)
        if step < 4:
            behind = around(behind, -1)
            full = put(full, behind, step)
    return full


def chip_groups():
    return [
        [d * 4 + 2 * x + core for d in range(lax.axis_size("dp")) for core in range(2)]
        for x in range(2)
    ]


def scatter_y(*grads):
    if lax.axis_size("dp") != 8:
        whole = jnp.concatenate(grads, axis=1)
        return whole, whole
    y = lax.axis_index("dp") & 1
    grads = [g.reshape(4, 2, g.shape[0] // 8, g.shape[1]) for g in grads]

    def rows(index, kind):
        parts = [lax.dynamic_index_in_dim(g, index, axis=1, keepdims=False).astype(kind) for g in grads]
        return jnp.concatenate(parts, axis=2)

    sent = rows(1 - y, BF16)
    return rows(y, F32) + swap(sent, "dp", 1).astype(F32), sent


def scatter_z(half):
    if lax.axis_size("dp") != 8:
        return lax.psum_scatter(half.astype(F32), "dp", scatter_dimension=0, tiled=True)
    z = lax.axis_index("dp") >> 1
    total = lax.dynamic_index_in_dim(half, z, axis=0, keepdims=False)
    for step in (1, 2, 3):
        part = lax.dynamic_index_in_dim(half, (z + step) & 3, axis=0, keepdims=False)
        total = total + to_z(part.astype(BF16), step).astype(F32)
    return total


def turned(array):
    return with_layout_constraint(array, Layout(major_to_minor=(0, 1))).T


def to_all(rows):
    return lax.all_to_all(rows, ("dp", "mp"), 0, 0, tiled=True)


def rotate_half(tensor):
    width = tensor.shape[-1]
    lane = lax.broadcasted_iota(jnp.int32, tensor.shape, 1)
    ahead = pltpu.roll(tensor, width - HEAD // 2, 1)
    behind = pltpu.roll(tensor, HEAD // 2, 1)
    return jnp.where((lane & (HEAD - 1)) < HEAD // 2, -ahead, behind)


def head_mean(tensor):
    width = tensor.shape[-1]
    row = lax.broadcasted_iota(jnp.int32, (width, width), 0) // HEAD
    col = lax.broadcasted_iota(jnp.int32, (width, width), 1) // HEAD
    ones = jnp.where(row == col, 1.0 / HEAD, 0.0).astype(BF16)
    high = tensor.astype(BF16)
    rest = (tensor - high.astype(F32)).astype(BF16)
    return dot(high, ones) + dot(rest, ones)


def wide(table):
    return jnp.concatenate([table, table], axis=1)


def project_body(m_ref, x_ref, w_ref, cos_ref, sin_ref, sqk_ref, *refs):
    q_ref, k_ref, v_ref, qr_ref, kr_ref = refs[-5:]
    rows = x_ref[...]
    cosine, sine = wide(cos_ref[...]), wide(sin_ref[...])
    scale = sqk_ref[0:1, :]
    width = q_ref.shape[1]
    raws = [dot(rows, w_ref[:, i * width : (i + 1) * width]) for i in range(3)]
    v_ref[...] = raws[2].astype(BF16)
    for raw, out_ref, rot_ref in ((raws[0], q_ref, qr_ref), (raws[1], k_ref, kr_ref)):
        turned = raw * cosine + rotate_half(raw) * sine
        rot_ref[...] = turned
        unit = turned * lax.rsqrt(head_mean(turned * turned) + EPS)
        out_ref[...] = (unit * scale).astype(BF16)


def project(place, x_rows, weight, cosine, sine, sqk, previous, first):
    rows, width = x_rows.shape[0], weight.shape[1] // 4
    total = cosine.shape[0]
    per = total // 4 // BLOCK

    def row_block(i, m):
        return ((m[0] ^ (first + 2 * (i // per))) * per + i % per, 0)

    any_spec = pl.BlockSpec(memory_space=pl.ANY)
    table = pl.BlockSpec((BLOCK, cosine.shape[1]), row_block)
    out = pl.BlockSpec((BLOCK, width), row_block)
    shapes = [jax.ShapeDtypeStruct((total, width), t) for t in (BF16, BF16, BF16, F32, F32)]
    extra = list(previous) if previous is not None else []
    return pl.pallas_call(
        project_body,
        out_shape=shapes,
        grid_spec=pltpu.PrefetchScalarGridSpec(
            num_scalar_prefetch=1,
            grid=(rows // BLOCK,),
            in_specs=[
                pl.BlockSpec((BLOCK, x_rows.shape[1]), lambda i, m: (i, 0)),
                pl.BlockSpec((x_rows.shape[1], 3 * width), lambda i, m: (0, 0)),
                table,
                table,
                pl.BlockSpec((8, width), lambda i, m: (0, 0)),
            ]
            + [any_spec] * len(extra),
            out_specs=[out] * 5,
        ),
        input_output_aliases={6 + i: i for i in range(len(extra))},
        cost_estimate=pl.CostEstimate(
            flops=6 * rows * D * width, bytes_accessed=8 * rows * D, transcendentals=rows
        ),
        name="project",
    )(place, x_rows, weight, cosine, sine, sqk, *extra)


def head_lanes(array, head):
    lane = lax.broadcasted_iota(jnp.int32, array.shape, 1)
    return jnp.where(lane // HEAD == head, array, jnp.zeros_like(array))


def stack_heads(array):
    heads = array.shape[1] // HEAD
    return jnp.concatenate([head_lanes(array, h) for h in range(heads)], axis=0)


def doc_start(meta_ref, docs, slots):
    start = jnp.zeros_like(slots)
    end = 0
    for i in range(docs):
        length = meta_ref[1 + i]
        end = end + length
        start = start + jnp.where(slots >= end, length, 0)
    return start


def slot_place(rel):
    return (rel >> 1) + 2 * (rel & 1)


def block_at(block):
    return pl.ds(pl.multiple_of(block * BLOCK, BLOCK), BLOCK)


def split_heads(source_ref, split_ref):
    def one(block, carry):
        split_ref[block] = stack_heads(source_ref[block_at(block), :])
        return carry

    lax.fori_loop(0, source_ref.shape[0] // BLOCK, one, 0)


def attend_body(docs, first, meta_ref, q_ref, k_ref, v_ref, kpos_ref, *refs):
    o_ref, inv_ref, acc_ref, sum_ref, vs_ref = refs[-5:]
    per = k_ref.shape[0] // 4 // BLOCK
    index = pl.program_id(0)
    step = ((first + index // per) ^ meta_ref[0]) * per + index % per
    heads = q_ref.shape[1] // HEAD
    base = step * BLOCK
    low = doc_start(meta_ref, docs, base) // BLOCK

    @pl.when(index == 0)
    def _():
        split_heads(v_ref, vs_ref)

    scaled = q_ref[...] * jnp.bfloat16(HEAD**-0.5)
    queries = [head_lanes(scaled, h) for h in range(heads)]
    rows = lax.broadcasted_iota(jnp.int32, (BLOCK, BLOCK), 0) + base
    starts = doc_start(meta_ref, docs, rows)
    acc_ref[...] = jnp.zeros_like(acc_ref)
    sum_ref[...] = jnp.zeros_like(sum_ref)

    def visit(block, allowed):
        keys = k_ref[block_at(block), :]
        bias = jnp.where(allowed, 0.0, NEG)
        expos = []
        for h in range(heads):
            expo = jnp.exp(dot(queries[h], keys, 1, 1) + bias)
            sum_ref[h * BLOCK : (h + 1) * BLOCK, :] += expo[:, :128] + expo[:, 128:]
            expos.append(expo.astype(BF16))
        acc_ref[...] += dot(jnp.concatenate(expos, axis=1), vs_ref[block])

    def off_diagonal(block, carry):
        visit(block, kpos_ref[0:1, block_at(block)] >= starts)
        return carry

    lax.fori_loop(low, step, off_diagonal, 0)
    cols = lax.broadcasted_iota(jnp.int32, (BLOCK, BLOCK), 1) + base
    visit(step, ((kpos_ref[0:1, block_at(step)] >= starts) & (cols <= rows)) | (cols == rows))
    lane = lax.broadcasted_iota(jnp.int32, (BLOCK, q_ref.shape[1]), 1) // HEAD
    inverse = jnp.zeros((BLOCK, q_ref.shape[1]), F32)
    for h in range(heads):
        mass = jnp.sum(sum_ref[h * BLOCK : (h + 1) * BLOCK, :], axis=1, keepdims=True)
        inverse = jnp.where(lane == h, 1.0 / mass, inverse)
    inv_ref[...] = inverse
    o_ref[...] = (acc_ref[...] * inverse).astype(BF16)


def attend(meta, queries, keys, vals, kpos, docs, first, previous):
    total, width = queries.shape
    per = total // 4 // BLOCK
    heads = width // HEAD
    whole = pl.BlockSpec((total, width), lambda i, m: (0, 0))

    def natural(i, m):
        return (((first + i // per) ^ m[0]) * per + i % per, 0)

    block = pl.BlockSpec((BLOCK, width), natural)
    out = pl.BlockSpec((BLOCK, width), lambda i, m: ((first ^ 2) * per + i, 0))
    extra = list(previous)
    return pl.pallas_call(
        functools.partial(attend_body, docs, first),
        out_shape=[
            jax.ShapeDtypeStruct((total, width), BF16),
            jax.ShapeDtypeStruct((total, width), F32),
        ],
        grid_spec=pltpu.PrefetchScalarGridSpec(
            num_scalar_prefetch=1,
            grid=(2 * per,),
            in_specs=[block, whole, whole, pl.BlockSpec((8, total), lambda i, m: (0, 0))]
            + [pl.BlockSpec(memory_space=pl.ANY)] * len(extra),
            out_specs=[out, block],
            scratch_shapes=[
                pltpu.VMEM((BLOCK, width), F32),
                pltpu.VMEM((heads * BLOCK, 128), F32),
                pltpu.VMEM((total // BLOCK, heads * BLOCK, width), BF16),
            ],
        ),
        input_output_aliases={5 + i: i for i in range(len(extra))},
        cost_estimate=pl.CostEstimate(
            flops=8_000_000_000, bytes_accessed=8 * total * width, transcendentals=3_000_000
        ),
        name="attend",
    )(meta, queries, keys, vals, kpos, *extra)


def finish(grad, turned, cosine, sine, scale):
    factor = lax.rsqrt(head_mean(turned * turned) + EPS)
    unit = turned * factor
    by_scale = jnp.sum(grad * unit, axis=0, keepdims=True)
    scaled = grad * scale
    back = factor * (scaled - unit * head_mean(scaled * unit))
    raw = back * cosine - rotate_half(back) * sine
    return raw.astype(BF16), by_scale


def back_body(
    docs,
    meta_ref,
    q_ref,
    qr_ref,
    o_ref,
    inv_ref,
    do_ref,
    k_ref,
    v_ref,
    kr_ref,
    kpos_ref,
    cos_ref,
    sin_ref,
    sqk_ref,
    g_ref,
    gs_ref,
    dq_ref,
    dk_ref,
    dv_ref,
    ks_ref,
):
    step = pl.program_id(0)
    width = q_ref.shape[1]
    heads = width // HEAD
    per = k_ref.shape[0] // 4 // BLOCK
    base = step * BLOCK
    low = doc_start(meta_ref, docs, base) // BLOCK

    @pl.when(step == 0)
    def _():
        dk_ref[...] = jnp.zeros_like(dk_ref)
        dv_ref[...] = jnp.zeros_like(dv_ref)
        gs_ref[...] = jnp.zeros_like(gs_ref)
        split_heads(k_ref, ks_ref)

    dq_ref[...] = jnp.zeros_like(dq_ref)
    scaled = q_ref[...] * jnp.bfloat16(HEAD**-0.5)
    queries = [head_lanes(scaled, h) for h in range(heads)]
    all_queries = jnp.concatenate(queries, axis=0)
    upward = do_ref[...].astype(F32) * inv_ref[...]
    ups = [head_lanes(upward.astype(BF16), h) for h in range(heads)]
    all_ups = jnp.concatenate(ups, axis=0)
    picks = lax.broadcasted_iota(jnp.int32, (8, width), 0)
    lanes = lax.broadcasted_iota(jnp.int32, (8, width), 1) // HEAD
    delta = lax.dot_general(
        jnp.where(picks == lanes, 1.0, 0.0).astype(F32),
        upward * o_ref[...].astype(F32),
        (((1,), (1,)), ((), ())),
        precision=lax.Precision.HIGHEST,
        preferred_element_type=F32,
    )
    cols = lax.broadcasted_iota(jnp.int32, (BLOCK, BLOCK), 1) + base
    starts = doc_start(meta_ref, docs, cols)

    def visit(block, allowed):
        at = block_at(block)
        keys, vals = k_ref[at, :], v_ref[at, :]
        bias = jnp.where(allowed, 0.0, NEG)
        expos, slopes = [], []
        for h in range(heads):
            expo = jnp.exp(dot(keys, queries[h], 1, 1) + bias)
            expos.append(expo.astype(BF16))
            slope = expo * (dot(vals, ups[h], 1, 1) - delta[h : h + 1, :])
            slopes.append(slope.astype(BF16))
        dv_ref[at, :] += dot(jnp.concatenate(expos, axis=1), all_ups)
        dk_ref[at, :] += dot(jnp.concatenate(slopes, axis=1), all_queries)
        dq_ref[...] += dot(jnp.concatenate(slopes, axis=0), ks_ref[block], 0, 0)

    def key_slots(block):
        return wide(kpos_ref[block_at(block), :])

    def off_diagonal(block, carry):
        visit(block, key_slots(block) >= starts)
        return carry

    lax.fori_loop(low, step, off_diagonal, 0)
    rows = lax.broadcasted_iota(jnp.int32, (BLOCK, BLOCK), 0) + base
    visit(step, ((key_slots(step) >= starts) & (rows <= cols)) | (rows == cols))

    scale = sqk_ref[0:1, :]
    here = pl.ds(pl.multiple_of(base, BLOCK), BLOCK)
    raw, by_scale = finish(
        dq_ref[...] * (HEAD**-0.5),
        qr_ref[...],
        wide(cos_ref[here, :]),
        wide(sin_ref[here, :]),
        scale,
    )
    slot = slot_place(meta_ref[0] ^ (step // per)) * per + step % per
    g_ref[pl.ds(pl.multiple_of(slot * BLOCK, BLOCK), BLOCK), :width] = raw
    gs_ref[0:1, :] += by_scale

    @pl.when(step == pl.num_programs(0) - 1)
    def _():
        def one(block, carry):
            at = pl.ds(pl.multiple_of(block * BLOCK, BLOCK), BLOCK)
            slot = slot_place(meta_ref[0] ^ (block // per)) * per + block % per
            to = pl.ds(pl.multiple_of(slot * BLOCK, BLOCK), BLOCK)
            raw, by_scale = finish(
                dk_ref[at, :], kr_ref[at, :], wide(cos_ref[at, :]), wide(sin_ref[at, :]), scale
            )
            g_ref[to, width : 2 * width] = raw
            gs_ref[0:1, :] += by_scale
            g_ref[to, 2 * width :] = dv_ref[at, :].astype(BF16)
            return carry

        lax.fori_loop(0, pl.num_programs(0), one, 0)


def attend_back(meta, queries, qrot, out, inverse, grad, keys, vals, krot, kpos, cosine, sine, sqk, docs):
    total, width = queries.shape
    per = total // 4 // BLOCK

    def rel(i, m):
        return ((m[0] ^ (i // per) ^ 2) * per + i % per, 0)

    whole = pl.BlockSpec((total, width), lambda i, m: (0, 0))
    half = pl.BlockSpec((total, 128), lambda i, m: (0, 0))
    block = pl.BlockSpec((BLOCK, width), lambda i, m: (i, 0))
    moved = pl.BlockSpec((BLOCK, width), rel)
    return pl.pallas_call(
        functools.partial(back_body, docs),
        out_shape=[
            jax.ShapeDtypeStruct((total, 3 * width), BF16),
            jax.ShapeDtypeStruct((8, width), F32),
        ],
        grid_spec=pltpu.PrefetchScalarGridSpec(
            num_scalar_prefetch=1,
            grid=(total // BLOCK,),
            in_specs=[block, block, moved, block, moved, whole, whole, whole, half, half, half]
            + [pl.BlockSpec((8, width), lambda i, m: (0, 0))],
            out_specs=[
                pl.BlockSpec((total, 3 * width), lambda i, m: (0, 0)),
                pl.BlockSpec((8, width), lambda i, m: (0, 0)),
            ],
            scratch_shapes=[
                pltpu.VMEM((BLOCK, width), F32),
                pltpu.VMEM((total, width), F32),
                pltpu.VMEM((total, width), F32),
                pltpu.VMEM((total // BLOCK, width // HEAD * BLOCK, width), BF16),
            ],
        ),
        cost_estimate=pl.CostEstimate(
            flops=40_000_000_000, bytes_accessed=12 * total * width, transcendentals=6_000_000
        ),
        name="attend_back",
    )(meta, queries, qrot, out, inverse, grad, keys, vals, krot, kpos, cosine, sine, sqk)


TILE = 256


def weight_tile(weight_ref, part, index):
    return weight_ref[:, part, index].reshape(D, TILE)


def weight_spec(weights):
    return pl.BlockSpec(weights.shape[:4] + (TILE,), lambda t: (0, 0, 0, 0, t))


def forward_body(
    h_ref, w_ref, sup_ref, sgate_ref, gate_ref, act_ref, by_up_ref, by_gate_ref, out_ref, acc_ref
):
    t = pl.program_id(0)
    rows = h_ref[...]
    acts = []
    for part in range(2):
        sup, sgate = sup_ref[part, 0:1, :], sgate_ref[part, 0:1, :]
        scaled = sup * dot(rows, weight_tile(w_ref, part, 0))
        gate_proj = dot(rows, weight_tile(w_ref, part, 1))
        outer = sgate * gate_proj
        sigma = jax.nn.sigmoid(outer)
        silu = outer * sigma
        acts.append((scaled * silu).astype(BF16))
        gate_ref[part] = gate_proj.astype(BF16)
        act_ref[part] = acts[part]
        by_up_ref[part] = (sup * silu).astype(BF16)
        by_gate_ref[part] = ((sgate * scaled) * (sigma + silu * (1.0 - sigma))).astype(BF16)
    total = dot(
        jnp.concatenate(acts, axis=1),
        jnp.concatenate([weight_tile(w_ref, part, 2) for part in range(2)], axis=1),
        1,
        1,
    )
    add_up(t, total, acc_ref, out_ref)


def add_up(t, total, acc_ref, out_ref):
    @pl.when(t == 0)
    def _():
        acc_ref[...] = total

    @pl.when((t > 0) & (t < pl.num_programs(0) - 1))
    def _():
        acc_ref[...] += total

    @pl.when(t == pl.num_programs(0) - 1)
    def _():
        out_ref[...] = (acc_ref[...] + total).astype(out_ref.dtype)


def ffn_specs(count):
    whole = pl.BlockSpec((count, D), lambda t: (0, 0))
    tile = pl.BlockSpec((2, count, TILE), lambda t: (0, 0, t))
    scale = pl.BlockSpec((2, 8, TILE), lambda t: (0, 0, t))
    return whole, tile, scale


def ffn_forward(rows, weights, sup, sgate, kind):
    count, hidden = rows.shape[0], sup.shape[2]
    whole, tile, scale = ffn_specs(count)
    return pl.pallas_call(
        forward_body,
        out_shape=[jax.ShapeDtypeStruct((2, count, hidden), BF16)] * 4
        + [jax.ShapeDtypeStruct((count, D), kind)],
        grid=(hidden // TILE,),
        in_specs=[whole, weight_spec(weights), scale, scale],
        out_specs=[tile] * 4 + [whole],
        scratch_shapes=[pltpu.VMEM((count, D), F32)],
        cost_estimate=pl.CostEstimate(
            flops=12 * count * D * hidden,
            bytes_accessed=12 * D * hidden + 12 * count * hidden,
            transcendentals=2 * count * hidden,
        ),
        name="ffn_forward",
    )(rows, weights, sup, sgate)


def backward_body(pieces, *refs):
    rows = jnp.concatenate([ref[...] for ref in refs[:pieces]], axis=0)
    w_ref, gate_ref, act_ref, by_up_ref, by_gate_ref, sup_ref, sgate_ref = refs[pieces : pieces + 7]
    gu_ref, gg_ref, bu_ref, bg_ref, out_ref, acc_ref = refs[pieces + 7 :]
    t = pl.program_id(0)
    lefts, rights = [], []
    for part in range(2):
        g_act = dot(rows, weight_tile(w_ref, part, 2))
        g_up = (g_act * by_up_ref[part].astype(F32)).astype(BF16)
        g_gate = g_act * by_gate_ref[part].astype(F32)
        up_sum = jnp.sum(g_act * act_ref[part].astype(F32), axis=0, keepdims=True)
        gate_sum = jnp.sum(g_gate * gate_ref[part].astype(F32), axis=0, keepdims=True)
        g_gate = g_gate.astype(BF16)
        bu_ref[part, 0:1, :] = up_sum / sup_ref[part, 0:1, :]
        bg_ref[part, 0:1, :] = gate_sum / sgate_ref[part, 0:1, :]
        gu_ref[part] = g_up
        gg_ref[part] = g_gate
        lefts += [g_up, g_gate]
        rights += [weight_tile(w_ref, part, 0), weight_tile(w_ref, part, 1)]
    total = dot(jnp.concatenate(lefts, axis=1), jnp.concatenate(rights, axis=1), 1, 1)
    add_up(t, total, acc_ref, out_ref)


def ffn_backward(grads, weights, saved, sup, sgate, kind):
    count, hidden = sum(g.shape[0] for g in grads), sup.shape[2]
    whole, tile, scale = ffn_specs(count)
    return pl.pallas_call(
        functools.partial(backward_body, len(grads)),
        out_shape=[jax.ShapeDtypeStruct((2, count, hidden), BF16)] * 2
        + [jax.ShapeDtypeStruct((2, 8, hidden), F32)] * 2
        + [jax.ShapeDtypeStruct((count, D), kind)],
        grid=(hidden // TILE,),
        in_specs=[pl.BlockSpec(g.shape, lambda t: (0, 0)) for g in grads]
        + [weight_spec(weights)]
        + [tile] * 4
        + [scale, scale],
        out_specs=[tile, tile, scale, scale, whole],
        scratch_shapes=[pltpu.VMEM((count, D), F32)],
        cost_estimate=pl.CostEstimate(
            flops=12 * count * D * hidden,
            bytes_accessed=12 * D * hidden + 24 * count * hidden,
            transcendentals=0,
        ),
        name="ffn_backward",
    )(*grads, weights, *saved, sup, sgate)


def weight_body(counts, *refs):
    h_count, g_count, m_count = counts
    take = iter(refs)
    hs = [next(take) for _ in range(h_count)]
    ms = [next(take) for _ in range(m_count)]
    ups, gates, acts = [[next(take) for _ in range(g_count)] for _ in range(3)]
    out_ref, ht_ref, mt_ref = refs[-3:]

    @pl.when(pl.program_id(0) == 0)
    def _():
        for pieces, to_ref in ((hs, ht_ref), (ms, mt_ref)):
            start = 0
            for ref in pieces:
                to_ref[:, start : start + ref.shape[0]] = ref[...].T
                start += ref.shape[0]

    for index, (left_ref, rights) in enumerate(((ht_ref, ups), (ht_ref, gates), (mt_ref, acts))):
        for part in range(2):
            right = jnp.concatenate([ref[part] for ref in rights], axis=0)
            total = dot(left_ref[...], right).astype(BF16)
            out_ref[:, part, index] = total.reshape(out_ref.shape[0], out_ref.shape[3], TILE)


def weight_grads(hs, ms, ups, gates, acts, shape):
    hidden = ups[0].shape[2]
    count = sum(h.shape[0] for h in hs)

    def whole(array):
        return pl.BlockSpec(array.shape, lambda t: (0, 0))

    def tile(array):
        return pl.BlockSpec((2, array.shape[1], TILE), lambda t: (0, 0, t))

    lefts, rights = list(hs) + list(ms), list(ups) + list(gates) + list(acts)
    return pl.pallas_call(
        functools.partial(weight_body, (len(hs), len(ups), len(ms))),
        out_shape=jax.ShapeDtypeStruct(shape, BF16),
        grid=(hidden // TILE,),
        in_specs=[whole(a) for a in lefts] + [tile(a) for a in rights],
        out_specs=pl.BlockSpec(shape[:4] + (TILE,), lambda t: (0, 0, 0, 0, t)),
        scratch_shapes=[pltpu.VMEM((D, count), BF16)] * 2,
        cost_estimate=pl.CostEstimate(
            flops=12 * count * D * hidden,
            bytes_accessed=12 * D * hidden + 12 * count * hidden,
            transcendentals=0,
        ),
        name="weight_grads",
    )(*lefts, *rights)


def own_call(body, name, rows_in, vectors, wholes, outs, sums, flops):
    count = outs[0][0]
    blocks = count // BLOCK

    def rows_spec(width, skip, column):
        return pl.BlockSpec((BLOCK, width), lambda i: (skip // BLOCK + i, column))

    in_specs = [rows_spec(w, s, c) for _, w, s, c in rows_in]
    in_specs += [pl.BlockSpec((8, v.shape[1]), lambda i: (0, 0)) for v in vectors]
    in_specs += [pl.BlockSpec((D, w), lambda i, c=c: (0, c)) for _, w, c in wholes]
    shapes = [jax.ShapeDtypeStruct((count, w), t) for count, w, t in outs]
    shapes += [jax.ShapeDtypeStruct((8, D), F32)] * sums
    out_specs = [pl.BlockSpec((BLOCK, w), lambda i: (i, 0)) for _, w, _ in outs]
    out_specs += [pl.BlockSpec((8, D), lambda i: (0, 0))] * sums
    return pl.pallas_call(
        body,
        out_shape=shapes,
        grid=(blocks,),
        in_specs=in_specs,
        out_specs=out_specs,
        cost_estimate=pl.CostEstimate(
            flops=flops, bytes_accessed=20 * count * D, transcendentals=count
        ),
        name=name,
    )(*[a for a, *_ in rows_in], *vectors, *[a for a, *_ in wholes])


def first_update(branch, x_rows, alpha):
    h_attn, attn_factor = normed(branch)
    hidden, one_factor = normed(x_rows + alpha * (h_attn - x_rows))
    return h_attn, attn_factor, hidden, one_factor


def attn_body(a0, a1, a2, a3, x_ref, alpha_ref, w0, w1, w2, w3, branch_ref, low_ref):
    branch = dot(a0[...], w0[...], 1, 1) + dot(a1[...], w1[...], 1, 1)
    branch = branch + dot(a2[...], w2[...], 1, 1) + dot(a3[...], w3[...], 1, 1)
    branch_ref[...] = branch
    hidden = first_update(branch, x_ref[...].astype(F32), alpha_ref[0:1, :])[2]
    low_ref[...] = hidden.astype(BF16)


def turn_body(own_ref, far_ref, branch_ref, x_ref, cot_ref, one_ref, two_ref, *refs):
    out_ref, keep_ref, gm_ref, sum_ref = refs[-4:]
    hidden = first_update(branch_ref[...], x_ref[...].astype(F32), one_ref[0:1, :])[2]
    alpha = two_ref[0:1, :]
    h_mlp, mlp_factor = normed(own_ref[...] + far_ref[...].astype(F32))
    step = h_mlp - hidden
    result, two_factor = normed(hidden + alpha * step)
    out_ref[...] = result.astype(BF16)
    grad_two = normed_back(cot_ref[...].astype(F32), result, two_factor)
    keep_ref[...] = grad_two * (1.0 - alpha)
    gm_ref[...] = normed_back(grad_two * alpha, h_mlp, mlp_factor).astype(BF16)

    sum_ref[0:1, :] = jnp.sum(grad_two * step, axis=0, keepdims=True)


def turn(chunk, own, far, branch, x_rows, cotangent, one, two, previous):
    count = branch.shape[0]
    rows = pl.BlockSpec((BLOCK, D), lambda i: (chunk, 0))
    first = pl.BlockSpec((BLOCK, D), lambda i: (0, 0))
    vector = pl.BlockSpec((8, D), lambda i: (0, 0))
    extra = list(previous)
    return pl.pallas_call(
        turn_body,
        out_shape=[
            jax.ShapeDtypeStruct((count, D), BF16),
            jax.ShapeDtypeStruct((count, D), F32),
            jax.ShapeDtypeStruct((BLOCK, D), BF16),
            jax.ShapeDtypeStruct((8, D), F32),
        ],
        grid=(1,),
        in_specs=[rows, first, rows, rows, rows, vector, vector]
        + [pl.BlockSpec(memory_space=pl.ANY)] * len(extra),
        out_specs=[rows, rows, first, vector],
        input_output_aliases={7 + i: i for i in range(len(extra))},
        cost_estimate=pl.CostEstimate(
            flops=60 * BLOCK * D, bytes_accessed=20 * BLOCK * D, transcendentals=BLOCK
        ),
        name="turn",
    )(own, far, branch, x_rows, cotangent, one, two, *extra)


def attn_back_body(
    own_ref, far_ref, keep_ref, branch_ref, x_ref, one_ref, w0, w1, w2, w3, ga_ref, gt_ref, o0, o1, o2, o3, sum_ref
):
    x_rows, alpha = x_ref[...].astype(F32), one_ref[0:1, :]
    h_attn, attn_factor, hidden, one_factor = first_update(branch_ref[...], x_rows, alpha)
    incoming = keep_ref[...] + own_ref[...] + far_ref[...].astype(F32)
    grad_one = normed_back(incoming, hidden, one_factor)
    gt_ref[...] = grad_one * (1.0 - alpha)
    grad_attn = normed_back(grad_one * alpha, h_attn, attn_factor).astype(BF16)
    ga_ref[...] = grad_attn
    for weight_ref, out_ref in ((w0, o0), (w1, o1), (w2, o2), (w3, o3)):
        out_ref[...] = dot(grad_attn, weight_ref[...]).astype(BF16)

    @pl.when(pl.program_id(0) == 0)
    def _():
        sum_ref[...] = jnp.zeros_like(sum_ref)

    sum_ref[0:1, :] += jnp.sum(grad_one * (h_attn - x_rows), axis=0, keepdims=True)


def shards(
    tokens,
    cotangent,
    lengths,
    key_mask,
    w_query,
    w_key,
    w_value,
    w_out,
    w_up,
    w_gate,
    w_down,
    s_qk,
    s_up,
    s_gate,
    alpha_attn,
    alpha_mlp,
):
    m = lax.axis_index("mp").astype(jnp.int32)
    devices = lax.axis_size("dp") * lax.axis_size("mp")
    local = tokens.shape[0]
    row_len = key_mask.shape[1]
    docs = lengths.shape[1]
    part = w_up.shape[1]
    width = w_query.shape[1]

    place = m.reshape(1)
    meta = jnp.concatenate([place, lengths[0]])
    slot_ids = jnp.arange(row_len, dtype=jnp.int32)
    positions, end = slot_ids, 0
    for i in range(docs):
        end = end + lengths[0, i]
        positions = positions - jnp.where(slot_ids >= end, lengths[0, i], 0)
    steps_even = jnp.arange(0, HEAD, 2).astype(F32)
    frequencies = jnp.power(jnp.float32(10000.0), -steps_even / HEAD)
    angles = positions.astype(F32)[:, None] * jnp.tile(frequencies, 4)[None, :]
    cosine, sine = jnp.cos(angles), jnp.sin(angles)
    shard = jnp.concatenate([w_up, w_gate, w_down.T], axis=0)
    shard = with_layout_constraint(shard, Layout(major_to_minor=(0, 1)))
    weights = lax.all_gather(
        shard, ("dp", "mp"), axis=0, tiled=True, axis_index_groups=chip_groups()
    ).reshape(-1, 2, 3, shard.shape[0] // 3, part)
    x_halves = [swap(tokens[i * local // 2 : (i + 1) * local // 2], "mp", 2) for i in range(2)]
    x_first = jnp.concatenate([tokens] + x_halves, axis=0)
    x_second = swap(x_first, "mp", 1)
    vector = jnp.concatenate([s_up, s_gate, s_qk, alpha_attn, alpha_mlp])[None]
    every = to_all(jnp.broadcast_to(vector, (devices, vector.shape[1])))
    attn = gather(
        jnp.concatenate([w_query, w_key, w_value, w_out.T], axis=1),
        [(), (x_halves[0], cosine, sine), (), (x_halves[1], every)],
    )
    cuts, start = [], 0
    for piece in (s_up, s_gate, s_qk, alpha_attn, alpha_mlp):
        cuts.append(every[:, start : start + piece.shape[0]].reshape(-1))
        start += piece.shape[0]
    sup_all, sgate_all, sqk_all, alpha_one, alpha_two = cuts

    def quarter(array, index):
        size = array.shape[0] // 4
        return lax.dynamic_slice_in_dim(array, index * size, size)

    def eight(array):
        return jnp.broadcast_to(array[None], (8, array.shape[0]))

    sqk = eight(quarter(sqk_all, m))
    low = m & 2
    sup = jnp.stack([eight(quarter(sup_all, low)), eight(quarter(sup_all, low + 1))])
    sgate = jnp.stack([eight(quarter(sgate_all, low)), eight(quarter(sgate_all, low + 1))])
    one, two = eight(alpha_one), eight(alpha_two)
    out_mine = attn[:, 3 * width :]
    out_core = swap(out_mine, "mp", 1)
    out_over = swap(out_mine, "mp", 2)
    out_cross = swap(out_over, "mp", 1)
    out_parts = [(w, width, 0) for w in (out_mine, out_core, out_over, out_cross)]

    kpos = jnp.where(key_mask[0] == 1, slot_ids, -1)
    kpos_rows = jnp.broadcast_to(kpos[None, :], (8, row_len))
    kpos_cols = jnp.broadcast_to(kpos[:, None], (row_len, 128))

    half = project(place, x_first, attn, cosine, sine, sqk, None, 0)
    queries, keys, vals, qrot, krot = project(place, x_second, attn, cosine, sine, sqk, half, 1)
    half = attend(meta, queries, keys, vals, kpos_rows, docs, 2, ())
    far_core = swap(half[0][local : 2 * local], "mp", 1)
    for_x = jnp.concatenate([half[0][:local], far_core])
    by_x = swap(for_x, "mp", 2)
    half = [after(half[0], for_x), half[1]]
    attended, inverse_mass = attend(meta, queries, keys, vals, kpos_rows, docs, 0, half)
    by_core = swap(attended[3 * local :], "mp", 1)
    heads_in = [(attended, width, 2 * local, 0), (by_core, width, 0, 0), (by_x, width, 0, 0), (by_x, width, local, 0)]
    branch, h_own = own_call(
        attn_body,
        "attn_out",
        heads_in + [(tokens, D, 0, 0)],
        [one],
        out_parts,
        [(local, D, F32), (local, D, BF16)],
        0,
        2 * local * D * D,
    )

    chunks = range(local // BLOCK)
    h_far = [swap(h_own[c * BLOCK : (c + 1) * BLOCK], "mp", 2) for c in chunks]
    *saved_own, sum_own = ffn_forward(h_own, weights, sup, sgate, F32)
    saved_far, sum_far, last = [], [], sum_own
    for c in chunks:
        *saved, last = ffn_forward(after(h_far[c], last), weights, sup, sgate, BF16)
        saved_far.append(saved)
        sum_far.append(swap(last, "mp", 2))
    done, gm_own, gm_far, by_two = (), [], [], 0.0
    for c in chunks:
        *done, gm, by = turn(c, after(sum_own, last), sum_far[c], branch, tokens, cotangent, one, two, done)
        gm_own.append(gm)
        gm_far.append(swap(gm, "mp", 2))
        by_two = by_two + by
    result, keep_two = done
    gu, gg, bu, bg, gh_own = ffn_backward(gm_own, weights, saved_own, sup, sgate, F32)
    gus, ggs, last, gh_over = [gu], [gg], gh_own, []
    for c in chunks:
        gu, gg, bu_c, bg_c, last = ffn_backward([after(gm_far[c], last)], weights, saved_far[c], sup, sgate, BF16)
        gh_over.append(swap(last, "mp", 2))
        gus.append(gu)
        ggs.append(gg)
        bu, bg = bu + bu_c, bg + bg_c
    grad_mlp = weight_grads(
        [h_own] + h_far,
        gm_own + gm_far,
        gus,
        ggs,
        [saved_own[1]] + [saved[1] for saved in saved_far],
        weights.shape,
    )
    grad_mlp, *gh_over = lax.optimization_barrier((grad_mlp, *gh_over))
    gh_over = jnp.concatenate(gh_over)
    grad_mlp = lax.psum_scatter(
        grad_mlp.reshape(-1, part), ("dp", "mp"), scatter_dimension=0, tiled=True, axis_index_groups=chip_groups()
    ).astype(F32)
    grad_up, grad_gate, grad_down = jnp.split(grad_mlp, 3, axis=0)

    grad_attn, grad_x, att0, att1, att2, att3, by_one = own_call(
        attn_back_body,
        "attn_back_out",
        [(gh_own, D, 0, 0), (gh_over, D, 0, 0), (keep_two, D, 0, 0), (branch, D, 0, 0), (tokens, D, 0, 0)],
        [one],
        out_parts,
        [(local, D, BF16), (local, D, F32)] + [(local, width, BF16)] * 4,
        1,
        2 * local * D * D,
    )
    back_x = swap(jnp.concatenate([att2, att3]), "mp", 2)
    back_core = swap(jnp.concatenate([att1, back_x[local:]]), "mp", 1)
    g_att = jnp.concatenate([back_x[:local], back_core[local:], att0, back_core[:local]])
    outs = [dot(grad_attn, a[s : s + local], 0, 0) for a, _, s, _ in heads_in]
    core_out = swap(jnp.concatenate([outs[1], outs[3]], axis=1).astype(BF16), "mp", 1)
    core_out, g_att = lax.optimization_barrier((core_out, g_att))
    over_out = swap((outs[2] + core_out[:, width:].astype(F32)).astype(BF16), "mp", 2)
    grad_out = outs[0] + core_out[:, :width].astype(F32) + over_out.astype(F32)
    grads, g_sqk = attend_back(
        meta, queries, qrot, attended, inverse_mass, g_att, keys, vals, krot, kpos_cols, cosine, sine, sqk, docs
    )
    first, second = grads[: 2 * local], grads[2 * local :]
    qkv_sum = dot(x_first, first, 0, 0) + dot(x_second, second, 0, 0)
    half_sum, sent = scatter_y(qkv_sum, grad_out)
    qkv = after(attn, sent)[:, : 3 * width]
    second_tokens = dot(second, qkv, 1, 1).astype(BF16)
    to_core = swap(second_tokens, "mp", 1)
    partial = dot(first, after(qkv, second_tokens), 1, 1)
    for_x = (partial[local:] + to_core[local:].astype(F32)).astype(BF16)
    to_x = swap(for_x, "mp", 2)

    def placed(array, index):
        slots = lax.broadcasted_iota(jnp.int32, (4, 1), 0)
        return jnp.where(slots == index, array[None], 0.0)

    def quarters(by):
        return placed(by[0, 0], m & 2) + placed(by[1, 0], (m & 2) + 1)

    rows = [quarters(bu), quarters(bg), placed(g_sqk[0], m), by_one[0], by_two[0]]
    rows = [row.reshape(devices, -1) for row in rows]
    small = jnp.sum(to_all(after(jnp.concatenate(rows, axis=1), for_x)), axis=0)
    cuts, start = [], 0
    for row in rows:
        cuts.append(small[start : start + row.shape[1]])
        start += row.shape[1]
    g_sup, g_sgate, g_sqk, g_alpha_one, g_alpha_two = cuts

    def squared(*arrays):
        return sum(jnp.sum(array * array) for array in arrays)

    squares = squared(grad_mlp)
    grad_attn = scatter_z(after(half_sum, for_x, squares))
    squares = squares + squared(grad_attn, small)
    g_qkv = [grad_attn[:, i * width : (i + 1) * width] for i in range(3)]
    grad_down, grad_out = turned(grad_down), turned(grad_attn[:, 3 * width :])
    to_x = after(to_x, squares)
    grad_tokens = grad_x + partial[:local] + to_core[:local].astype(F32) + to_x.astype(F32)
    pieces = tuple(g_qkv) + (grad_out, grad_up, grad_gate, grad_down)
    pieces = pieces + (g_sqk, g_sup, g_sgate, g_alpha_one, g_alpha_two)
    squares = jnp.sum(to_all(jnp.broadcast_to(squares, (devices, 128))), axis=0)
    grad_norm = jnp.sqrt(squares[0])
    mean_alphas = jnp.stack([jnp.mean(alpha_one), jnp.mean(alpha_two)])
    return (result, grad_tokens) + pieces + (grad_norm, mean_alphas)


def solution(mesh):
    both_axes = P(("dp", "mp"))
    rows = P(("dp", "mp"), None)
    in_specs = (
        (rows, rows, P("dp", None), P("dp", None))
        + (P("dp", "mp"),) * 3
        + (P("mp", "dp"),)
        + (P("dp", "mp"),) * 2
        + (P("mp", "dp"),)
        + (both_axes,) * 5
    )
    out_specs = (
        (rows, rows)
        + (P("dp", "mp"),) * 3
        + (P("mp", "dp"),)
        + (P("dp", "mp"),) * 2
        + (P("mp", "dp"),)
        + (both_axes,) * 5
        + (P(), P())
    )
    return jax.shard_map(shards, mesh=mesh, in_specs=in_specs, out_specs=out_specs, check_vma=False)
```

```python
import functools

import jax
import jax.numpy as jnp
from jax import lax
from jax.experimental import pallas as pl
from jax.experimental.layout import Layout, with_layout_constraint
from jax.experimental.pallas import tpu as pltpu
from jax.sharding import PartitionSpec as P

D = 1024
HEADS = 16
HEAD = D // HEADS
EPS = 1e-06
NEG = -1e30
BLOCK = 256
F32 = jnp.float32
BF16 = jnp.bfloat16


def mean_rows(tensor):
    return jnp.mean(tensor, axis=-1, keepdims=True)


def normed(tensor):
    factor = lax.rsqrt(mean_rows(tensor * tensor) + EPS)
    return tensor * factor, factor


def normed_back(incoming, unit, factor):
    return factor * (incoming - unit * mean_rows(incoming * unit))


def dot(left, right, left_dim=1, right_dim=0):
    return lax.dot_general(
        left, right, (((left_dim,), (right_dim,)), ((), ())), preferred_element_type=F32
    )


RING = (0, 2, 4, 6, 7, 5, 3, 1)


def swap(array, axis, bit):
    size = lax.axis_size(axis)
    return lax.ppermute(array, axis, [(i, i ^ bit) for i in range(size)])


def to_z(array, step):
    return lax.ppermute(
        array, "dp", [(z * 2 + y, ((z + step) % 4) * 2 + y) for z in range(4) for y in range(2)]
    )


def around(array, step):
    return lax.ppermute(array, "dp", [(RING[p], RING[(p + step) % 8]) for p in range(8)])


def after(array, *others):
    if not others:
        return array
    return lax.optimization_barrier((array,) + others)[0]


def gather(shard, before):
    if lax.axis_size("dp") != 8:
        full = lax.all_gather(shard, "dp", axis=0, tiled=True)
        return full, full
    d = lax.axis_index("dp")
    rows, width = shard.shape
    place = jnp.where((d & 1) == 0, d >> 1, 7 - (d >> 1))

    def put(full, part, step):
        q = (place + step) & 7
        index = jnp.where(q < 4, 2 * q, 2 * (7 - q) + 1)
        return lax.dynamic_update_slice(full, part, (index * rows, jnp.int32(0)))

    full = put(jnp.zeros((8 * rows, width), shard.dtype), shard, 0)
    ahead = behind = shard
    for step in (1, 2, 3, 4):
        if step > 1:
            ahead, behind = lax.optimization_barrier((ahead, behind) + tuple(before[step - 1]))[:2]
        ahead = around(ahead, 1)
        full = put(full, ahead, -step)
        if step < 4:
            behind = around(behind, -1)
            full = put(full, behind, step)
        if step == 3:
            third = behind
    return full, third


def chip_groups():
    return [
        [d * 4 + 2 * x + core for d in range(lax.axis_size("dp")) for core in range(2)]
        for x in range(2)
    ]


def scatter_y(*grads):
    if lax.axis_size("dp") != 8:
        whole = jnp.concatenate(grads, axis=1)
        return whole, whole
    y = lax.axis_index("dp") & 1
    grads = [g.reshape(4, 2, g.shape[0] // 8, g.shape[1]) for g in grads]

    def rows(index, kind):
        parts = [lax.dynamic_index_in_dim(g, index, axis=1, keepdims=False).astype(kind) for g in grads]
        return jnp.concatenate(parts, axis=2)

    sent = rows(1 - y, BF16)
    return rows(y, F32) + swap(sent, "dp", 1).astype(F32), sent


def scatter_z(half, *before_sum):
    if lax.axis_size("dp") != 8:
        return lax.psum_scatter(half.astype(F32), "dp", scatter_dimension=0, tiled=True)
    z = lax.axis_index("dp") >> 1
    total = lax.dynamic_index_in_dim(half, z, axis=0, keepdims=False)
    for step in (1, 2, 3):
        part = lax.dynamic_index_in_dim(half, (z + step) & 3, axis=0, keepdims=False)
        total = total + after(to_z(part.astype(BF16), step), *before_sum).astype(F32)
    return total


def turned(array):
    return with_layout_constraint(array, Layout(major_to_minor=(0, 1))).T


def to_all(rows):
    return lax.all_to_all(rows, ("dp", "mp"), 0, 0, tiled=True)


def rotate_half(tensor):
    width = tensor.shape[-1]
    lane = lax.broadcasted_iota(jnp.int32, tensor.shape, 1)
    ahead = pltpu.roll(tensor, width - HEAD // 2, 1)
    behind = pltpu.roll(tensor, HEAD // 2, 1)
    return jnp.where((lane & (HEAD - 1)) < HEAD // 2, -ahead, behind)


def head_mean(tensor):
    width = tensor.shape[-1]
    row = lax.broadcasted_iota(jnp.int32, (width, width), 0) // HEAD
    col = lax.broadcasted_iota(jnp.int32, (width, width), 1) // HEAD
    ones = jnp.where(row == col, 1.0 / HEAD, 0.0).astype(BF16)
    high = tensor.astype(BF16)
    rest = (tensor - high.astype(F32)).astype(BF16)
    return dot(high, ones) + dot(rest, ones)


def wide(table):
    return jnp.concatenate([table, table], axis=1)


def project_body(m_ref, x_ref, w_ref, cos_ref, sin_ref, sqk_ref, *refs):
    q_ref, k_ref, v_ref, qr_ref, kr_ref = refs[-5:]
    rows = x_ref[...]
    cosine, sine = wide(cos_ref[...]), wide(sin_ref[...])
    scale = sqk_ref[0:1, :]
    width = q_ref.shape[1]
    raws = [dot(rows, w_ref[:, i * width : (i + 1) * width]) for i in range(3)]
    v_ref[...] = raws[2].astype(BF16)
    for raw, out_ref, rot_ref in ((raws[0], q_ref, qr_ref), (raws[1], k_ref, kr_ref)):
        turned = raw * cosine + rotate_half(raw) * sine
        rot_ref[...] = turned
        unit = turned * lax.rsqrt(head_mean(turned * turned) + EPS)
        out_ref[...] = (unit * scale).astype(BF16)


def project(place, x_rows, weight, cosine, sine, sqk, previous, first):
    rows, width = x_rows.shape[0], weight.shape[1] // 4
    total = cosine.shape[0]
    per = total // 4 // BLOCK

    def row_block(i, m):
        return ((m[0] ^ (first + 2 * (i // per))) * per + i % per, 0)

    any_spec = pl.BlockSpec(memory_space=pl.ANY)
    table = pl.BlockSpec((BLOCK, cosine.shape[1]), row_block)
    out = pl.BlockSpec((BLOCK, width), row_block)
    shapes = [jax.ShapeDtypeStruct((total, width), t) for t in (BF16, BF16, BF16, F32, F32)]
    extra = list(previous) if previous is not None else []
    return pl.pallas_call(
        project_body,
        out_shape=shapes,
        grid_spec=pltpu.PrefetchScalarGridSpec(
            num_scalar_prefetch=1,
            grid=(rows // BLOCK,),
            in_specs=[
                pl.BlockSpec((BLOCK, x_rows.shape[1]), lambda i, m: (i, 0)),
                pl.BlockSpec((x_rows.shape[1], 3 * width), lambda i, m: (0, 0)),
                table,
                table,
                pl.BlockSpec((1, width), lambda i, m: (0, 0)),
            ]
            + [any_spec] * len(extra),
            out_specs=[out] * 5,
        ),
        input_output_aliases={6 + i: i for i in range(len(extra))},
        cost_estimate=pl.CostEstimate(
            flops=6 * rows * D * width, bytes_accessed=8 * rows * D, transcendentals=rows
        ),
        name="project",
    )(place, x_rows, weight, cosine, sine, sqk, *extra)


def head_lanes(array, head):
    lane = lax.broadcasted_iota(jnp.int32, array.shape, 1)
    return jnp.where(lane // HEAD == head, array, jnp.zeros_like(array))


def stack_heads(array):
    heads = array.shape[1] // HEAD
    return jnp.concatenate([head_lanes(array, h) for h in range(heads)], axis=0)


def doc_start(meta_ref, docs, slots):
    start = jnp.zeros_like(slots)
    end = 0
    for i in range(docs):
        length = meta_ref[1 + i]
        end = end + length
        start = start + jnp.where(slots >= end, length, 0)
    return start


def slot_place(rel):
    return (rel >> 1) + 2 * (rel & 1)


def block_at(block):
    return pl.ds(pl.multiple_of(block * BLOCK, BLOCK), BLOCK)


def by_pairs(low, high, visit):
    def pair(i, carry):
        visit(low + 2 * i, low + 2 * i + 1)
        return carry

    lax.fori_loop(0, (high - low) >> 1, pair, 0)

    @pl.when(((high - low) & 1) == 1)
    def _():
        visit(high - 1)


def split_heads(source_ref, split_ref):
    def one(block, carry):
        split_ref[block] = stack_heads(source_ref[block_at(block), :])
        return carry

    lax.fori_loop(0, source_ref.shape[0] // BLOCK, one, 0)


def attend_body(docs, first, meta_ref, q_ref, k_ref, v_ref, kpos_ref, *refs):
    o_ref, inv_ref, acc_ref, sum_ref, vs_ref = refs[-5:]
    per = k_ref.shape[0] // 4 // BLOCK
    index = pl.program_id(0)
    step = ((first + index // per) ^ meta_ref[0]) * per + index % per
    heads = q_ref.shape[1] // HEAD
    base = step * BLOCK
    low = doc_start(meta_ref, docs, base) // BLOCK

    @pl.when(index == 0)
    def _():
        split_heads(v_ref, vs_ref)

    scaled = q_ref[...] * jnp.bfloat16(HEAD**-0.5)
    queries = [head_lanes(scaled, h) for h in range(heads)]
    rows = lax.broadcasted_iota(jnp.int32, (BLOCK, BLOCK), 0) + base
    starts = doc_start(meta_ref, docs, rows)
    acc_ref[...] = jnp.zeros_like(acc_ref)
    sum_ref[...] = jnp.zeros_like(sum_ref)

    def visit(blocks, allowed):
        expos = []
        sums = [0.0] * heads
        for block, mask in zip(blocks, allowed):
            keys = k_ref[block_at(block), :]
            bias = jnp.where(mask, 0.0, NEG)
            for h in range(heads):
                expo = jnp.exp(dot(queries[h], keys, 1, 1) + bias)
                sums[h] = sums[h] + expo[:, :128] + expo[:, 128:]
                expos.append(expo.astype(BF16))
        for h in range(heads):
            sum_ref[h * BLOCK : (h + 1) * BLOCK, :] += sums[h]
        vals = jnp.concatenate([vs_ref[block] for block in blocks], axis=0)
        acc_ref[...] += dot(jnp.concatenate(expos, axis=1), vals)

    def off_diagonal(*blocks):
        visit(blocks, [kpos_ref[0:1, block_at(block)] >= starts for block in blocks])

    by_pairs(low, step, off_diagonal)
    cols = lax.broadcasted_iota(jnp.int32, (BLOCK, BLOCK), 1) + base
    visit([step], [((kpos_ref[0:1, block_at(step)] >= starts) & (cols <= rows)) | (cols == rows)])
    lane = lax.broadcasted_iota(jnp.int32, (BLOCK, q_ref.shape[1]), 1) // HEAD
    inverse = jnp.zeros((BLOCK, q_ref.shape[1]), F32)
    for h in range(heads):
        mass = jnp.sum(sum_ref[h * BLOCK : (h + 1) * BLOCK, :], axis=1, keepdims=True)
        inverse = jnp.where(lane == h, 1.0 / mass, inverse)
    inv_ref[...] = inverse
    o_ref[...] = (acc_ref[...] * inverse).astype(BF16)


def attend(meta, queries, keys, vals, kpos, docs, first, previous):
    total, width = queries.shape
    per = total // 4 // BLOCK
    heads = width // HEAD
    whole = pl.BlockSpec((total, width), lambda i, m: (0, 0))

    def natural(i, m):
        return (((first + i // per) ^ m[0]) * per + i % per, 0)

    block = pl.BlockSpec((BLOCK, width), natural)
    out = pl.BlockSpec((BLOCK, width), lambda i, m: ((first ^ 2) * per + i, 0))
    extra = list(previous)
    return pl.pallas_call(
        functools.partial(attend_body, docs, first),
        out_shape=[
            jax.ShapeDtypeStruct((total, width), BF16),
            jax.ShapeDtypeStruct((total, width), F32),
        ],
        grid_spec=pltpu.PrefetchScalarGridSpec(
            num_scalar_prefetch=1,
            grid=(2 * per,),
            in_specs=[block, whole, whole, pl.BlockSpec((1, total), lambda i, m: (0, 0))]
            + [pl.BlockSpec(memory_space=pl.ANY)] * len(extra),
            out_specs=[out, block],
            scratch_shapes=[
                pltpu.VMEM((BLOCK, width), F32),
                pltpu.VMEM((heads * BLOCK, 128), F32),
                pltpu.VMEM((total // BLOCK, heads * BLOCK, width), BF16),
            ],
        ),
        input_output_aliases={5 + i: i for i in range(len(extra))},
        cost_estimate=pl.CostEstimate(
            flops=8_000_000_000, bytes_accessed=8 * total * width, transcendentals=3_000_000
        ),
        name="attend",
    )(meta, queries, keys, vals, kpos, *extra)


def finish(grad, turned, cosine, sine, scale):
    factor = lax.rsqrt(head_mean(turned * turned) + EPS)
    unit = turned * factor
    by_scale = jnp.sum(grad * unit, axis=0, keepdims=True)
    scaled = grad * scale
    back = factor * (scaled - unit * head_mean(scaled * unit))
    raw = back * cosine - rotate_half(back) * sine
    return raw.astype(BF16), by_scale


def back_body(
    docs,
    meta_ref,
    q_ref,
    qr_ref,
    o_ref,
    inv_ref,
    do_ref,
    k_ref,
    v_ref,
    kr_ref,
    kpos_ref,
    cos_ref,
    sin_ref,
    sqk_ref,
    g_ref,
    gs_ref,
    dq_ref,
    dk_ref,
    dv_ref,
    ks_ref,
):
    step = pl.program_id(0)
    width = q_ref.shape[1]
    heads = width // HEAD
    per = k_ref.shape[0] // 4 // BLOCK
    base = step * BLOCK
    low = doc_start(meta_ref, docs, base) // BLOCK

    @pl.when(step == 0)
    def _():
        dk_ref[...] = jnp.zeros_like(dk_ref)
        dv_ref[...] = jnp.zeros_like(dv_ref)
        gs_ref[...] = jnp.zeros_like(gs_ref)
        split_heads(k_ref, ks_ref)

    dq_ref[...] = jnp.zeros_like(dq_ref)
    scaled = q_ref[...] * jnp.bfloat16(HEAD**-0.5)
    queries = [head_lanes(scaled, h) for h in range(heads)]
    all_queries = jnp.concatenate(queries, axis=0)
    upward = do_ref[...].astype(F32) * inv_ref[...]
    ups = [head_lanes(upward.astype(BF16), h) for h in range(heads)]
    all_ups = jnp.concatenate(ups, axis=0)
    picks = lax.broadcasted_iota(jnp.int32, (8, width), 0)
    lanes = lax.broadcasted_iota(jnp.int32, (8, width), 1) // HEAD
    delta = lax.dot_general(
        jnp.where(picks == lanes, 1.0, 0.0).astype(F32),
        upward * o_ref[...].astype(F32),
        (((1,), (1,)), ((), ())),
        precision=lax.Precision.HIGHEST,
        preferred_element_type=F32,
    )
    cols = lax.broadcasted_iota(jnp.int32, (BLOCK, BLOCK), 1) + base
    starts = doc_start(meta_ref, docs, cols)

    def visit(block, count, allowed):
        rows_at = pl.ds(pl.multiple_of(block * BLOCK, BLOCK), count * BLOCK)
        keys, vals = k_ref[rows_at, :], v_ref[rows_at, :]
        bias = jnp.where(allowed, 0.0, NEG)
        expos, slopes = [], []
        for h in range(heads):
            expo = jnp.exp(dot(keys, queries[h], 1, 1) + bias)
            expos.append(expo.astype(BF16))
            slope = expo * (dot(vals, ups[h], 1, 1) - delta[h : h + 1, :])
            slopes.append(slope.astype(BF16))
        dv_ref[rows_at, :] += dot(jnp.concatenate(expos, axis=1), all_ups)
        dk_ref[rows_at, :] += dot(jnp.concatenate(slopes, axis=1), all_queries)
        pieces = [slope[i * BLOCK : (i + 1) * BLOCK] for i in range(count) for slope in slopes]
        split = jnp.concatenate([ks_ref[block + i] for i in range(count)], axis=0)
        dq_ref[...] += dot(jnp.concatenate(pieces, axis=0), split, 0, 0)

    def off_diagonal(*blocks):
        keys_at = pl.ds(pl.multiple_of(blocks[0] * BLOCK, BLOCK), len(blocks) * BLOCK)
        again = jnp.concatenate([starts] * len(blocks), axis=0)
        visit(blocks[0], len(blocks), wide(kpos_ref[keys_at, :]) >= again)

    by_pairs(low, step, off_diagonal)
    rows = lax.broadcasted_iota(jnp.int32, (BLOCK, BLOCK), 0) + base
    key_slots = wide(kpos_ref[block_at(step), :])
    visit(step, 1, ((key_slots >= starts) & (rows <= cols)) | (rows == cols))

    scale = sqk_ref[0:1, :]
    here = pl.ds(pl.multiple_of(base, BLOCK), BLOCK)
    raw, by_scale = finish(
        dq_ref[...] * (HEAD**-0.5),
        qr_ref[...],
        wide(cos_ref[here, :]),
        wide(sin_ref[here, :]),
        scale,
    )
    slot = slot_place(meta_ref[0] ^ (step // per)) * per + step % per
    g_ref[pl.ds(pl.multiple_of(slot * BLOCK, BLOCK), BLOCK), :width] = raw
    gs_ref[0:1, :] += by_scale

    @pl.when(step == pl.num_programs(0) - 1)
    def _():
        def one(block, carry):
            at = pl.ds(pl.multiple_of(block * BLOCK, BLOCK), BLOCK)
            slot = slot_place(meta_ref[0] ^ (block // per)) * per + block % per
            to = pl.ds(pl.multiple_of(slot * BLOCK, BLOCK), BLOCK)
            raw, by_scale = finish(
                dk_ref[at, :], kr_ref[at, :], wide(cos_ref[at, :]), wide(sin_ref[at, :]), scale
            )
            g_ref[to, width : 2 * width] = raw
            gs_ref[0:1, :] += by_scale
            g_ref[to, 2 * width :] = dv_ref[at, :].astype(BF16)
            return carry

        lax.fori_loop(0, pl.num_programs(0), one, 0)


def attend_back(meta, queries, qrot, out, inverse, grad, keys, vals, krot, kpos, cosine, sine, sqk, docs):
    total, width = queries.shape
    per = total // 4 // BLOCK

    def rel(i, m):
        return ((m[0] ^ (i // per) ^ 2) * per + i % per, 0)

    whole = pl.BlockSpec((total, width), lambda i, m: (0, 0))
    half = pl.BlockSpec((total, 128), lambda i, m: (0, 0))
    block = pl.BlockSpec((BLOCK, width), lambda i, m: (i, 0))
    moved = pl.BlockSpec((BLOCK, width), rel)
    return pl.pallas_call(
        functools.partial(back_body, docs),
        out_shape=[
            jax.ShapeDtypeStruct((total, 3 * width), BF16),
            jax.ShapeDtypeStruct((8, width), F32),
        ],
        grid_spec=pltpu.PrefetchScalarGridSpec(
            num_scalar_prefetch=1,
            grid=(total // BLOCK,),
            in_specs=[block, block, moved, block, moved, whole, whole, whole, half, half, half]
            + [pl.BlockSpec((1, width), lambda i, m: (0, 0))],
            out_specs=[
                pl.BlockSpec((total, 3 * width), lambda i, m: (0, 0)),
                pl.BlockSpec((8, width), lambda i, m: (0, 0)),
            ],
            scratch_shapes=[
                pltpu.VMEM((BLOCK, width), F32),
                pltpu.VMEM((total, width), F32),
                pltpu.VMEM((total, width), F32),
                pltpu.VMEM((total // BLOCK, width // HEAD * BLOCK, width), BF16),
            ],
        ),
        cost_estimate=pl.CostEstimate(
            flops=40_000_000_000, bytes_accessed=12 * total * width, transcendentals=6_000_000
        ),
        name="attend_back",
    )(meta, queries, qrot, out, inverse, grad, keys, vals, krot, kpos, cosine, sine, sqk)


TILE = 256


def weight_tile(weight_ref, part, index):
    return weight_ref[:, part, index].reshape(D, TILE)


def weight_spec(weights):
    return pl.BlockSpec(weights.shape[:4] + (TILE,), lambda t: (0, 0, 0, 0, t))


def forward_body(
    h_ref, w_ref, sup_ref, sgate_ref, gate_ref, act_ref, by_up_ref, by_gate_ref, out_ref, acc_ref
):
    t = pl.program_id(0)
    rows = h_ref[...]
    acts = []
    for part in range(2):
        sup, sgate = sup_ref[part, 0:1, :], sgate_ref[part, 0:1, :]
        scaled = sup * dot(rows, weight_tile(w_ref, part, 0))
        gate_proj = dot(rows, weight_tile(w_ref, part, 1))
        outer = sgate * gate_proj
        sigma = jax.nn.sigmoid(outer)
        silu = outer * sigma
        acts.append((scaled * silu).astype(BF16))
        gate_ref[part] = gate_proj.astype(BF16)
        act_ref[part] = acts[part]
        by_up_ref[part] = (sup * silu).astype(BF16)
        by_gate_ref[part] = ((sgate * scaled) * (sigma + silu * (1.0 - sigma))).astype(BF16)
    total = dot(
        jnp.concatenate(acts, axis=1),
        jnp.concatenate([weight_tile(w_ref, part, 2) for part in range(2)], axis=1),
        1,
        1,
    )
    add_up(t, total, acc_ref, out_ref)


def add_up(t, total, acc_ref, out_ref):
    @pl.when(t == 0)
    def _():
        acc_ref[...] = total

    @pl.when((t > 0) & (t < pl.num_programs(0) - 1))
    def _():
        acc_ref[...] += total

    @pl.when(t == pl.num_programs(0) - 1)
    def _():
        out_ref[...] = (acc_ref[...] + total).astype(out_ref.dtype)


def ffn_specs(count):
    whole = pl.BlockSpec((count, D), lambda t: (0, 0))
    tile = pl.BlockSpec((2, count, TILE), lambda t: (0, 0, t))
    scale = pl.BlockSpec((2, 1, TILE), lambda t: (0, 0, t))
    return whole, tile, scale


def ffn_forward(rows, weights, sup, sgate, kind):
    count, hidden = rows.shape[0], sup.shape[2]
    whole, tile, scale = ffn_specs(count)
    return pl.pallas_call(
        forward_body,
        out_shape=[jax.ShapeDtypeStruct((2, count, hidden), BF16)] * 4
        + [jax.ShapeDtypeStruct((count, D), kind)],
        grid=(hidden // TILE,),
        in_specs=[whole, weight_spec(weights), scale, scale],
        out_specs=[tile] * 4 + [whole],
        scratch_shapes=[pltpu.VMEM((count, D), F32)],
        cost_estimate=pl.CostEstimate(
            flops=12 * count * D * hidden,
            bytes_accessed=12 * D * hidden + 12 * count * hidden,
            transcendentals=2 * count * hidden,
        ),
        name="ffn_forward",
    )(rows, weights, sup, sgate)


def backward_body(pieces, *refs):
    rows = jnp.concatenate([ref[...] for ref in refs[:pieces]], axis=0)
    w_ref, gate_ref, act_ref, by_up_ref, by_gate_ref, sup_ref, sgate_ref = refs[pieces : pieces + 7]
    gu_ref, gg_ref, bu_ref, bg_ref, out_ref, acc_ref = refs[pieces + 7 :]
    t = pl.program_id(0)
    lefts, rights = [], []
    for part in range(2):
        g_act = dot(rows, weight_tile(w_ref, part, 2))
        g_up = (g_act * by_up_ref[part].astype(F32)).astype(BF16)
        g_gate = g_act * by_gate_ref[part].astype(F32)
        up_sum = jnp.sum(g_act * act_ref[part].astype(F32), axis=0, keepdims=True)
        gate_sum = jnp.sum(g_gate * gate_ref[part].astype(F32), axis=0, keepdims=True)
        g_gate = g_gate.astype(BF16)
        bu_ref[part, 0:1, :] = up_sum / sup_ref[part, 0:1, :]
        bg_ref[part, 0:1, :] = gate_sum / sgate_ref[part, 0:1, :]
        gu_ref[part] = g_up
        gg_ref[part] = g_gate
        lefts += [g_up, g_gate]
        rights += [weight_tile(w_ref, part, 0), weight_tile(w_ref, part, 1)]
    total = dot(jnp.concatenate(lefts, axis=1), jnp.concatenate(rights, axis=1), 1, 1)
    add_up(t, total, acc_ref, out_ref)


def ffn_backward(grads, weights, saved, sup, sgate, kind):
    count, hidden = sum(g.shape[0] for g in grads), sup.shape[2]
    whole, tile, scale = ffn_specs(count)
    sums = pl.BlockSpec((2, 8, TILE), lambda t: (0, 0, t))
    return pl.pallas_call(
        functools.partial(backward_body, len(grads)),
        out_shape=[jax.ShapeDtypeStruct((2, count, hidden), BF16)] * 2
        + [jax.ShapeDtypeStruct((2, 8, hidden), F32)] * 2
        + [jax.ShapeDtypeStruct((count, D), kind)],
        grid=(hidden // TILE,),
        in_specs=[pl.BlockSpec(g.shape, lambda t: (0, 0)) for g in grads]
        + [weight_spec(weights)]
        + [tile] * 4
        + [scale, scale],
        out_specs=[tile, tile, sums, sums, whole],
        scratch_shapes=[pltpu.VMEM((count, D), F32)],
        cost_estimate=pl.CostEstimate(
            flops=12 * count * D * hidden,
            bytes_accessed=12 * D * hidden + 24 * count * hidden,
            transcendentals=0,
        ),
        name="ffn_backward",
    )(*grads, weights, *saved, sup, sgate)


def weight_body(counts, *refs):
    h_count, g_count, m_count = counts
    take = iter(refs)
    hs = [next(take) for _ in range(h_count)]
    ms = [next(take) for _ in range(m_count)]
    ups, gates, acts = [[next(take) for _ in range(g_count)] for _ in range(3)]
    out_ref, ht_ref, mt_ref = refs[-3:]

    @pl.when(pl.program_id(0) == 0)
    def _():
        for pieces, to_ref in ((hs, ht_ref), (ms, mt_ref)):
            start = 0
            for ref in pieces:
                to_ref[:, start : start + ref.shape[0]] = ref[...].T
                start += ref.shape[0]

    for index, (left_ref, rights) in enumerate(((ht_ref, ups), (ht_ref, gates), (mt_ref, acts))):
        for part in range(2):
            right = jnp.concatenate([ref[part] for ref in rights], axis=0)
            total = dot(left_ref[...], right).astype(BF16)
            out_ref[:, part, index] = total.reshape(out_ref.shape[0], out_ref.shape[3], TILE)


def weight_grads(hs, ms, ups, gates, acts, shape):
    hidden = ups[0].shape[2]
    count = sum(h.shape[0] for h in hs)

    def whole(array):
        return pl.BlockSpec(array.shape, lambda t: (0, 0))

    def tile(array):
        return pl.BlockSpec((2, array.shape[1], TILE), lambda t: (0, 0, t))

    lefts, rights = list(hs) + list(ms), list(ups) + list(gates) + list(acts)
    return pl.pallas_call(
        functools.partial(weight_body, (len(hs), len(ups), len(ms))),
        out_shape=jax.ShapeDtypeStruct(shape, BF16),
        grid=(hidden // TILE,),
        in_specs=[whole(a) for a in lefts] + [tile(a) for a in rights],
        out_specs=pl.BlockSpec(shape[:4] + (TILE,), lambda t: (0, 0, 0, 0, t)),
        scratch_shapes=[pltpu.VMEM((D, count), BF16)] * 2,
        cost_estimate=pl.CostEstimate(
            flops=12 * count * D * hidden,
            bytes_accessed=12 * D * hidden + 12 * count * hidden,
            transcendentals=0,
        ),
        name="weight_grads",
    )(*lefts, *rights)


def own_call(body, name, rows_in, vectors, wholes, outs, sums, flops):
    count = outs[0][0]
    blocks = count // BLOCK

    def rows_spec(width, skip, column):
        return pl.BlockSpec((BLOCK, width), lambda i: (skip // BLOCK + i, column))

    in_specs = [rows_spec(w, s, c) for _, w, s, c in rows_in]
    in_specs += [pl.BlockSpec((1, v.shape[1]), lambda i: (0, 0)) for v in vectors]
    in_specs += [pl.BlockSpec((D, w), lambda i, c=c: (0, c)) for _, w, c in wholes]
    shapes = [jax.ShapeDtypeStruct((count, w), t) for count, w, t in outs]
    shapes += [jax.ShapeDtypeStruct((8, D), F32)] * sums
    out_specs = [pl.BlockSpec((BLOCK, w), lambda i: (i, 0)) for _, w, _ in outs]
    out_specs += [pl.BlockSpec((8, D), lambda i: (0, 0))] * sums
    return pl.pallas_call(
        body,
        out_shape=shapes,
        grid=(blocks,),
        in_specs=in_specs,
        out_specs=out_specs,
        cost_estimate=pl.CostEstimate(
            flops=flops, bytes_accessed=20 * count * D, transcendentals=count
        ),
        name=name,
    )(*[a for a, *_ in rows_in], *vectors, *[a for a, *_ in wholes])


def first_update(branch, x_rows, alpha):
    h_attn, attn_factor = normed(branch)
    hidden, one_factor = normed(x_rows + alpha * (h_attn - x_rows))
    return h_attn, attn_factor, hidden, one_factor


def attn_body(a0, a1, a2, a3, x_ref, alpha_ref, w0, w1, w2, w3, branch_ref, low_ref):
    branch = dot(a0[...], w0[...], 1, 1) + dot(a1[...], w1[...], 1, 1)
    branch = branch + dot(a2[...], w2[...], 1, 1) + dot(a3[...], w3[...], 1, 1)
    branch_ref[...] = branch
    hidden = first_update(branch, x_ref[...].astype(F32), alpha_ref[0:1, :])[2]
    low_ref[...] = hidden.astype(BF16)


def turn_body(own_ref, far_ref, branch_ref, x_ref, cot_ref, one_ref, two_ref, *refs):
    out_ref, keep_ref, gm_ref, sum_ref = refs[-4:]
    hidden = first_update(branch_ref[...], x_ref[...].astype(F32), one_ref[0:1, :])[2]
    alpha = two_ref[0:1, :]
    h_mlp, mlp_factor = normed(own_ref[...] + far_ref[...].astype(F32))
    step = h_mlp - hidden
    result, two_factor = normed(hidden + alpha * step)
    out_ref[...] = result.astype(BF16)
    grad_two = normed_back(cot_ref[...].astype(F32), result, two_factor)
    keep_ref[...] = grad_two * (1.0 - alpha)
    gm_ref[...] = normed_back(grad_two * alpha, h_mlp, mlp_factor).astype(BF16)

    sum_ref[0:1, :] = jnp.sum(grad_two * step, axis=0, keepdims=True)


def turn(chunk, own, far, branch, x_rows, cotangent, one, two, previous):
    count = branch.shape[0]
    rows = pl.BlockSpec((BLOCK, D), lambda i: (chunk, 0))
    first = pl.BlockSpec((BLOCK, D), lambda i: (0, 0))
    vector = pl.BlockSpec((1, D), lambda i: (0, 0))
    total = pl.BlockSpec((8, D), lambda i: (0, 0))
    extra = list(previous)
    return pl.pallas_call(
        turn_body,
        out_shape=[
            jax.ShapeDtypeStruct((count, D), BF16),
            jax.ShapeDtypeStruct((count, D), F32),
            jax.ShapeDtypeStruct((BLOCK, D), BF16),
            jax.ShapeDtypeStruct((8, D), F32),
        ],
        grid=(1,),
        in_specs=[rows, first, rows, rows, rows, vector, vector]
        + [pl.BlockSpec(memory_space=pl.ANY)] * len(extra),
        out_specs=[rows, rows, first, total],
        input_output_aliases={7 + i: i for i in range(len(extra))},
        cost_estimate=pl.CostEstimate(
            flops=60 * BLOCK * D, bytes_accessed=20 * BLOCK * D, transcendentals=BLOCK
        ),
        name="turn",
    )(own, far, branch, x_rows, cotangent, one, two, *extra)


def attn_back_body(
    own_ref, far_ref, keep_ref, branch_ref, x_ref, one_ref, w0, w1, w2, w3, ga_ref, gt_ref, o0, o1, o2, o3, sum_ref
):
    x_rows, alpha = x_ref[...].astype(F32), one_ref[0:1, :]
    h_attn, attn_factor, hidden, one_factor = first_update(branch_ref[...], x_rows, alpha)
    incoming = keep_ref[...] + own_ref[...] + far_ref[...].astype(F32)
    grad_one = normed_back(incoming, hidden, one_factor)
    gt_ref[...] = grad_one * (1.0 - alpha)
    grad_attn = normed_back(grad_one * alpha, h_attn, attn_factor).astype(BF16)
    ga_ref[...] = grad_attn
    for weight_ref, out_ref in ((w0, o0), (w1, o1), (w2, o2), (w3, o3)):
        out_ref[...] = dot(grad_attn, weight_ref[...]).astype(BF16)

    @pl.when(pl.program_id(0) == 0)
    def _():
        sum_ref[...] = jnp.zeros_like(sum_ref)

    sum_ref[0:1, :] += jnp.sum(grad_one * (h_attn - x_rows), axis=0, keepdims=True)


def shards(
    tokens,
    cotangent,
    lengths,
    key_mask,
    w_query,
    w_key,
    w_value,
    w_out,
    w_up,
    w_gate,
    w_down,
    s_qk,
    s_up,
    s_gate,
    alpha_attn,
    alpha_mlp,
):
    m = lax.axis_index("mp").astype(jnp.int32)
    devices = lax.axis_size("dp") * lax.axis_size("mp")
    local = tokens.shape[0]
    row_len = key_mask.shape[1]
    docs = lengths.shape[1]
    part = w_up.shape[1]
    width = w_query.shape[1]

    place = m.reshape(1)
    meta = jnp.concatenate([place, lengths[0]])
    slot_ids = jnp.arange(row_len, dtype=jnp.int32)
    steps_even = jnp.arange(0, HEAD, 2).astype(F32)
    frequencies = jnp.power(jnp.float32(10000.0), -steps_even / HEAD)
    frequencies = jnp.tile(frequencies, 4)[None, :]

    def turn_by(steps):
        angles = steps.astype(F32)[:, None] * frequencies
        return jnp.cos(angles), jnp.sin(angles)

    coarse_cos, coarse_sin = (t[:, None] for t in turn_by(jnp.arange(0, row_len, 64)))
    fine_cos, fine_sin = (t[None] for t in turn_by(jnp.arange(64)))
    slot_cos = (coarse_cos * fine_cos - coarse_sin * fine_sin).reshape(row_len, -1)
    slot_sin = (coarse_sin * fine_cos + coarse_cos * fine_sin).reshape(row_len, -1)
    first_slots = jnp.cumsum(lengths[0]) - lengths[0]
    doc_cos, doc_sin = turn_by(first_slots)
    start_cos, start_sin = doc_cos[0:1], doc_sin[0:1]
    for i in range(1, docs):
        later = (slot_ids >= first_slots[i])[:, None]
        start_cos = jnp.where(later, doc_cos[i : i + 1], start_cos)
        start_sin = jnp.where(later, doc_sin[i : i + 1], start_sin)
    cosine = slot_cos * start_cos + slot_sin * start_sin
    sine = slot_sin * start_cos - slot_cos * start_sin
    x_halves = [swap(tokens[i * local // 2 : (i + 1) * local // 2], "mp", 2) for i in range(2)]
    x_first = jnp.concatenate([tokens] + x_halves, axis=0)
    vector = jnp.concatenate([s_up, s_gate, s_qk, alpha_attn, alpha_mlp])[None]
    every = to_all(jnp.broadcast_to(vector, (devices, vector.shape[1])))
    attn, third = gather(
        jnp.concatenate([w_query, w_key, w_value, w_out.T], axis=1),
        [(), (), (x_halves[0],), (x_halves[1], every)],
    )
    x_second = swap(x_first, "mp", 1)
    shard = jnp.concatenate([w_up, w_gate, w_down.T], axis=0)
    shard = with_layout_constraint(after(shard, third), Layout(major_to_minor=(0, 1)))
    weights = lax.all_gather(
        shard, ("dp", "mp"), axis=0, tiled=True, axis_index_groups=chip_groups()
    ).reshape(-1, 2, 3, shard.shape[0] // 3, part)
    cuts, start = [], 0
    for piece in (s_up, s_gate, s_qk, alpha_attn, alpha_mlp):
        cuts.append(every[:, start : start + piece.shape[0]].reshape(-1))
        start += piece.shape[0]
    sup_all, sgate_all, sqk_all, alpha_one, alpha_two = cuts

    def quarter(array, index):
        size = array.shape[0] // 4
        return lax.dynamic_slice_in_dim(array, index * size, size)

    def row(array):
        return array[None]

    sqk = row(quarter(sqk_all, m))
    low = m & 2
    sup = jnp.stack([row(quarter(sup_all, low)), row(quarter(sup_all, low + 1))])
    sgate = jnp.stack([row(quarter(sgate_all, low)), row(quarter(sgate_all, low + 1))])
    one, two = row(alpha_one), row(alpha_two)
    out_mine = attn[:, 3 * width :]
    out_core = swap(out_mine, "mp", 1)
    out_over = swap(out_mine, "mp", 2)
    out_cross = swap(out_over, "mp", 1)
    out_parts = [(w, width, 0) for w in (out_mine, out_core, out_over, out_cross)]

    kpos = jnp.where(key_mask[0] == 1, slot_ids, -1)
    kpos_rows = kpos[None, :]
    kpos_cols = jnp.broadcast_to(kpos[:, None], (row_len, 128))

    half = project(place, x_first, attn, cosine, sine, sqk, None, 0)
    queries, keys, vals, qrot, krot = project(place, x_second, attn, cosine, sine, sqk, half, 1)
    half = attend(meta, queries, keys, vals, kpos_rows, docs, 2, ())
    far_core = swap(half[0][local : 2 * local], "mp", 1)
    for_x = jnp.concatenate([half[0][:local], far_core])
    by_x = swap(for_x, "mp", 2)
    half = [after(half[0], for_x), half[1]]
    attended, inverse_mass = attend(meta, queries, keys, vals, kpos_rows, docs, 0, half)
    by_core = swap(attended[3 * local :], "mp", 1)
    heads_in = [(attended, width, 2 * local, 0), (by_core, width, 0, 0), (by_x, width, 0, 0), (by_x, width, local, 0)]
    branch, h_own = own_call(
        attn_body,
        "attn_out",
        heads_in + [(tokens, D, 0, 0)],
        [one],
        out_parts,
        [(local, D, F32), (local, D, BF16)],
        0,
        2 * local * D * D,
    )

    chunks = range(local // BLOCK)
    h_far = [swap(h_own[c * BLOCK : (c + 1) * BLOCK], "mp", 2) for c in chunks]
    *saved_own, sum_own = ffn_forward(h_own, weights, sup, sgate, F32)
    saved_far, sum_far, last = [], [], sum_own
    for c in chunks:
        *saved, last = ffn_forward(after(h_far[c], last), weights, sup, sgate, BF16)
        saved_far.append(saved)
        sum_far.append(swap(last, "mp", 2))
    done, gm_own, gm_far, by_two = (), [], [], 0.0
    for c in chunks:
        *done, gm, by = turn(c, after(sum_own, last), sum_far[c], branch, tokens, cotangent, one, two, done)
        gm_own.append(gm)
        gm_far.append(swap(gm, "mp", 2))
        by_two = by_two + by
    result, keep_two = done
    gu, gg, bu, bg, gh_own = ffn_backward(gm_own, weights, saved_own, sup, sgate, F32)
    gus, ggs, last, gh_over = [gu], [gg], gh_own, []
    for c in chunks:
        gu, gg, bu_c, bg_c, last = ffn_backward([after(gm_far[c], last)], weights, saved_far[c], sup, sgate, BF16)
        gh_over.append(swap(last, "mp", 2))
        gus.append(gu)
        ggs.append(gg)
        bu, bg = bu + bu_c, bg + bg_c
    grad_mlp = weight_grads(
        [h_own] + h_far,
        gm_own + gm_far,
        gus,
        ggs,
        [saved_own[1]] + [saved[1] for saved in saved_far],
        weights.shape,
    )
    grad_mlp, *gh_over = lax.optimization_barrier((grad_mlp, *gh_over))
    gh_over = jnp.concatenate(gh_over)
    grad_mlp = lax.psum_scatter(
        grad_mlp.reshape(-1, part), ("dp", "mp"), scatter_dimension=0, tiled=True, axis_index_groups=chip_groups()
    ).astype(F32)
    grad_up, grad_gate, grad_down = jnp.split(grad_mlp, 3, axis=0)

    grad_attn, grad_x, att0, att1, att2, att3, by_one = own_call(
        attn_back_body,
        "attn_back_out",
        [(gh_own, D, 0, 0), (gh_over, D, 0, 0), (keep_two, D, 0, 0), (branch, D, 0, 0), (tokens, D, 0, 0)],
        [one],
        out_parts,
        [(local, D, BF16), (local, D, F32)] + [(local, width, BF16)] * 4,
        1,
        2 * local * D * D,
    )
    back_x = swap(jnp.concatenate([att2, att3]), "mp", 2)
    back_core = swap(jnp.concatenate([att1, back_x[local:]]), "mp", 1)
    g_att = jnp.concatenate([back_x[:local], back_core[local:], att0, back_core[:local]])
    outs = [dot(grad_attn, a[s : s + local], 0, 0) for a, _, s, _ in heads_in]
    core_out = swap(jnp.concatenate([outs[1], outs[3]], axis=1).astype(BF16), "mp", 1)
    core_out, g_att = lax.optimization_barrier((core_out, g_att))
    over_out = swap((outs[2] + core_out[:, width:].astype(F32)).astype(BF16), "mp", 2)
    grad_out = outs[0] + core_out[:, :width].astype(F32) + over_out.astype(F32)
    grads, g_sqk = attend_back(
        meta, queries, qrot, attended, inverse_mass, g_att, keys, vals, krot, kpos_cols, cosine, sine, sqk, docs
    )
    first, second = grads[: 2 * local], grads[2 * local :]
    qkv_sum = dot(x_first, first, 0, 0) + dot(x_second, second, 0, 0)
    half_sum, sent = scatter_y(qkv_sum, grad_out)
    mlp_squares = jnp.sum(grad_mlp * grad_mlp)
    qkv = after(attn, sent)[:, : 3 * width]
    second_tokens = dot(second, qkv, 1, 1).astype(BF16)
    to_core = swap(second_tokens, "mp", 1)
    partial = dot(first, after(qkv, second_tokens), 1, 1)
    for_x = (partial[local:] + to_core[local:].astype(F32)).astype(BF16)
    to_x = swap(for_x, "mp", 2)

    def placed(array, index):
        slots = lax.broadcasted_iota(jnp.int32, (4, 1), 0)
        return jnp.where(slots == index, array[None], 0.0)

    def quarters(by):
        return placed(by[0, 0], m & 2) + placed(by[1, 0], (m & 2) + 1)

    bu, bg, g_sqk, by_one, by_two, _ = lax.optimization_barrier((bu, bg, g_sqk, by_one, by_two, second_tokens))
    rows = [quarters(bu), quarters(bg), placed(g_sqk[0], m), by_one[0], by_two[0]]
    rows = [row.reshape(devices, -1) for row in rows]
    small = jnp.sum(to_all(after(jnp.concatenate(rows, axis=1), for_x)), axis=0)
    cuts, start = [], 0
    for row in rows:
        cuts.append(small[start : start + row.shape[1]])
        start += row.shape[1]
    g_sup, g_sgate, g_sqk, g_alpha_one, g_alpha_two = cuts

    def squared(*arrays):
        return sum(jnp.sum(array * array) for array in arrays)

    grad_attn = scatter_z(after(half_sum, for_x), mlp_squares)
    squares = mlp_squares + squared(grad_attn, small)
    g_qkv = [grad_attn[:, i * width : (i + 1) * width] for i in range(3)]
    grad_down, grad_out = turned(grad_down), turned(grad_attn[:, 3 * width :])
    to_x = after(to_x, squares)
    grad_tokens = grad_x + partial[:local] + to_core[:local].astype(F32) + to_x.astype(F32)
    pieces = tuple(g_qkv) + (grad_out, grad_up, grad_gate, grad_down)
    pieces = pieces + (g_sqk, g_sup, g_sgate, g_alpha_one, g_alpha_two)
    squares = jnp.sum(to_all(jnp.broadcast_to(squares, (devices, 128))), axis=0)
    grad_norm = jnp.sqrt(squares[0])
    mean_alphas = jnp.stack([jnp.mean(alpha_one), jnp.mean(alpha_two)])
    return (result, grad_tokens) + pieces + (grad_norm, mean_alphas)


def solution(mesh):
    both_axes = P(("dp", "mp"))
    rows = P(("dp", "mp"), None)
    in_specs = (
        (rows, rows, P("dp", None), P("dp", None))
        + (P("dp", "mp"),) * 3
        + (P("mp", "dp"),)
        + (P("dp", "mp"),) * 2
        + (P("mp", "dp"),)
        + (both_axes,) * 5
    )
    out_specs = (
        (rows, rows)
        + (P("dp", "mp"),) * 3
        + (P("mp", "dp"),)
        + (P("dp", "mp"),) * 2
        + (P("mp", "dp"),)
        + (both_axes,) * 5
        + (P(), P())
    )
    return jax.shard_map(shards, mesh=mesh, in_specs=in_specs, out_specs=out_specs, check_vma=False)
```

```python
import functools

import jax
import jax.numpy as jnp
from jax import lax
from jax.experimental import pallas as pl
from jax.experimental.layout import Layout, with_layout_constraint
from jax.experimental.pallas import tpu as pltpu
from jax.sharding import PartitionSpec as P

D = 1024
HEADS = 16
HEAD = D // HEADS
EPS = 1e-06
NEG = -1e30
BLOCK = 256
F32 = jnp.float32
BF16 = jnp.bfloat16


def mean_rows(tensor):
    return jnp.mean(tensor, axis=-1, keepdims=True)


def normed(tensor):
    factor = lax.rsqrt(mean_rows(tensor * tensor) + EPS)
    return tensor * factor, factor


def normed_back(incoming, unit, factor):
    return factor * (incoming - unit * mean_rows(incoming * unit))


def dot(left, right, left_dim=1, right_dim=0):
    return lax.dot_general(
        left, right, (((left_dim,), (right_dim,)), ((), ())), preferred_element_type=F32
    )


RING = (0, 2, 4, 6, 7, 5, 3, 1)


def swap(array, axis, bit):
    size = lax.axis_size(axis)
    return lax.ppermute(array, axis, [(i, i ^ bit) for i in range(size)])


def to_z(array, step):
    return lax.ppermute(
        array, "dp", [(z * 2 + y, ((z + step) % 4) * 2 + y) for z in range(4) for y in range(2)]
    )


def around(array, step):
    return lax.ppermute(array, "dp", [(RING[p], RING[(p + step) % 8]) for p in range(8)])


def after(array, *others):
    if not others:
        return array
    return lax.optimization_barrier((array,) + others)[0]


def gather(shard, before):
    if lax.axis_size("dp") != 8:
        full = lax.all_gather(shard, "dp", axis=0, tiled=True)
        return full, [(full,)] * 4
    d = lax.axis_index("dp")
    rows, width = shard.shape
    place = jnp.where((d & 1) == 0, d >> 1, 7 - (d >> 1))

    def put(full, part, step):
        q = (place + step) & 7
        index = jnp.where(q < 4, 2 * q, 2 * (7 - q) + 1)
        return lax.dynamic_update_slice(full, part, (index * rows, jnp.int32(0)))

    full = put(jnp.zeros((8 * rows, width), shard.dtype), shard, 0)
    ahead, behind, arrived = shard, shard, []
    for step in (1, 2, 3, 4):
        if step > 1:
            ahead, behind = lax.optimization_barrier((ahead, behind) + tuple(before[step - 1]))[:2]
        ahead = around(ahead, 1)
        full = put(full, ahead, -step)
        if step < 4:
            behind = around(behind, -1)
            full = put(full, behind, step)
        arrived.append((ahead, behind))
    return full, arrived


def chip_groups():
    return [
        [d * 4 + 2 * x + core for d in range(lax.axis_size("dp")) for core in range(2)]
        for x in range(2)
    ]


def scatter_z(half):
    if lax.axis_size("dp") != 8:
        return lax.psum_scatter(half.astype(F32), "dp", scatter_dimension=0, tiled=True)
    z = lax.axis_index("dp") >> 1
    total = lax.dynamic_index_in_dim(half, z, axis=0, keepdims=False)
    for step in (1, 2, 3):
        part = lax.dynamic_index_in_dim(half, (z + step) & 3, axis=0, keepdims=False)
        total = total + to_z(part.astype(BF16), step).astype(F32)
    return total


def turned(array):
    return with_layout_constraint(array, Layout(major_to_minor=(0, 1))).T


def to_all(rows):
    return lax.all_to_all(rows, ("dp", "mp"), 0, 0, tiled=True)


def rotate_half(tensor):
    width = tensor.shape[-1]
    lane = lax.broadcasted_iota(jnp.int32, tensor.shape, 1)
    ahead = pltpu.roll(tensor, width - HEAD // 2, 1)
    behind = pltpu.roll(tensor, HEAD // 2, 1)
    return jnp.where((lane & (HEAD - 1)) < HEAD // 2, -ahead, behind)


def head_mean(tensor):
    width = tensor.shape[-1]
    row = lax.broadcasted_iota(jnp.int32, (width, width), 0) // HEAD
    col = lax.broadcasted_iota(jnp.int32, (width, width), 1) // HEAD
    ones = jnp.where(row == col, 1.0 / HEAD, 0.0).astype(BF16)
    high = tensor.astype(BF16)
    rest = (tensor - high.astype(F32)).astype(BF16)
    return dot(high, ones) + dot(rest, ones)


def wide(table):
    return jnp.concatenate([table, table], axis=1)


def project_body(m_ref, x_ref, w_ref, cos_ref, sin_ref, sqk_ref, *refs):
    q_ref, k_ref, v_ref, qr_ref, kr_ref = refs[-5:]
    rows = x_ref[...]
    cosine, sine = wide(cos_ref[...]), wide(sin_ref[...])
    scale = sqk_ref[0:1, :]
    width = q_ref.shape[1]
    raws = [dot(rows, w_ref[:, i * width : (i + 1) * width]) for i in range(3)]
    v_ref[...] = raws[2].astype(BF16)
    for raw, out_ref, rot_ref in ((raws[0], q_ref, qr_ref), (raws[1], k_ref, kr_ref)):
        turned = raw * cosine + rotate_half(raw) * sine
        rot_ref[...] = turned
        unit = turned * lax.rsqrt(head_mean(turned * turned) + EPS)
        out_ref[...] = (unit * scale).astype(BF16)


def project(place, x_rows, weight, cosine, sine, sqk, previous, first):
    rows, width = x_rows.shape[0], weight.shape[1] // 4
    total = cosine.shape[0]
    per = total // 4 // BLOCK

    def row_block(i, m):
        return ((m[0] ^ (first + 2 * (i // per))) * per + i % per, 0)

    any_spec = pl.BlockSpec(memory_space=pl.ANY)
    table = pl.BlockSpec((BLOCK, cosine.shape[1]), row_block)
    out = pl.BlockSpec((BLOCK, width), row_block)
    shapes = [jax.ShapeDtypeStruct((total, width), t) for t in (BF16, BF16, BF16, F32, F32)]
    extra = list(previous) if previous is not None else []
    return pl.pallas_call(
        project_body,
        out_shape=shapes,
        grid_spec=pltpu.PrefetchScalarGridSpec(
            num_scalar_prefetch=1,
            grid=(rows // BLOCK,),
            in_specs=[
                pl.BlockSpec((BLOCK, x_rows.shape[1]), lambda i, m: (i, 0)),
                pl.BlockSpec((x_rows.shape[1], 3 * width), lambda i, m: (0, 0)),
                table,
                table,
                pl.BlockSpec((1, width), lambda i, m: (0, 0)),
            ]
            + [any_spec] * len(extra),
            out_specs=[out] * 5,
        ),
        input_output_aliases={6 + i: i for i in range(len(extra))},
        cost_estimate=pl.CostEstimate(
            flops=6 * rows * D * width, bytes_accessed=8 * rows * D, transcendentals=rows
        ),
        name="project",
    )(place, x_rows, weight, cosine, sine, sqk, *extra)


def head_lanes(array, head):
    lane = lax.broadcasted_iota(jnp.int32, array.shape, 1)
    return jnp.where(lane // HEAD == head, array, jnp.zeros_like(array))


def stack_heads(array):
    heads = array.shape[1] // HEAD
    return jnp.concatenate([head_lanes(array, h) for h in range(heads)], axis=0)


def doc_start(meta_ref, docs, slots):
    start = jnp.zeros_like(slots)
    end = 0
    for i in range(docs):
        length = meta_ref[1 + i]
        end = end + length
        start = start + jnp.where(slots >= end, length, 0)
    return start


def slot_place(rel):
    return (rel >> 1) + 2 * (rel & 1)


def block_at(block):
    return pl.ds(pl.multiple_of(block * BLOCK, BLOCK), BLOCK)


def split_heads(source_ref, split_ref):
    def one(block, carry):
        split_ref[block] = stack_heads(source_ref[block_at(block), :])
        return carry

    lax.fori_loop(0, source_ref.shape[0] // BLOCK, one, 0)


def attend_body(docs, first, meta_ref, q_ref, k_ref, v_ref, kpos_ref, *refs):
    o_ref, inv_ref, acc_ref, sum_ref, vs_ref = refs[-5:]
    per = k_ref.shape[0] // 4 // BLOCK
    index = pl.program_id(0)
    step = ((first + index // per) ^ meta_ref[0]) * per + index % per
    heads = q_ref.shape[1] // HEAD
    base = step * BLOCK
    low = doc_start(meta_ref, docs, base) // BLOCK

    @pl.when(index == 0)
    def _():
        split_heads(v_ref, vs_ref)

    scaled = q_ref[...] * jnp.bfloat16(HEAD**-0.5)
    queries = [head_lanes(scaled, h) for h in range(heads)]
    rows = lax.broadcasted_iota(jnp.int32, (BLOCK, BLOCK), 0) + base
    starts = doc_start(meta_ref, docs, rows)
    acc_ref[...] = jnp.zeros_like(acc_ref)
    sum_ref[...] = jnp.zeros_like(sum_ref)

    def visit(blocks, allowed):
        expos = []
        sums = [0.0] * heads
        for block, mask in zip(blocks, allowed):
            keys = k_ref[block_at(block), :]
            bias = jnp.where(mask, 0.0, NEG)
            for h in range(heads):
                expo = jnp.exp(dot(queries[h], keys, 1, 1) + bias)
                sums[h] = sums[h] + expo[:, :128] + expo[:, 128:]
                expos.append(expo.astype(BF16))
        for h in range(heads):
            sum_ref[h * BLOCK : (h + 1) * BLOCK, :] += sums[h]
        vals = jnp.concatenate([vs_ref[block] for block in blocks], axis=0)
        acc_ref[...] += dot(jnp.concatenate(expos, axis=1), vals)

    def one(block, carry):
        cols = lax.broadcasted_iota(jnp.int32, (BLOCK, BLOCK), 1) + block * BLOCK
        same = kpos_ref[0:1, block_at(block)] >= starts
        visit([block], [(same & (cols <= rows)) | (cols == rows)])
        return carry

    lax.fori_loop(low, step + 1, one, 0)
    lane = lax.broadcasted_iota(jnp.int32, (BLOCK, q_ref.shape[1]), 1) // HEAD
    inverse = jnp.zeros((BLOCK, q_ref.shape[1]), F32)
    for h in range(heads):
        mass = jnp.sum(sum_ref[h * BLOCK : (h + 1) * BLOCK, :], axis=1, keepdims=True)
        inverse = jnp.where(lane == h, 1.0 / mass, inverse)
    inv_ref[...] = inverse
    o_ref[...] = (acc_ref[...] * inverse).astype(BF16)


def attend(meta, queries, keys, vals, kpos, docs, first, previous):
    total, width = queries.shape
    per = total // 4 // BLOCK
    heads = width // HEAD
    whole = pl.BlockSpec((total, width), lambda i, m: (0, 0))

    def natural(i, m):
        return (((first + i // per) ^ m[0]) * per + i % per, 0)

    block = pl.BlockSpec((BLOCK, width), natural)
    out = pl.BlockSpec((BLOCK, width), lambda i, m: ((first ^ 2) * per + i, 0))
    extra = list(previous)
    return pl.pallas_call(
        functools.partial(attend_body, docs, first),
        out_shape=[
            jax.ShapeDtypeStruct((total, width), BF16),
            jax.ShapeDtypeStruct((total, width), F32),
        ],
        grid_spec=pltpu.PrefetchScalarGridSpec(
            num_scalar_prefetch=1,
            grid=(2 * per,),
            in_specs=[block, whole, whole, pl.BlockSpec((1, total), lambda i, m: (0, 0))]
            + [pl.BlockSpec(memory_space=pl.ANY)] * len(extra),
            out_specs=[out, block],
            scratch_shapes=[
                pltpu.VMEM((BLOCK, width), F32),
                pltpu.VMEM((heads * BLOCK, 128), F32),
                pltpu.VMEM((total // BLOCK, heads * BLOCK, width), BF16),
            ],
        ),
        input_output_aliases={5 + i: i for i in range(len(extra))},
        cost_estimate=pl.CostEstimate(
            flops=8_000_000_000, bytes_accessed=8 * total * width, transcendentals=3_000_000
        ),
        name="attend",
    )(meta, queries, keys, vals, kpos, *extra)


def finish(grad, turned, cosine, sine, scale):
    factor = lax.rsqrt(head_mean(turned * turned) + EPS)
    unit = turned * factor
    by_scale = jnp.sum(grad * unit, axis=0, keepdims=True)
    scaled = grad * scale
    back = factor * (scaled - unit * head_mean(scaled * unit))
    raw = back * cosine - rotate_half(back) * sine
    return raw.astype(BF16), by_scale


def back_body(
    docs,
    meta_ref,
    q_ref,
    qr_ref,
    o_ref,
    inv_ref,
    do_ref,
    k_ref,
    v_ref,
    kr_ref,
    kpos_ref,
    cos_ref,
    sin_ref,
    sqk_ref,
    g_ref,
    gs_ref,
    dq_ref,
    dk_ref,
    dv_ref,
    ks_ref,
):
    step = pl.program_id(0)
    width = q_ref.shape[1]
    heads = width // HEAD
    per = k_ref.shape[0] // 4 // BLOCK
    base = step * BLOCK
    low = doc_start(meta_ref, docs, base) // BLOCK

    @pl.when(step == 0)
    def _():
        dk_ref[...] = jnp.zeros_like(dk_ref)
        dv_ref[...] = jnp.zeros_like(dv_ref)
        gs_ref[...] = jnp.zeros_like(gs_ref)
        split_heads(k_ref, ks_ref)

    dq_ref[...] = jnp.zeros_like(dq_ref)
    scaled = q_ref[...] * jnp.bfloat16(HEAD**-0.5)
    queries = [head_lanes(scaled, h) for h in range(heads)]
    all_queries = jnp.concatenate(queries, axis=0)
    upward = do_ref[...].astype(F32) * inv_ref[...]
    ups = [head_lanes(upward.astype(BF16), h) for h in range(heads)]
    all_ups = jnp.concatenate(ups, axis=0)
    picks = lax.broadcasted_iota(jnp.int32, (8, width), 0)
    lanes = lax.broadcasted_iota(jnp.int32, (8, width), 1) // HEAD
    delta = lax.dot_general(
        jnp.where(picks == lanes, 1.0, 0.0).astype(F32),
        upward * o_ref[...].astype(F32),
        (((1,), (1,)), ((), ())),
        precision=lax.Precision.HIGHEST,
        preferred_element_type=F32,
    )
    cols = lax.broadcasted_iota(jnp.int32, (BLOCK, BLOCK), 1) + base
    starts = doc_start(meta_ref, docs, cols)

    def visit(block, count, allowed):
        rows_at = pl.ds(pl.multiple_of(block * BLOCK, BLOCK), count * BLOCK)
        keys, vals = k_ref[rows_at, :], v_ref[rows_at, :]
        bias = jnp.where(allowed, 0.0, NEG)
        expos, slopes = [], []
        for h in range(heads):
            expo = jnp.exp(dot(keys, queries[h], 1, 1) + bias)
            expos.append(expo.astype(BF16))
            slope = expo * (dot(vals, ups[h], 1, 1) - delta[h : h + 1, :])
            slopes.append(slope.astype(BF16))
        dv_ref[rows_at, :] += dot(jnp.concatenate(expos, axis=1), all_ups)
        dk_ref[rows_at, :] += dot(jnp.concatenate(slopes, axis=1), all_queries)
        pieces = [slope[i * BLOCK : (i + 1) * BLOCK] for i in range(count) for slope in slopes]
        split = jnp.concatenate([ks_ref[block + i] for i in range(count)], axis=0)
        dq_ref[...] += dot(jnp.concatenate(pieces, axis=0), split, 0, 0)

    pairs = (step - low) >> 1

    def pair(i, carry):
        block = low + 2 * i
        keys_at = pl.ds(pl.multiple_of(block * BLOCK, BLOCK), 2 * BLOCK)
        visit(block, 2, wide(kpos_ref[keys_at, :]) >= jnp.concatenate([starts, starts], axis=0))
        return carry

    def one(block, carry):
        rows = lax.broadcasted_iota(jnp.int32, (BLOCK, BLOCK), 0) + block * BLOCK
        same = wide(kpos_ref[block_at(block), :]) >= starts
        visit(block, 1, (same & (rows <= cols)) | (rows == cols))
        return carry

    lax.fori_loop(0, pairs, pair, 0)
    lax.fori_loop(low + 2 * pairs, step + 1, one, 0)

    scale = sqk_ref[0:1, :]
    here = pl.ds(pl.multiple_of(base, BLOCK), BLOCK)
    raw, by_scale = finish(
        dq_ref[...] * (HEAD**-0.5),
        qr_ref[...],
        wide(cos_ref[here, :]),
        wide(sin_ref[here, :]),
        scale,
    )
    slot = slot_place(meta_ref[0] ^ (step // per)) * per + step % per
    g_ref[pl.ds(pl.multiple_of(slot * BLOCK, BLOCK), BLOCK), :width] = raw
    gs_ref[0:1, :] += by_scale

    @pl.when(step == pl.num_programs(0) - 1)
    def _():
        def one(block, carry):
            at = pl.ds(pl.multiple_of(block * BLOCK, BLOCK), BLOCK)
            slot = slot_place(meta_ref[0] ^ (block // per)) * per + block % per
            to = pl.ds(pl.multiple_of(slot * BLOCK, BLOCK), BLOCK)
            raw, by_scale = finish(
                dk_ref[at, :], kr_ref[at, :], wide(cos_ref[at, :]), wide(sin_ref[at, :]), scale
            )
            g_ref[to, width : 2 * width] = raw
            gs_ref[0:1, :] += by_scale
            g_ref[to, 2 * width :] = dv_ref[at, :].astype(BF16)
            return carry

        lax.fori_loop(0, pl.num_programs(0), one, 0)


def attend_back(meta, queries, qrot, out, inverse, grad, keys, vals, krot, kpos, cosine, sine, sqk, docs):
    total, width = queries.shape
    per = total // 4 // BLOCK

    def rel(i, m):
        return ((m[0] ^ (i // per) ^ 2) * per + i % per, 0)

    whole = pl.BlockSpec((total, width), lambda i, m: (0, 0))
    half = pl.BlockSpec((total, 128), lambda i, m: (0, 0))
    block = pl.BlockSpec((BLOCK, width), lambda i, m: (i, 0))
    moved = pl.BlockSpec((BLOCK, width), rel)
    return pl.pallas_call(
        functools.partial(back_body, docs),
        out_shape=[
            jax.ShapeDtypeStruct((total, 3 * width), BF16),
            jax.ShapeDtypeStruct((8, width), F32),
        ],
        grid_spec=pltpu.PrefetchScalarGridSpec(
            num_scalar_prefetch=1,
            grid=(total // BLOCK,),
            in_specs=[block, block, moved, block, moved, whole, whole, whole, half, half, half]
            + [pl.BlockSpec((1, width), lambda i, m: (0, 0))],
            out_specs=[
                pl.BlockSpec((total, 3 * width), lambda i, m: (0, 0)),
                pl.BlockSpec((8, width), lambda i, m: (0, 0)),
            ],
            scratch_shapes=[
                pltpu.VMEM((BLOCK, width), F32),
                pltpu.VMEM((total, width), F32),
                pltpu.VMEM((total, width), F32),
                pltpu.VMEM((total // BLOCK, width // HEAD * BLOCK, width), BF16),
            ],
        ),
        cost_estimate=pl.CostEstimate(
            flops=40_000_000_000, bytes_accessed=12 * total * width, transcendentals=6_000_000
        ),
        name="attend_back",
    )(meta, queries, qrot, out, inverse, grad, keys, vals, krot, kpos, cosine, sine, sqk)


TILE = 256


def weight_tile(weight_ref, part, index):
    return weight_ref[:, part, index].reshape(D, TILE)


def weight_spec(weights):
    return pl.BlockSpec(weights.shape[:4] + (TILE,), lambda t: (0, 0, 0, 0, t))


def forward_body(
    h_ref, w_ref, sup_ref, sgate_ref, gate_ref, act_ref, by_up_ref, by_gate_ref, out_ref, acc_ref
):
    t = pl.program_id(0)
    rows = h_ref[...]
    acts = []
    for part in range(2):
        sup, sgate = sup_ref[part, 0:1, :], sgate_ref[part, 0:1, :]
        scaled = sup * dot(rows, weight_tile(w_ref, part, 0))
        gate_proj = dot(rows, weight_tile(w_ref, part, 1))
        outer = sgate * gate_proj
        sigma = jax.nn.sigmoid(outer)
        silu = outer * sigma
        acts.append((scaled * silu).astype(BF16))
        gate_ref[part] = gate_proj.astype(BF16)
        act_ref[part] = acts[part]
        by_up_ref[part] = (sup * silu).astype(BF16)
        by_gate_ref[part] = ((sgate * scaled) * (sigma + silu * (1.0 - sigma))).astype(BF16)
    total = dot(
        jnp.concatenate(acts, axis=1),
        jnp.concatenate([weight_tile(w_ref, part, 2) for part in range(2)], axis=1),
        1,
        1,
    )
    add_up(t, total, acc_ref, out_ref)


def add_up(t, total, acc_ref, out_ref):
    @pl.when(t == 0)
    def _():
        acc_ref[...] = total

    @pl.when((t > 0) & (t < pl.num_programs(0) - 1))
    def _():
        acc_ref[...] += total

    @pl.when(t == pl.num_programs(0) - 1)
    def _():
        out_ref[...] = (acc_ref[...] + total).astype(out_ref.dtype)


def ffn_specs(count):
    whole = pl.BlockSpec((count, D), lambda t: (0, 0))
    tile = pl.BlockSpec((2, count, TILE), lambda t: (0, 0, t))
    scale = pl.BlockSpec((2, 1, TILE), lambda t: (0, 0, t))
    return whole, tile, scale


def ffn_forward(rows, weights, sup, sgate, kind):
    count, hidden = rows.shape[0], sup.shape[2]
    whole, tile, scale = ffn_specs(count)
    return pl.pallas_call(
        forward_body,
        out_shape=[jax.ShapeDtypeStruct((2, count, hidden), BF16)] * 4
        + [jax.ShapeDtypeStruct((count, D), kind)],
        grid=(hidden // TILE,),
        in_specs=[whole, weight_spec(weights), scale, scale],
        out_specs=[tile] * 4 + [whole],
        scratch_shapes=[pltpu.VMEM((count, D), F32)],
        cost_estimate=pl.CostEstimate(
            flops=12 * count * D * hidden,
            bytes_accessed=12 * D * hidden + 12 * count * hidden,
            transcendentals=2 * count * hidden,
        ),
        name="ffn_forward",
    )(rows, weights, sup, sgate)


def backward_body(pieces, *refs):
    rows = jnp.concatenate([ref[...] for ref in refs[:pieces]], axis=0)
    w_ref, gate_ref, act_ref, by_up_ref, by_gate_ref, sup_ref, sgate_ref = refs[pieces : pieces + 7]
    gu_ref, gg_ref, bu_ref, bg_ref, out_ref, acc_ref = refs[pieces + 7 :]
    t = pl.program_id(0)
    lefts, rights = [], []
    for part in range(2):
        g_act = dot(rows, weight_tile(w_ref, part, 2))
        g_up = (g_act * by_up_ref[part].astype(F32)).astype(BF16)
        g_gate = g_act * by_gate_ref[part].astype(F32)
        up_sum = jnp.sum(g_act * act_ref[part].astype(F32), axis=0, keepdims=True)
        gate_sum = jnp.sum(g_gate * gate_ref[part].astype(F32), axis=0, keepdims=True)
        g_gate = g_gate.astype(BF16)
        bu_ref[part, 0:1, :] = up_sum / sup_ref[part, 0:1, :]
        bg_ref[part, 0:1, :] = gate_sum / sgate_ref[part, 0:1, :]
        gu_ref[part] = g_up
        gg_ref[part] = g_gate
        lefts += [g_up, g_gate]
        rights += [weight_tile(w_ref, part, 0), weight_tile(w_ref, part, 1)]
    total = dot(jnp.concatenate(lefts, axis=1), jnp.concatenate(rights, axis=1), 1, 1)
    add_up(t, total, acc_ref, out_ref)


def ffn_backward(grads, weights, saved, sup, sgate, kind):
    count, hidden = sum(g.shape[0] for g in grads), sup.shape[2]
    whole, tile, scale = ffn_specs(count)
    sums = pl.BlockSpec((2, 8, TILE), lambda t: (0, 0, t))
    return pl.pallas_call(
        functools.partial(backward_body, len(grads)),
        out_shape=[jax.ShapeDtypeStruct((2, count, hidden), BF16)] * 2
        + [jax.ShapeDtypeStruct((2, 8, hidden), F32)] * 2
        + [jax.ShapeDtypeStruct((count, D), kind)],
        grid=(hidden // TILE,),
        in_specs=[pl.BlockSpec(g.shape, lambda t: (0, 0)) for g in grads]
        + [weight_spec(weights)]
        + [tile] * 4
        + [scale, scale],
        out_specs=[tile, tile, sums, sums, whole],
        scratch_shapes=[pltpu.VMEM((count, D), F32)],
        cost_estimate=pl.CostEstimate(
            flops=12 * count * D * hidden,
            bytes_accessed=12 * D * hidden + 24 * count * hidden,
            transcendentals=0,
        ),
        name="ffn_backward",
    )(*grads, weights, *saved, sup, sgate)


def weight_body(counts, *refs):
    h_count, g_count, m_count = counts
    take = iter(refs)
    hs = [next(take) for _ in range(h_count)]
    ms = [next(take) for _ in range(m_count)]
    ups, gates, acts = [[next(take) for _ in range(g_count)] for _ in range(3)]
    out_ref, ht_ref, mt_ref = refs[-3:]

    @pl.when(pl.program_id(0) == 0)
    def _():
        for pieces, to_ref in ((hs, ht_ref), (ms, mt_ref)):
            start = 0
            for ref in pieces:
                to_ref[:, start : start + ref.shape[0]] = ref[...].T
                start += ref.shape[0]

    for index, (left_ref, rights) in enumerate(((ht_ref, ups), (ht_ref, gates), (mt_ref, acts))):
        for part in range(2):
            right = jnp.concatenate([ref[part] for ref in rights], axis=0)
            total = dot(left_ref[...], right).astype(BF16)
            out_ref[:, part, index] = total.reshape(out_ref.shape[0], out_ref.shape[3], TILE)


def weight_grads(hs, ms, ups, gates, acts, shape):
    hidden = ups[0].shape[2]
    count = sum(h.shape[0] for h in hs)

    def whole(array):
        return pl.BlockSpec(array.shape, lambda t: (0, 0))

    def tile(array):
        return pl.BlockSpec((2, array.shape[1], TILE), lambda t: (0, 0, t))

    lefts, rights = list(hs) + list(ms), list(ups) + list(gates) + list(acts)
    return pl.pallas_call(
        functools.partial(weight_body, (len(hs), len(ups), len(ms))),
        out_shape=jax.ShapeDtypeStruct(shape, BF16),
        grid=(hidden // TILE,),
        in_specs=[whole(a) for a in lefts] + [tile(a) for a in rights],
        out_specs=pl.BlockSpec(shape[:4] + (TILE,), lambda t: (0, 0, 0, 0, t)),
        scratch_shapes=[pltpu.VMEM((D, count), BF16)] * 2,
        cost_estimate=pl.CostEstimate(
            flops=12 * count * D * hidden,
            bytes_accessed=12 * D * hidden + 12 * count * hidden,
            transcendentals=0,
        ),
        name="weight_grads",
    )(*lefts, *rights)


def attn_grad_body(m_ref, xf_ref, xs_ref, g_ref, out_ref, over_ref, mine_ref, sent_ref, xt_ref, sum_ref):
    t = pl.program_id(0)
    rows = xf_ref.shape[0]
    y = m_ref[1]

    @pl.when(t == 0)
    def _():
        def one(block, carry):
            for start, ref in ((0, xf_ref), (rows, xs_ref)):
                at = pl.ds(pl.multiple_of(start + block * BLOCK, BLOCK), BLOCK)
                xt_ref[:, at] = ref[block_at(block), :].T
            return carry

        lax.fori_loop(0, rows // BLOCK, one, 0)

    @pl.when(t < 3)
    def _():
        sum_ref[...] = dot(xt_ref[...], g_ref[...]).reshape(sum_ref.shape)

    @pl.when(t == 3)
    def _():
        sum_ref[...] = (out_ref[...] + over_ref[...].astype(F32)).reshape(sum_ref.shape)

    mine_ref[...] = sum_ref[:, y]
    sent_ref[...] = sum_ref[:, 1 - y].astype(BF16)


def attn_grads(place, x_first, x_second, grads, out_sum, over_out):
    width = out_sum.shape[1]
    rows = D // lax.axis_size("dp")

    def whole(array):
        return pl.BlockSpec(array.shape, lambda t, m: (0, 0))

    half = (D // rows // 2, rows, width)
    out = pl.BlockSpec(half, lambda t, m: (0, 0, t))
    return pl.pallas_call(
        attn_grad_body,
        out_shape=[
            jax.ShapeDtypeStruct(half[:2] + (4 * width,), F32),
            jax.ShapeDtypeStruct(half[:2] + (4 * width,), BF16),
        ],
        grid_spec=pltpu.PrefetchScalarGridSpec(
            num_scalar_prefetch=1,
            grid=(4,),
            in_specs=[
                whole(x_first),
                whole(x_second),
                pl.BlockSpec((grads.shape[0], width), lambda t, m: (0, jnp.minimum(t, 2))),
                whole(out_sum),
                whole(over_out),
            ],
            out_specs=[out, out],
            scratch_shapes=[
                pltpu.VMEM((D, grads.shape[0]), BF16),
                pltpu.VMEM((half[0], 2) + half[1:], F32),
            ],
        ),
        cost_estimate=pl.CostEstimate(
            flops=2 * D * grads.size, bytes_accessed=4 * grads.size, transcendentals=0
        ),
        name="attn_grads",
    )(place, x_first, x_second, grads, out_sum, over_out)


def to_tokens(grads, half, weight, kind):
    rows, width = grads.shape[0] // 2, grads.shape[1]
    step = rows // 2
    row = weight.shape[0]

    def body(g_ref, w_ref, out_ref):
        out_ref[...] = dot(g_ref[...], w_ref[...], 1, 1).astype(kind)

    return pl.pallas_call(
        body,
        out_shape=jax.ShapeDtypeStruct((rows, row), kind),
        grid=(2,),
        in_specs=[
            pl.BlockSpec((step, width), lambda i: (2 * half + i, 0)),
            pl.BlockSpec((row, width), lambda i: (0, 0)),
        ],
        out_specs=pl.BlockSpec((step, row), lambda i: (i, 0)),
        cost_estimate=pl.CostEstimate(
            flops=2 * rows * width * row, bytes_accessed=6 * rows * row, transcendentals=0
        ),
        name="to_tokens",
    )(grads, weight)


def own_call(body, name, rows_in, vectors, wholes, outs, sums, flops):
    count = outs[0][0]
    blocks = count // BLOCK

    def rows_spec(width, skip, column):
        return pl.BlockSpec((BLOCK, width), lambda i: (skip // BLOCK + i, column))

    in_specs = [rows_spec(w, s, c) for _, w, s, c in rows_in]
    in_specs += [pl.BlockSpec((1, v.shape[1]), lambda i: (0, 0)) for v in vectors]
    in_specs += [pl.BlockSpec((D, w), lambda i, c=c: (0, c)) for _, w, c in wholes]
    shapes = [jax.ShapeDtypeStruct((count, w), t) for count, w, t in outs]
    shapes += [jax.ShapeDtypeStruct((8, D), F32)] * sums
    out_specs = [pl.BlockSpec((BLOCK, w), lambda i: (i, 0)) for _, w, _ in outs]
    out_specs += [pl.BlockSpec((8, D), lambda i: (0, 0))] * sums
    return pl.pallas_call(
        body,
        out_shape=shapes,
        grid=(blocks,),
        in_specs=in_specs,
        out_specs=out_specs,
        cost_estimate=pl.CostEstimate(
            flops=flops, bytes_accessed=20 * count * D, transcendentals=count
        ),
        name=name,
    )(*[a for a, *_ in rows_in], *vectors, *[a for a, *_ in wholes])


def first_update(branch, x_rows, alpha):
    h_attn, attn_factor = normed(branch)
    hidden, one_factor = normed(x_rows + alpha * (h_attn - x_rows))
    return h_attn, attn_factor, hidden, one_factor


def attn_body(a0, a1, a2, a3, x_ref, alpha_ref, w0, w1, w2, w3, branch_ref, low_ref):
    branch = dot(a0[...], w0[...], 1, 1) + dot(a1[...], w1[...], 1, 1)
    branch = branch + dot(a2[...], w2[...], 1, 1) + dot(a3[...], w3[...], 1, 1)
    branch_ref[...] = branch
    hidden = first_update(branch, x_ref[...].astype(F32), alpha_ref[0:1, :])[2]
    low_ref[...] = hidden.astype(BF16)


def turn_body(own_ref, far_ref, branch_ref, x_ref, cot_ref, one_ref, two_ref, *refs):
    out_ref, keep_ref, gm_ref, sum_ref = refs[-4:]
    hidden = first_update(branch_ref[...], x_ref[...].astype(F32), one_ref[0:1, :])[2]
    alpha = two_ref[0:1, :]
    h_mlp, mlp_factor = normed(own_ref[...] + far_ref[...].astype(F32))
    step = h_mlp - hidden
    result, two_factor = normed(hidden + alpha * step)
    out_ref[...] = result.astype(BF16)
    grad_two = normed_back(cot_ref[...].astype(F32), result, two_factor)
    keep_ref[...] = grad_two * (1.0 - alpha)
    gm_ref[...] = normed_back(grad_two * alpha, h_mlp, mlp_factor).astype(BF16)

    @pl.when(pl.program_id(0) == 0)
    def _():
        sum_ref[...] = jnp.zeros_like(sum_ref)

    sum_ref[0:1, :] += jnp.sum(grad_two * step, axis=0, keepdims=True)


def turn(chunk, own, far, branch, x_rows, cotangent, one, two, previous):
    count = branch.shape[0]
    rows = pl.BlockSpec((BLOCK // 2, D), lambda i: (2 * chunk + i, 0))
    first = pl.BlockSpec((BLOCK // 2, D), lambda i: (i, 0))
    vector = pl.BlockSpec((1, D), lambda i: (0, 0))
    total = pl.BlockSpec((8, D), lambda i: (0, 0))
    extra = list(previous)
    return pl.pallas_call(
        turn_body,
        out_shape=[
            jax.ShapeDtypeStruct((count, D), BF16),
            jax.ShapeDtypeStruct((count, D), F32),
            jax.ShapeDtypeStruct((BLOCK, D), BF16),
            jax.ShapeDtypeStruct((8, D), F32),
        ],
        grid=(2,),
        in_specs=[rows, first, rows, rows, rows, vector, vector]
        + [pl.BlockSpec(memory_space=pl.ANY)] * len(extra),
        out_specs=[rows, rows, first, total],
        input_output_aliases={7 + i: i for i in range(len(extra))},
        cost_estimate=pl.CostEstimate(
            flops=60 * BLOCK * D, bytes_accessed=20 * BLOCK * D, transcendentals=BLOCK
        ),
        name="turn",
    )(own, far, branch, x_rows, cotangent, one, two, *extra)


def attn_back_body(
    own_ref, far_ref, keep_ref, branch_ref, x_ref, one_ref, w0, w1, w2, w3, ga_ref, gt_ref, o0, o1, o2, o3, sum_ref
):
    x_rows, alpha = x_ref[...].astype(F32), one_ref[0:1, :]
    h_attn, attn_factor, hidden, one_factor = first_update(branch_ref[...], x_rows, alpha)
    incoming = keep_ref[...] + own_ref[...] + far_ref[...].astype(F32)
    grad_one = normed_back(incoming, hidden, one_factor)
    gt_ref[...] = grad_one * (1.0 - alpha)
    grad_attn = normed_back(grad_one * alpha, h_attn, attn_factor).astype(BF16)
    ga_ref[...] = grad_attn
    for weight_ref, out_ref in ((w0, o0), (w1, o1), (w2, o2), (w3, o3)):
        out_ref[...] = dot(grad_attn, weight_ref[...]).astype(BF16)

    @pl.when(pl.program_id(0) == 0)
    def _():
        sum_ref[...] = jnp.zeros_like(sum_ref)

    sum_ref[0:1, :] += jnp.sum(grad_one * (h_attn - x_rows), axis=0, keepdims=True)


def shards(
    tokens,
    cotangent,
    lengths,
    key_mask,
    w_query,
    w_key,
    w_value,
    w_out,
    w_up,
    w_gate,
    w_down,
    s_qk,
    s_up,
    s_gate,
    alpha_attn,
    alpha_mlp,
):
    m = lax.axis_index("mp").astype(jnp.int32)
    devices = lax.axis_size("dp") * lax.axis_size("mp")
    local = tokens.shape[0]
    row_len = key_mask.shape[1]
    docs = lengths.shape[1]
    part = w_up.shape[1]
    width = w_query.shape[1]

    place = m.reshape(1)
    meta = jnp.concatenate([place, lengths[0]])
    slot_ids = jnp.arange(row_len, dtype=jnp.int32)
    steps_even = jnp.arange(0, HEAD, 2).astype(F32)
    frequencies = jnp.power(jnp.float32(10000.0), -steps_even / HEAD)
    frequencies = jnp.tile(frequencies, 4)[None, :]

    def turn_by(steps):
        angles = steps.astype(F32)[:, None] * frequencies
        return jnp.cos(angles), jnp.sin(angles)

    coarse_cos, coarse_sin = (t[:, None] for t in turn_by(jnp.arange(0, row_len, 64)))
    fine_cos, fine_sin = (t[None] for t in turn_by(jnp.arange(64)))
    slot_cos = (coarse_cos * fine_cos - coarse_sin * fine_sin).reshape(row_len, -1)
    slot_sin = (coarse_sin * fine_cos + coarse_cos * fine_sin).reshape(row_len, -1)
    first_slots = jnp.cumsum(lengths[0]) - lengths[0]
    doc_cos, doc_sin = turn_by(first_slots)
    start_cos, start_sin = doc_cos[0:1], doc_sin[0:1]
    for i in range(1, docs):
        later = (slot_ids >= first_slots[i])[:, None]
        start_cos = jnp.where(later, doc_cos[i : i + 1], start_cos)
        start_sin = jnp.where(later, doc_sin[i : i + 1], start_sin)
    cosine = slot_cos * start_cos + slot_sin * start_sin
    sine = slot_sin * start_cos - slot_cos * start_sin
    x_halves = [swap(tokens[i * local // 2 : (i + 1) * local // 2], "mp", 2) for i in range(2)]
    vector = jnp.concatenate([s_up, s_gate, s_qk, alpha_attn, alpha_mlp])[None]
    every = to_all(jnp.broadcast_to(vector, (devices, vector.shape[1])))
    attn, arrived = gather(
        jnp.concatenate([w_query, w_key, w_value, w_out.T], axis=1),
        [(), (), (x_halves[0],), (x_halves[1], every)],
    )
    x_first = jnp.concatenate([tokens, x_halves[0], after(x_halves[1], *arrived[2])], axis=0)
    x_second = swap(x_first, "mp", 1)
    shard = jnp.concatenate([w_up, w_gate, w_down.T], axis=0)
    shard = with_layout_constraint(after(shard, *arrived[2]), Layout(major_to_minor=(0, 1)))
    weights = lax.all_gather(
        shard, ("dp", "mp"), axis=0, tiled=True, axis_index_groups=chip_groups()
    ).reshape(-1, 2, 3, shard.shape[0] // 3, part)
    cuts, start = [], 0
    for piece in (s_up, s_gate, s_qk, alpha_attn, alpha_mlp):
        cuts.append(every[:, start : start + piece.shape[0]].reshape(-1))
        start += piece.shape[0]
    sup_all, sgate_all, sqk_all, alpha_one, alpha_two = cuts

    def quarter(array, index):
        size = array.shape[0] // 4
        return lax.dynamic_slice_in_dim(array, index * size, size)

    def row(array):
        return array[None]

    sqk = row(quarter(sqk_all, m))
    low = m & 2
    sup = jnp.stack([row(quarter(sup_all, low)), row(quarter(sup_all, low + 1))])
    sgate = jnp.stack([row(quarter(sgate_all, low)), row(quarter(sgate_all, low + 1))])
    one, two = row(alpha_one), row(alpha_two)
    out_mine = attn[:, 3 * width :]
    out_core = swap(out_mine, "mp", 1)
    out_over = swap(out_mine, "mp", 2)
    out_cross = swap(out_over, "mp", 1)
    out_parts = [(w, width, 0) for w in (out_mine, out_core, out_over, out_cross)]

    kpos = jnp.where(key_mask[0] == 1, slot_ids, -1)
    kpos_rows = kpos[None, :]
    kpos_cols = jnp.broadcast_to(kpos[:, None], (row_len, 128))

    half = project(place, x_first, attn, cosine, sine, sqk, None, 0)
    queries, keys, vals, qrot, krot = project(place, x_second, attn, cosine, sine, sqk, half, 1)
    half = attend(meta, queries, keys, vals, kpos_rows, docs, 2, ())
    far_core = swap(half[0][local : 2 * local], "mp", 1)
    for_x = jnp.concatenate([half[0][:local], far_core])
    by_x = swap(for_x, "mp", 2)
    half = [after(half[0], for_x), half[1]]
    attended, inverse_mass = attend(meta, queries, keys, vals, kpos_rows, docs, 0, half)
    by_core = swap(attended[3 * local :], "mp", 1)
    heads_in = [(attended, width, 2 * local, 0), (by_core, width, 0, 0), (by_x, width, 0, 0), (by_x, width, local, 0)]
    branch, h_own = own_call(
        attn_body,
        "attn_out",
        heads_in + [(tokens, D, 0, 0)],
        [one],
        out_parts,
        [(local, D, F32), (local, D, BF16)],
        0,
        2 * local * D * D,
    )

    chunks = range(local // BLOCK)
    h_far = [swap(h_own[c * BLOCK : (c + 1) * BLOCK], "mp", 2) for c in chunks]
    *saved_own, sum_own = ffn_forward(h_own, weights, sup, sgate, F32)
    saved_far, sum_far, last = [], [], sum_own
    for c in chunks:
        *saved, last = ffn_forward(after(h_far[c], last), weights, sup, sgate, BF16)
        saved_far.append(saved)
        sum_far.append(swap(last, "mp", 2))
    done, gm_own, gm_far, by_two = (), [], [], 0.0
    for c in chunks:
        *done, gm, by = turn(c, after(sum_own, last), sum_far[c], branch, tokens, cotangent, one, two, done)
        gm_own.append(gm)
        gm_far.append(swap(gm, "mp", 2))
        by_two = by_two + by
    result, keep_two = done
    gu, gg, bu, bg, gh_own = ffn_backward(gm_own, weights, saved_own, sup, sgate, F32)
    gus, ggs, last, gh_over = [gu], [gg], gh_own, []
    for c in chunks:
        gu, gg, bu_c, bg_c, last = ffn_backward([after(gm_far[c], last)], weights, saved_far[c], sup, sgate, BF16)
        gh_over.append(swap(last, "mp", 2))
        gus.append(gu)
        ggs.append(gg)
        bu, bg = bu + bu_c, bg + bg_c
    grad_mlp = weight_grads(
        [h_own] + h_far,
        gm_own + gm_far,
        gus,
        ggs,
        [saved_own[1]] + [saved[1] for saved in saved_far],
        weights.shape,
    )
    grad_mlp, *gh_over = lax.optimization_barrier((grad_mlp, *gh_over))
    gh_over = jnp.concatenate(gh_over)
    grad_mlp = lax.psum_scatter(
        grad_mlp.reshape(-1, part), ("dp", "mp"), scatter_dimension=0, tiled=True, axis_index_groups=chip_groups()
    ).astype(F32)
    grad_up, grad_gate, grad_down = jnp.split(grad_mlp, 3, axis=0)

    grad_attn, grad_x, att0, att1, att2, att3, by_one = own_call(
        attn_back_body,
        "attn_back_out",
        [(gh_own, D, 0, 0), (gh_over, D, 0, 0), (keep_two, D, 0, 0), (branch, D, 0, 0), (tokens, D, 0, 0)],
        [one],
        out_parts,
        [(local, D, BF16), (local, D, F32)] + [(local, width, BF16)] * 4,
        1,
        2 * local * D * D,
    )
    back_x = swap(jnp.concatenate([att2, att3]), "mp", 2)
    back_core = swap(jnp.concatenate([att1, back_x[local:]]), "mp", 1)
    g_att = jnp.concatenate([back_x[:local], back_core[local:], att0, back_core[:local]])
    outs = [dot(grad_attn, a[s : s + local], 0, 0) for a, _, s, _ in heads_in]
    core_out = swap(jnp.concatenate([outs[1], outs[3]], axis=1).astype(BF16), "mp", 1)
    core_out, g_att = lax.optimization_barrier((core_out, g_att))
    over_out = swap((outs[2] + core_out[:, width:].astype(F32)).astype(BF16), "mp", 2)
    out_sum = outs[0] + core_out[:, :width].astype(F32)
    grads, g_sqk = attend_back(
        meta, queries, qrot, attended, inverse_mass, g_att, keys, vals, krot, kpos_cols, cosine, sine, sqk, docs
    )
    if lax.axis_size("dp") == 8:
        both = jnp.stack([m, lax.axis_index("dp").astype(jnp.int32) & 1])
        half_sum, sent = attn_grads(both, x_first, x_second, grads, out_sum, over_out)
        half_sum = half_sum + swap(sent, "dp", 1).astype(F32)
    else:
        sent = dot(x_first, grads[: 2 * local], 0, 0) + dot(x_second, grads[2 * local :], 0, 0)
        half_sum = jnp.concatenate([sent, out_sum + over_out.astype(F32)], axis=1)
    mlp_squares = jnp.sum(grad_mlp * grad_mlp)
    second_tokens = to_tokens(after(grads, sent), 1, attn, BF16)
    to_core = swap(second_tokens, "mp", 1)
    partial = to_tokens(after(grads, second_tokens), 0, attn, F32)
    for_x = (partial[local:] + to_core[local:].astype(F32)).astype(BF16)
    to_x = swap(for_x, "mp", 2)

    def placed(array, index):
        slots = lax.broadcasted_iota(jnp.int32, (4, 1), 0)
        return jnp.where(slots == index, array[None], 0.0)

    def quarters(by):
        return placed(by[0, 0], m & 2) + placed(by[1, 0], (m & 2) + 1)

    bu, bg, g_sqk, by_one, by_two, _ = lax.optimization_barrier((bu, bg, g_sqk, by_one, by_two, second_tokens))
    rows = [quarters(bu), quarters(bg), placed(g_sqk[0], m), by_one[0], by_two[0]]
    rows = [row.reshape(devices, -1) for row in rows]
    small = jnp.sum(to_all(after(jnp.concatenate(rows, axis=1), for_x)), axis=0)
    cuts, start = [], 0
    for row in rows:
        cuts.append(small[start : start + row.shape[1]])
        start += row.shape[1]
    g_sup, g_sgate, g_sqk, g_alpha_one, g_alpha_two = cuts

    def squared(*arrays):
        return sum(jnp.sum(array * array) for array in arrays)

    grad_attn = scatter_z(after(half_sum, for_x))
    squares = mlp_squares + squared(grad_attn, small)
    g_qkv = [grad_attn[:, i * width : (i + 1) * width] for i in range(3)]
    grad_down, grad_out = turned(after(grad_down, squares)), turned(after(grad_attn, squares)[:, 3 * width :])
    to_x = after(to_x, squares)
    grad_tokens = grad_x + partial[:local] + to_core[:local].astype(F32) + to_x.astype(F32)
    pieces = tuple(g_qkv) + (grad_out, grad_up, grad_gate, grad_down)
    pieces = pieces + (g_sqk, g_sup, g_sgate, g_alpha_one, g_alpha_two)
    squares = jnp.sum(to_all(jnp.broadcast_to(squares, (devices, 128))), axis=0)
    grad_norm = jnp.sqrt(squares[0])
    mean_alphas = jnp.stack([jnp.mean(alpha_one), jnp.mean(alpha_two)])
    return (result, grad_tokens) + pieces + (grad_norm, mean_alphas)


def solution(mesh):
    both_axes = P(("dp", "mp"))
    rows = P(("dp", "mp"), None)
    in_specs = (
        (rows, rows, P("dp", None), P("dp", None))
        + (P("dp", "mp"),) * 3
        + (P("mp", "dp"),)
        + (P("dp", "mp"),) * 2
        + (P("mp", "dp"),)
        + (both_axes,) * 5
    )
    out_specs = (
        (rows, rows)
        + (P("dp", "mp"),) * 3
        + (P("mp", "dp"),)
        + (P("dp", "mp"),) * 2
        + (P("mp", "dp"),)
        + (both_axes,) * 5
        + (P(), P())
    )
    return jax.shard_map(shards, mesh=mesh, in_specs=in_specs, out_specs=out_specs, check_vma=False)
```

```python
import functools

import jax
import jax.numpy as jnp
from jax import lax
from jax.experimental import pallas as pl
from jax.experimental.layout import Layout, with_layout_constraint
from jax.experimental.pallas import tpu as pltpu
from jax.sharding import PartitionSpec as P

D = 1024
HEADS = 16
HEAD = D // HEADS
EPS = 1e-06
NEG = -1e30
BLOCK = 256
F32 = jnp.float32
BF16 = jnp.bfloat16


def mean_rows(tensor):
    return jnp.mean(tensor, axis=-1, keepdims=True)


def normed(tensor):
    factor = lax.rsqrt(mean_rows(tensor * tensor) + EPS)
    return tensor * factor, factor


def normed_back(incoming, unit, factor):
    return factor * (incoming - unit * mean_rows(incoming * unit))


def dot(left, right, left_dim=1, right_dim=0):
    return lax.dot_general(
        left, right, (((left_dim,), (right_dim,)), ((), ())), preferred_element_type=F32
    )


RING = (0, 2, 4, 6, 7, 5, 3, 1)


def swap(array, axis, bit):
    size = lax.axis_size(axis)
    return lax.ppermute(array, axis, [(i, i ^ bit) for i in range(size)])


def to_z(array, step):
    return lax.ppermute(
        array, "dp", [(z * 2 + y, ((z + step) % 4) * 2 + y) for z in range(4) for y in range(2)]
    )


def around(array, step):
    return lax.ppermute(array, "dp", [(RING[p], RING[(p + step) % 8]) for p in range(8)])


def after(array, *others):
    if not others:
        return array
    return lax.optimization_barrier((array,) + others)[0]


def gather(shard, before):
    if lax.axis_size("dp") != 8:
        full = lax.all_gather(shard, "dp", axis=0, tiled=True)
        return full, [(full,)] * 4
    d = lax.axis_index("dp")
    rows, width = shard.shape
    place = jnp.where((d & 1) == 0, d >> 1, 7 - (d >> 1))

    def put(full, part, step):
        q = (place + step) & 7
        index = jnp.where(q < 4, 2 * q, 2 * (7 - q) + 1)
        return lax.dynamic_update_slice(full, part, (index * rows, jnp.int32(0)))

    full = put(jnp.zeros((8 * rows, width), shard.dtype), shard, 0)
    ahead, behind, arrived = shard, shard, []
    for step in (1, 2, 3, 4):
        if step > 1:
            ahead, behind = lax.optimization_barrier((ahead, behind) + tuple(before[step - 1]))[:2]
        ahead = around(ahead, 1)
        full = put(full, ahead, -step)
        if step < 4:
            behind = around(behind, -1)
            full = put(full, behind, step)
        arrived.append((ahead, behind))
    return full, arrived


def chip_groups():
    return [
        [d * 4 + 2 * x + core for d in range(lax.axis_size("dp")) for core in range(2)]
        for x in range(2)
    ]


def scatter_z(half):
    if lax.axis_size("dp") != 8:
        return lax.psum_scatter(half.astype(F32), "dp", scatter_dimension=0, tiled=True)
    z = lax.axis_index("dp") >> 1
    total = lax.dynamic_index_in_dim(half, z, axis=0, keepdims=False)
    for step in (1, 2, 3):
        part = lax.dynamic_index_in_dim(half, (z + step) & 3, axis=0, keepdims=False)
        total = total + to_z(part.astype(BF16), step).astype(F32)
    return total


def turned(array):
    return with_layout_constraint(array, Layout(major_to_minor=(0, 1))).T


def to_all(rows):
    return lax.all_to_all(rows, ("dp", "mp"), 0, 0, tiled=True)


def rotate_half(tensor):
    width = tensor.shape[-1]
    lane = lax.broadcasted_iota(jnp.int32, tensor.shape, 1)
    ahead = pltpu.roll(tensor, width - HEAD // 2, 1)
    behind = pltpu.roll(tensor, HEAD // 2, 1)
    return jnp.where((lane & (HEAD - 1)) < HEAD // 2, -ahead, behind)


def head_mean(tensor):
    width = tensor.shape[-1]
    row = lax.broadcasted_iota(jnp.int32, (width, width), 0) // HEAD
    col = lax.broadcasted_iota(jnp.int32, (width, width), 1) // HEAD
    ones = jnp.where(row == col, 1.0 / HEAD, 0.0).astype(BF16)
    high = tensor.astype(BF16)
    rest = (tensor - high.astype(F32)).astype(BF16)
    return dot(high, ones) + dot(rest, ones)


def wide(table):
    return jnp.concatenate([table, table], axis=1)


def project_body(m_ref, x_ref, w_ref, cos_ref, sin_ref, sqk_ref, *refs):
    q_ref, k_ref, v_ref, qr_ref, kr_ref = refs[-5:]
    rows = x_ref[...]
    cosine, sine = wide(cos_ref[...]), wide(sin_ref[...])
    scale = sqk_ref[0:1, :]
    width = q_ref.shape[1]
    raws = [dot(rows, w_ref[:, i * width : (i + 1) * width]) for i in range(3)]
    v_ref[...] = raws[2].astype(BF16)
    for raw, out_ref, rot_ref in ((raws[0], q_ref, qr_ref), (raws[1], k_ref, kr_ref)):
        turned = raw * cosine + rotate_half(raw) * sine
        rot_ref[...] = turned
        unit = turned * lax.rsqrt(head_mean(turned * turned) + EPS)
        out_ref[...] = (unit * scale).astype(BF16)


def project(place, x_rows, weight, cosine, sine, sqk, previous, first):
    rows, width = x_rows.shape[0], weight.shape[1] // 4
    total = cosine.shape[0]
    per = total // 4 // BLOCK

    def row_block(i, m):
        return ((m[0] ^ (first + 2 * (i // per))) * per + i % per, 0)

    any_spec = pl.BlockSpec(memory_space=pl.ANY)
    table = pl.BlockSpec((BLOCK, cosine.shape[1]), row_block)
    out = pl.BlockSpec((BLOCK, width), row_block)
    shapes = [jax.ShapeDtypeStruct((total, width), t) for t in (BF16, BF16, BF16, F32, F32)]
    extra = list(previous) if previous is not None else []
    return pl.pallas_call(
        project_body,
        out_shape=shapes,
        grid_spec=pltpu.PrefetchScalarGridSpec(
            num_scalar_prefetch=1,
            grid=(rows // BLOCK,),
            in_specs=[
                pl.BlockSpec((BLOCK, x_rows.shape[1]), lambda i, m: (i, 0)),
                pl.BlockSpec((x_rows.shape[1], 3 * width), lambda i, m: (0, 0)),
                table,
                table,
                pl.BlockSpec((1, width), lambda i, m: (0, 0)),
            ]
            + [any_spec] * len(extra),
            out_specs=[out] * 5,
        ),
        input_output_aliases={6 + i: i for i in range(len(extra))},
        cost_estimate=pl.CostEstimate(
            flops=6 * rows * D * width, bytes_accessed=8 * rows * D, transcendentals=rows
        ),
        name="project",
    )(place, x_rows, weight, cosine, sine, sqk, *extra)


def head_lanes(array, head):
    lane = lax.broadcasted_iota(jnp.int32, array.shape, 1)
    return jnp.where(lane // HEAD == head, array, jnp.zeros_like(array))


def stack_heads(array):
    heads = array.shape[1] // HEAD
    return jnp.concatenate([head_lanes(array, h) for h in range(heads)], axis=0)


def doc_start(meta_ref, docs, slots):
    start = jnp.zeros_like(slots)
    end = 0
    for i in range(docs):
        length = meta_ref[1 + i]
        end = end + length
        start = start + jnp.where(slots >= end, length, 0)
    return start


def slot_place(rel):
    return (rel >> 1) + 2 * (rel & 1)


def block_at(block):
    return pl.ds(pl.multiple_of(block * BLOCK, BLOCK), BLOCK)


def split_heads(source_ref, split_ref):
    def one(block, carry):
        split_ref[block] = stack_heads(source_ref[block_at(block), :])
        return carry

    lax.fori_loop(0, source_ref.shape[0] // BLOCK, one, 0)


def attend_body(docs, first, meta_ref, q_ref, k_ref, v_ref, kpos_ref, *refs):
    o_ref, inv_ref, acc_ref, sum_ref, vs_ref = refs[-5:]
    per = k_ref.shape[0] // 4 // BLOCK
    index = pl.program_id(0)
    step = ((first + index // per) ^ meta_ref[0]) * per + index % per
    heads = q_ref.shape[1] // HEAD
    base = step * BLOCK
    low = doc_start(meta_ref, docs, base) // BLOCK

    @pl.when(index == 0)
    def _():
        split_heads(v_ref, vs_ref)

    scaled = q_ref[...] * jnp.bfloat16(HEAD**-0.5)
    queries = [head_lanes(scaled, h) for h in range(heads)]
    rows = lax.broadcasted_iota(jnp.int32, (BLOCK, BLOCK), 0) + base
    starts = doc_start(meta_ref, docs, rows)
    acc_ref[...] = jnp.zeros_like(acc_ref)
    sum_ref[...] = jnp.zeros_like(sum_ref)

    def visit(blocks, allowed):
        expos = []
        sums = [0.0] * heads
        for block, mask in zip(blocks, allowed):
            keys = k_ref[block_at(block), :]
            bias = jnp.where(mask, 0.0, NEG)
            for h in range(heads):
                expo = jnp.exp(dot(queries[h], keys, 1, 1) + bias)
                sums[h] = sums[h] + expo[:, :128] + expo[:, 128:]
                expos.append(expo.astype(BF16))
        for h in range(heads):
            sum_ref[h * BLOCK : (h + 1) * BLOCK, :] += sums[h]
        vals = jnp.concatenate([vs_ref[block] for block in blocks], axis=0)
        acc_ref[...] += dot(jnp.concatenate(expos, axis=1), vals)

    def one(block, carry):
        cols = lax.broadcasted_iota(jnp.int32, (BLOCK, BLOCK), 1) + block * BLOCK
        same = kpos_ref[0:1, block_at(block)] >= starts
        visit([block], [(same & (cols <= rows)) | (cols == rows)])
        return carry

    lax.fori_loop(low, step + 1, one, 0)
    lane = lax.broadcasted_iota(jnp.int32, (BLOCK, q_ref.shape[1]), 1) // HEAD
    inverse = jnp.zeros((BLOCK, q_ref.shape[1]), F32)
    for h in range(heads):
        mass = jnp.sum(sum_ref[h * BLOCK : (h + 1) * BLOCK, :], axis=1, keepdims=True)
        inverse = jnp.where(lane == h, 1.0 / mass, inverse)
    inv_ref[...] = inverse
    o_ref[...] = (acc_ref[...] * inverse).astype(BF16)


def attend(meta, queries, keys, vals, kpos, docs, first, previous):
    total, width = queries.shape
    per = total // 4 // BLOCK
    heads = width // HEAD
    whole = pl.BlockSpec((total, width), lambda i, m: (0, 0))

    def natural(i, m):
        return (((first + i // per) ^ m[0]) * per + i % per, 0)

    block = pl.BlockSpec((BLOCK, width), natural)
    out = pl.BlockSpec((BLOCK, width), lambda i, m: ((first ^ 2) * per + i, 0))
    extra = list(previous)
    return pl.pallas_call(
        functools.partial(attend_body, docs, first),
        out_shape=[
            jax.ShapeDtypeStruct((total, width), BF16),
            jax.ShapeDtypeStruct((total, width), F32),
        ],
        grid_spec=pltpu.PrefetchScalarGridSpec(
            num_scalar_prefetch=1,
            grid=(2 * per,),
            in_specs=[block, whole, whole, pl.BlockSpec((1, total), lambda i, m: (0, 0))]
            + [pl.BlockSpec(memory_space=pl.ANY)] * len(extra),
            out_specs=[out, block],
            scratch_shapes=[
                pltpu.VMEM((BLOCK, width), F32),
                pltpu.VMEM((heads * BLOCK, 128), F32),
                pltpu.VMEM((total // BLOCK, heads * BLOCK, width), BF16),
            ],
        ),
        input_output_aliases={5 + i: i for i in range(len(extra))},
        cost_estimate=pl.CostEstimate(
            flops=8_000_000_000, bytes_accessed=8 * total * width, transcendentals=3_000_000
        ),
        name="attend",
    )(meta, queries, keys, vals, kpos, *extra)


def finish(grad, turned, cosine, sine, scale):
    factor = lax.rsqrt(head_mean(turned * turned) + EPS)
    unit = turned * factor
    by_scale = jnp.sum(grad * unit, axis=0, keepdims=True)
    scaled = grad * scale
    back = factor * (scaled - unit * head_mean(scaled * unit))
    raw = back * cosine - rotate_half(back) * sine
    return raw.astype(BF16), by_scale


def back_body(
    docs,
    meta_ref,
    q_ref,
    qr_ref,
    o_ref,
    inv_ref,
    do_ref,
    k_ref,
    v_ref,
    kr_ref,
    kpos_ref,
    cos_ref,
    sin_ref,
    sqk_ref,
    g_ref,
    gs_ref,
    dq_ref,
    dk_ref,
    dv_ref,
    ks_ref,
):
    step = pl.program_id(0)
    width = q_ref.shape[1]
    heads = width // HEAD
    per = k_ref.shape[0] // 4 // BLOCK
    base = step * BLOCK
    low = doc_start(meta_ref, docs, base) // BLOCK

    @pl.when(step == 0)
    def _():
        dk_ref[...] = jnp.zeros_like(dk_ref)
        dv_ref[...] = jnp.zeros_like(dv_ref)
        gs_ref[...] = jnp.zeros_like(gs_ref)
        split_heads(k_ref, ks_ref)

    dq_ref[...] = jnp.zeros_like(dq_ref)
    scaled = q_ref[...] * jnp.bfloat16(HEAD**-0.5)
    queries = [head_lanes(scaled, h) for h in range(heads)]
    all_queries = jnp.concatenate(queries, axis=0)
    upward = do_ref[...].astype(F32) * inv_ref[...]
    ups = [head_lanes(upward.astype(BF16), h) for h in range(heads)]
    all_ups = jnp.concatenate(ups, axis=0)
    picks = lax.broadcasted_iota(jnp.int32, (8, width), 0)
    lanes = lax.broadcasted_iota(jnp.int32, (8, width), 1) // HEAD
    delta = lax.dot_general(
        jnp.where(picks == lanes, 1.0, 0.0).astype(F32),
        upward * o_ref[...].astype(F32),
        (((1,), (1,)), ((), ())),
        precision=lax.Precision.HIGHEST,
        preferred_element_type=F32,
    )
    cols = lax.broadcasted_iota(jnp.int32, (BLOCK, BLOCK), 1) + base
    starts = doc_start(meta_ref, docs, cols)

    def visit(block, count, allowed):
        rows_at = pl.ds(pl.multiple_of(block * BLOCK, BLOCK), count * BLOCK)
        keys, vals = k_ref[rows_at, :], v_ref[rows_at, :]
        bias = jnp.where(allowed, 0.0, NEG)
        expos, slopes = [], []
        for h in range(heads):
            expo = jnp.exp(dot(keys, queries[h], 1, 1) + bias)
            expos.append(expo.astype(BF16))
            slope = expo * (dot(vals, ups[h], 1, 1) - delta[h : h + 1, :])
            slopes.append(slope.astype(BF16))
        dv_ref[rows_at, :] += dot(jnp.concatenate(expos, axis=1), all_ups)
        dk_ref[rows_at, :] += dot(jnp.concatenate(slopes, axis=1), all_queries)
        pieces = [slope[i * BLOCK : (i + 1) * BLOCK] for i in range(count) for slope in slopes]
        split = jnp.concatenate([ks_ref[block + i] for i in range(count)], axis=0)
        dq_ref[...] += dot(jnp.concatenate(pieces, axis=0), split, 0, 0)

    pairs = (step - low) >> 1

    def pair(i, carry):
        block = low + 2 * i
        keys_at = pl.ds(pl.multiple_of(block * BLOCK, BLOCK), 2 * BLOCK)
        visit(block, 2, wide(kpos_ref[keys_at, :]) >= jnp.concatenate([starts, starts], axis=0))
        return carry

    def one(block, carry):
        rows = lax.broadcasted_iota(jnp.int32, (BLOCK, BLOCK), 0) + block * BLOCK
        same = wide(kpos_ref[block_at(block), :]) >= starts
        visit(block, 1, (same & (rows <= cols)) | (rows == cols))
        return carry

    lax.fori_loop(0, pairs, pair, 0)
    lax.fori_loop(low + 2 * pairs, step + 1, one, 0)

    scale = sqk_ref[0:1, :]
    here = pl.ds(pl.multiple_of(base, BLOCK), BLOCK)
    raw, by_scale = finish(
        dq_ref[...] * (HEAD**-0.5),
        qr_ref[...],
        wide(cos_ref[here, :]),
        wide(sin_ref[here, :]),
        scale,
    )
    slot = slot_place(meta_ref[0] ^ (step // per)) * per + step % per
    g_ref[pl.ds(pl.multiple_of(slot * BLOCK, BLOCK), BLOCK), :width] = raw
    gs_ref[0:1, :] += by_scale

    @pl.when(step == pl.num_programs(0) - 1)
    def _():
        def one(block, carry):
            at = pl.ds(pl.multiple_of(block * BLOCK, BLOCK), BLOCK)
            slot = slot_place(meta_ref[0] ^ (block // per)) * per + block % per
            to = pl.ds(pl.multiple_of(slot * BLOCK, BLOCK), BLOCK)
            raw, by_scale = finish(
                dk_ref[at, :], kr_ref[at, :], wide(cos_ref[at, :]), wide(sin_ref[at, :]), scale
            )
            g_ref[to, width : 2 * width] = raw
            gs_ref[0:1, :] += by_scale
            g_ref[to, 2 * width :] = dv_ref[at, :].astype(BF16)
            return carry

        lax.fori_loop(0, pl.num_programs(0), one, 0)


def attend_back(meta, queries, qrot, out, inverse, grad, keys, vals, krot, kpos, cosine, sine, sqk, docs):
    total, width = queries.shape
    per = total // 4 // BLOCK

    def rel(i, m):
        return ((m[0] ^ (i // per) ^ 2) * per + i % per, 0)

    whole = pl.BlockSpec((total, width), lambda i, m: (0, 0))
    half = pl.BlockSpec((total, 128), lambda i, m: (0, 0))
    block = pl.BlockSpec((BLOCK, width), lambda i, m: (i, 0))
    moved = pl.BlockSpec((BLOCK, width), rel)
    return pl.pallas_call(
        functools.partial(back_body, docs),
        out_shape=[
            jax.ShapeDtypeStruct((total, 3 * width), BF16),
            jax.ShapeDtypeStruct((8, width), F32),
        ],
        grid_spec=pltpu.PrefetchScalarGridSpec(
            num_scalar_prefetch=1,
            grid=(total // BLOCK,),
            in_specs=[block, block, moved, block, moved, whole, whole, whole, half, half, half]
            + [pl.BlockSpec((1, width), lambda i, m: (0, 0))],
            out_specs=[
                pl.BlockSpec((total, 3 * width), lambda i, m: (0, 0)),
                pl.BlockSpec((8, width), lambda i, m: (0, 0)),
            ],
            scratch_shapes=[
                pltpu.VMEM((BLOCK, width), F32),
                pltpu.VMEM((total, width), F32),
                pltpu.VMEM((total, width), F32),
                pltpu.VMEM((total // BLOCK, width // HEAD * BLOCK, width), BF16),
            ],
        ),
        cost_estimate=pl.CostEstimate(
            flops=40_000_000_000, bytes_accessed=12 * total * width, transcendentals=6_000_000
        ),
        name="attend_back",
    )(meta, queries, qrot, out, inverse, grad, keys, vals, krot, kpos, cosine, sine, sqk)


TILE = 256


def weight_tile(weight_ref, part, index):
    return weight_ref[:, part, index].reshape(D, TILE)


def weight_spec(weights):
    return pl.BlockSpec(weights.shape[:4] + (TILE,), lambda t: (0, 0, 0, 0, t))


def forward_body(
    h_ref, w_ref, sup_ref, sgate_ref, gate_ref, act_ref, by_up_ref, by_gate_ref, out_ref, acc_ref
):
    t = pl.program_id(0)
    rows = h_ref[...]
    acts = []
    for part in range(2):
        sup, sgate = sup_ref[part, 0:1, :], sgate_ref[part, 0:1, :]
        scaled = sup * dot(rows, weight_tile(w_ref, part, 0))
        gate_proj = dot(rows, weight_tile(w_ref, part, 1))
        outer = sgate * gate_proj
        sigma = jax.nn.sigmoid(outer)
        silu = outer * sigma
        acts.append((scaled * silu).astype(BF16))
        gate_ref[part] = gate_proj.astype(BF16)
        act_ref[part] = acts[part]
        by_up_ref[part] = (sup * silu).astype(BF16)
        by_gate_ref[part] = ((sgate * scaled) * (sigma + silu * (1.0 - sigma))).astype(BF16)
    total = dot(
        jnp.concatenate(acts, axis=1),
        jnp.concatenate([weight_tile(w_ref, part, 2) for part in range(2)], axis=1),
        1,
        1,
    )
    add_up(t, total, acc_ref, out_ref)


def add_up(t, total, acc_ref, out_ref):
    @pl.when(t == 0)
    def _():
        acc_ref[...] = total

    @pl.when((t > 0) & (t < pl.num_programs(0) - 1))
    def _():
        acc_ref[...] += total

    @pl.when(t == pl.num_programs(0) - 1)
    def _():
        out_ref[...] = (acc_ref[...] + total).astype(out_ref.dtype)


def ffn_specs(count):
    whole = pl.BlockSpec((count, D), lambda t: (0, 0))
    tile = pl.BlockSpec((2, count, TILE), lambda t: (0, 0, t))
    scale = pl.BlockSpec((2, 1, TILE), lambda t: (0, 0, t))
    return whole, tile, scale


def ffn_forward(rows, weights, sup, sgate, kind):
    count, hidden = rows.shape[0], sup.shape[2]
    whole, tile, scale = ffn_specs(count)
    return pl.pallas_call(
        forward_body,
        out_shape=[jax.ShapeDtypeStruct((2, count, hidden), BF16)] * 4
        + [jax.ShapeDtypeStruct((count, D), kind)],
        grid=(hidden // TILE,),
        in_specs=[whole, weight_spec(weights), scale, scale],
        out_specs=[tile] * 4 + [whole],
        scratch_shapes=[pltpu.VMEM((count, D), F32)],
        cost_estimate=pl.CostEstimate(
            flops=12 * count * D * hidden,
            bytes_accessed=12 * D * hidden + 12 * count * hidden,
            transcendentals=2 * count * hidden,
        ),
        name="ffn_forward",
    )(rows, weights, sup, sgate)


def backward_body(pieces, groups, *refs):
    rows = jnp.concatenate([ref[...] for ref in refs[:pieces]], axis=0)
    w_ref, kept = refs[pieces], refs[pieces + 1 : pieces + 1 + 4 * groups]
    sup_ref, sgate_ref, gu_ref, gg_ref, bu_ref, bg_ref, out_ref, acc_ref = refs[pieces + 1 + 4 * groups :]
    t = pl.program_id(0)

    def saved(index, part):
        return jnp.concatenate([kept[4 * g + index][part] for g in range(groups)], axis=0).astype(F32)

    lefts, rights = [], []
    for part in range(2):
        g_act = dot(rows, weight_tile(w_ref, part, 2))
        g_up = (g_act * saved(2, part)).astype(BF16)
        g_gate = g_act * saved(3, part)
        up_sum = jnp.sum(g_act * saved(1, part), axis=0, keepdims=True)
        gate_sum = jnp.sum(g_gate * saved(0, part), axis=0, keepdims=True)
        g_gate = g_gate.astype(BF16)
        bu_ref[part, 0:1, :] = up_sum / sup_ref[part, 0:1, :]
        bg_ref[part, 0:1, :] = gate_sum / sgate_ref[part, 0:1, :]
        gu_ref[part] = g_up
        gg_ref[part] = g_gate
        lefts += [g_up, g_gate]
        rights += [weight_tile(w_ref, part, 0), weight_tile(w_ref, part, 1)]
    total = dot(jnp.concatenate(lefts, axis=1), jnp.concatenate(rights, axis=1), 1, 1)
    add_up(t, total, acc_ref, out_ref)


def ffn_backward(grads, weights, saved, sup, sgate, kind):
    count, hidden = sum(g.shape[0] for g in grads), sup.shape[2]
    whole, tile, scale = ffn_specs(count)
    sums = pl.BlockSpec((2, 8, TILE), lambda t: (0, 0, t))
    return pl.pallas_call(
        functools.partial(backward_body, len(grads), len(saved)),
        out_shape=[jax.ShapeDtypeStruct((2, count, hidden), BF16)] * 2
        + [jax.ShapeDtypeStruct((2, 8, hidden), F32)] * 2
        + [jax.ShapeDtypeStruct((count, D), kind)],
        grid=(hidden // TILE,),
        in_specs=[pl.BlockSpec(g.shape, lambda t: (0, 0)) for g in grads]
        + [weight_spec(weights)]
        + [pl.BlockSpec((2, k.shape[1], TILE), lambda t: (0, 0, t)) for group in saved for k in group]
        + [scale, scale],
        out_specs=[tile, tile, sums, sums, whole],
        scratch_shapes=[pltpu.VMEM((count, D), F32)],
        cost_estimate=pl.CostEstimate(
            flops=12 * count * D * hidden,
            bytes_accessed=12 * D * hidden + 24 * count * hidden,
            transcendentals=0,
        ),
        name="ffn_backward",
    )(*grads, weights, *[k for group in saved for k in group], sup, sgate)


def weight_body(counts, *refs):
    h_count, m_count, g_count, a_count = counts
    take = iter(refs)
    hs = [next(take) for _ in range(h_count)]
    ms = [next(take) for _ in range(m_count)]
    ups, gates, acts = [[next(take) for _ in range(n)] for n in (g_count, g_count, a_count)]
    out_ref, ht_ref, mt_ref = refs[-3:]

    @pl.when(pl.program_id(0) == 0)
    def _():
        for pieces, to_ref in ((hs, ht_ref), (ms, mt_ref)):
            start = 0
            for ref in pieces:
                to_ref[:, start : start + ref.shape[0]] = ref[...].T
                start += ref.shape[0]

    for index, (left_ref, rights) in enumerate(((ht_ref, ups), (ht_ref, gates), (mt_ref, acts))):
        for part in range(2):
            right = jnp.concatenate([ref[part] for ref in rights], axis=0)
            total = dot(left_ref[...], right).astype(BF16)
            out_ref[:, part, index] = total.reshape(out_ref.shape[0], out_ref.shape[3], TILE)


def weight_grads(hs, ms, ups, gates, acts, shape):
    hidden = ups[0].shape[2]
    count = sum(h.shape[0] for h in hs)

    def whole(array):
        return pl.BlockSpec(array.shape, lambda t: (0, 0))

    def tile(array):
        return pl.BlockSpec((2, array.shape[1], TILE), lambda t: (0, 0, t))

    lefts, rights = list(hs) + list(ms), list(ups) + list(gates) + list(acts)
    return pl.pallas_call(
        functools.partial(weight_body, (len(hs), len(ms), len(ups), len(acts))),
        out_shape=jax.ShapeDtypeStruct(shape, BF16),
        grid=(hidden // TILE,),
        in_specs=[whole(a) for a in lefts] + [tile(a) for a in rights],
        out_specs=pl.BlockSpec(shape[:4] + (TILE,), lambda t: (0, 0, 0, 0, t)),
        scratch_shapes=[pltpu.VMEM((D, count), BF16)] * 2,
        cost_estimate=pl.CostEstimate(
            flops=12 * count * D * hidden,
            bytes_accessed=12 * D * hidden + 12 * count * hidden,
            transcendentals=0,
        ),
        name="weight_grads",
    )(*lefts, *rights)


def attn_grad_body(m_ref, xf_ref, xs_ref, g_ref, out_ref, over_ref, mine_ref, sent_ref, xt_ref, sum_ref):
    t = pl.program_id(0)
    rows = xf_ref.shape[0]
    y = m_ref[1]

    @pl.when(t == 0)
    def _():
        def one(block, carry):
            for start, ref in ((0, xf_ref), (rows, xs_ref)):
                at = pl.ds(pl.multiple_of(start + block * BLOCK, BLOCK), BLOCK)
                xt_ref[:, at] = ref[block_at(block), :].T
            return carry

        lax.fori_loop(0, rows // BLOCK, one, 0)

    @pl.when(t < 3)
    def _():
        sum_ref[...] = dot(xt_ref[...], g_ref[...]).reshape(sum_ref.shape)

    @pl.when(t == 3)
    def _():
        sum_ref[...] = (out_ref[...] + over_ref[...].astype(F32)).reshape(sum_ref.shape)

    mine_ref[...] = sum_ref[:, y]
    sent_ref[...] = sum_ref[:, 1 - y].astype(BF16)


def attn_grads(place, x_first, x_second, grads, out_sum, over_out):
    width = out_sum.shape[1]
    rows = D // lax.axis_size("dp")

    def whole(array):
        return pl.BlockSpec(array.shape, lambda t, m: (0, 0))

    half = (D // rows // 2, rows, width)
    out = pl.BlockSpec(half, lambda t, m: (0, 0, t))
    return pl.pallas_call(
        attn_grad_body,
        out_shape=[
            jax.ShapeDtypeStruct(half[:2] + (4 * width,), F32),
            jax.ShapeDtypeStruct(half[:2] + (4 * width,), BF16),
        ],
        grid_spec=pltpu.PrefetchScalarGridSpec(
            num_scalar_prefetch=1,
            grid=(4,),
            in_specs=[
                whole(x_first),
                whole(x_second),
                pl.BlockSpec((grads.shape[0], width), lambda t, m: (0, jnp.minimum(t, 2))),
                whole(out_sum),
                whole(over_out),
            ],
            out_specs=[out, out],
            scratch_shapes=[
                pltpu.VMEM((D, grads.shape[0]), BF16),
                pltpu.VMEM((half[0], 2) + half[1:], F32),
            ],
        ),
        cost_estimate=pl.CostEstimate(
            flops=2 * D * grads.size, bytes_accessed=4 * grads.size, transcendentals=0
        ),
        name="attn_grads",
    )(place, x_first, x_second, grads, out_sum, over_out)


def to_tokens(grads, half, weight, kind):
    rows, width = grads.shape[0] // 2, grads.shape[1]
    step = rows // 2
    row = weight.shape[0]

    def body(g_ref, w_ref, out_ref):
        out_ref[...] = dot(g_ref[...], w_ref[...], 1, 1).astype(kind)

    return pl.pallas_call(
        body,
        out_shape=jax.ShapeDtypeStruct((rows, row), kind),
        grid=(2,),
        in_specs=[
            pl.BlockSpec((step, width), lambda i: (2 * half + i, 0)),
            pl.BlockSpec((row, width), lambda i: (0, 0)),
        ],
        out_specs=pl.BlockSpec((step, row), lambda i: (i, 0)),
        cost_estimate=pl.CostEstimate(
            flops=2 * rows * width * row, bytes_accessed=6 * rows * row, transcendentals=0
        ),
        name="to_tokens",
    )(grads, weight)


def own_call(body, name, rows_in, vectors, wholes, outs, sums, flops):
    count = outs[0][0]
    blocks = count // BLOCK

    def rows_spec(width, skip, column):
        return pl.BlockSpec((BLOCK, width), lambda i: (skip // BLOCK + i, column))

    in_specs = [rows_spec(w, s, c) for _, w, s, c in rows_in]
    in_specs += [pl.BlockSpec((1, v.shape[1]), lambda i: (0, 0)) for v in vectors]
    in_specs += [pl.BlockSpec((D, w), lambda i, c=c: (0, c)) for _, w, c in wholes]
    shapes = [jax.ShapeDtypeStruct((count, w), t) for count, w, t in outs]
    shapes += [jax.ShapeDtypeStruct((8, D), F32)] * sums
    out_specs = [pl.BlockSpec((BLOCK, w), lambda i: (i, 0)) for _, w, _ in outs]
    out_specs += [pl.BlockSpec((8, D), lambda i: (0, 0))] * sums
    return pl.pallas_call(
        body,
        out_shape=shapes,
        grid=(blocks,),
        in_specs=in_specs,
        out_specs=out_specs,
        cost_estimate=pl.CostEstimate(
            flops=flops, bytes_accessed=20 * count * D, transcendentals=count
        ),
        name=name,
    )(*[a for a, *_ in rows_in], *vectors, *[a for a, *_ in wholes])


def first_update(branch, x_rows, alpha):
    h_attn, attn_factor = normed(branch)
    hidden, one_factor = normed(x_rows + alpha * (h_attn - x_rows))
    return h_attn, attn_factor, hidden, one_factor


def attn_body(a0, a1, a2, a3, x_ref, alpha_ref, w0, w1, w2, w3, branch_ref, low_ref):
    branch = dot(a0[...], w0[...], 1, 1) + dot(a1[...], w1[...], 1, 1)
    branch = branch + dot(a2[...], w2[...], 1, 1) + dot(a3[...], w3[...], 1, 1)
    branch_ref[...] = branch
    hidden = first_update(branch, x_ref[...].astype(F32), alpha_ref[0:1, :])[2]
    low_ref[...] = hidden.astype(BF16)


def turn_body(own_ref, far_ref, branch_ref, x_ref, cot_ref, one_ref, two_ref, *refs):
    out_ref, keep_ref, gm_ref, sum_ref = refs[-4:]
    hidden = first_update(branch_ref[...], x_ref[...].astype(F32), one_ref[0:1, :])[2]
    alpha = two_ref[0:1, :]
    h_mlp, mlp_factor = normed(own_ref[...] + far_ref[...].astype(F32))
    step = h_mlp - hidden
    result, two_factor = normed(hidden + alpha * step)
    out_ref[...] = result.astype(BF16)
    grad_two = normed_back(cot_ref[...].astype(F32), result, two_factor)
    keep_ref[...] = grad_two * (1.0 - alpha)
    gm_ref[...] = normed_back(grad_two * alpha, h_mlp, mlp_factor).astype(BF16)

    @pl.when(pl.program_id(0) == 0)
    def _():
        sum_ref[...] = jnp.zeros_like(sum_ref)

    sum_ref[0:1, :] += jnp.sum(grad_two * step, axis=0, keepdims=True)


def turn(chunk, own, far, branch, x_rows, cotangent, one, two, previous):
    count = branch.shape[0]
    rows = pl.BlockSpec((BLOCK // 2, D), lambda i: (2 * chunk + i, 0))
    first = pl.BlockSpec((BLOCK // 2, D), lambda i: (i, 0))
    vector = pl.BlockSpec((1, D), lambda i: (0, 0))
    total = pl.BlockSpec((8, D), lambda i: (0, 0))
    extra = list(previous)
    return pl.pallas_call(
        turn_body,
        out_shape=[
            jax.ShapeDtypeStruct((count, D), BF16),
            jax.ShapeDtypeStruct((count, D), F32),
            jax.ShapeDtypeStruct((BLOCK, D), BF16),
            jax.ShapeDtypeStruct((8, D), F32),
        ],
        grid=(2,),
        in_specs=[rows, first, rows, rows, rows, vector, vector]
        + [pl.BlockSpec(memory_space=pl.ANY)] * len(extra),
        out_specs=[rows, rows, first, total],
        input_output_aliases={7 + i: i for i in range(len(extra))},
        cost_estimate=pl.CostEstimate(
            flops=60 * BLOCK * D, bytes_accessed=20 * BLOCK * D, transcendentals=BLOCK
        ),
        name="turn",
    )(own, far, branch, x_rows, cotangent, one, two, *extra)


def attn_back_body(
    own_ref, far_ref, keep_ref, branch_ref, x_ref, one_ref, w0, w1, w2, w3, ga_ref, gt_ref, o0, o1, o2, o3, sum_ref
):
    x_rows, alpha = x_ref[...].astype(F32), one_ref[0:1, :]
    h_attn, attn_factor, hidden, one_factor = first_update(branch_ref[...], x_rows, alpha)
    incoming = keep_ref[...] + own_ref[...] + far_ref[...].astype(F32)
    grad_one = normed_back(incoming, hidden, one_factor)
    gt_ref[...] = grad_one * (1.0 - alpha)
    grad_attn = normed_back(grad_one * alpha, h_attn, attn_factor).astype(BF16)
    ga_ref[...] = grad_attn
    for weight_ref, out_ref in ((w0, o0), (w1, o1), (w2, o2), (w3, o3)):
        out_ref[...] = dot(grad_attn, weight_ref[...]).astype(BF16)

    @pl.when(pl.program_id(0) == 0)
    def _():
        sum_ref[...] = jnp.zeros_like(sum_ref)

    sum_ref[0:1, :] += jnp.sum(grad_one * (h_attn - x_rows), axis=0, keepdims=True)


def shards(
    tokens,
    cotangent,
    lengths,
    key_mask,
    w_query,
    w_key,
    w_value,
    w_out,
    w_up,
    w_gate,
    w_down,
    s_qk,
    s_up,
    s_gate,
    alpha_attn,
    alpha_mlp,
):
    m = lax.axis_index("mp").astype(jnp.int32)
    devices = lax.axis_size("dp") * lax.axis_size("mp")
    local = tokens.shape[0]
    row_len = key_mask.shape[1]
    docs = lengths.shape[1]
    part = w_up.shape[1]
    width = w_query.shape[1]

    place = m.reshape(1)
    meta = jnp.concatenate([place, lengths[0]])
    slot_ids = jnp.arange(row_len, dtype=jnp.int32)
    steps_even = jnp.arange(0, HEAD, 2).astype(F32)
    frequencies = jnp.power(jnp.float32(10000.0), -steps_even / HEAD)
    frequencies = jnp.tile(frequencies, 4)[None, :]

    def turn_by(steps):
        angles = steps.astype(F32)[:, None] * frequencies
        return jnp.cos(angles), jnp.sin(angles)

    coarse_cos, coarse_sin = (t[:, None] for t in turn_by(jnp.arange(0, row_len, 64)))
    fine_cos, fine_sin = (t[None] for t in turn_by(jnp.arange(64)))
    slot_cos = (coarse_cos * fine_cos - coarse_sin * fine_sin).reshape(row_len, -1)
    slot_sin = (coarse_sin * fine_cos + coarse_cos * fine_sin).reshape(row_len, -1)
    first_slots = jnp.cumsum(lengths[0]) - lengths[0]
    doc_cos, doc_sin = turn_by(first_slots)
    start_cos, start_sin = doc_cos[0:1], doc_sin[0:1]
    for i in range(1, docs):
        later = (slot_ids >= first_slots[i])[:, None]
        start_cos = jnp.where(later, doc_cos[i : i + 1], start_cos)
        start_sin = jnp.where(later, doc_sin[i : i + 1], start_sin)
    cosine = slot_cos * start_cos + slot_sin * start_sin
    sine = slot_sin * start_cos - slot_cos * start_sin
    x_halves = [swap(tokens[i * local // 2 : (i + 1) * local // 2], "mp", 2) for i in range(2)]
    vector = jnp.concatenate([s_up, s_gate, s_qk, alpha_attn, alpha_mlp])[None]
    every = to_all(jnp.broadcast_to(vector, (devices, vector.shape[1])))
    attn, arrived = gather(
        jnp.concatenate([w_query, w_key, w_value, w_out.T], axis=1),
        [(), (), (x_halves[0],), (x_halves[1], every)],
    )
    x_first = jnp.concatenate([tokens, x_halves[0], after(x_halves[1], *arrived[2])], axis=0)
    x_second = swap(x_first, "mp", 1)
    shard = jnp.concatenate([w_up, w_gate, w_down.T], axis=0)
    shard = with_layout_constraint(after(shard, *arrived[2]), Layout(major_to_minor=(0, 1)))
    weights = lax.all_gather(
        shard, ("dp", "mp"), axis=0, tiled=True, axis_index_groups=chip_groups()
    ).reshape(-1, 2, 3, shard.shape[0] // 3, part)
    cuts, start = [], 0
    for piece in (s_up, s_gate, s_qk, alpha_attn, alpha_mlp):
        cuts.append(every[:, start : start + piece.shape[0]].reshape(-1))
        start += piece.shape[0]
    sup_all, sgate_all, sqk_all, alpha_one, alpha_two = cuts

    def quarter(array, index):
        size = array.shape[0] // 4
        return lax.dynamic_slice_in_dim(array, index * size, size)

    def row(array):
        return array[None]

    sqk = row(quarter(sqk_all, m))
    low = m & 2
    sup = jnp.stack([row(quarter(sup_all, low)), row(quarter(sup_all, low + 1))])
    sgate = jnp.stack([row(quarter(sgate_all, low)), row(quarter(sgate_all, low + 1))])
    one, two = row(alpha_one), row(alpha_two)
    out_mine = attn[:, 3 * width :]
    out_core = swap(out_mine, "mp", 1)
    out_over = swap(out_mine, "mp", 2)
    out_cross = swap(out_over, "mp", 1)
    out_parts = [(w, width, 0) for w in (out_mine, out_core, out_over, out_cross)]

    kpos = jnp.where(key_mask[0] == 1, slot_ids, -1)
    kpos_rows = kpos[None, :]
    kpos_cols = jnp.broadcast_to(kpos[:, None], (row_len, 128))
    x_second, kpos_cols = lax.optimization_barrier((x_second, kpos_cols))

    half = project(place, x_first, attn, cosine, sine, sqk, None, 0)
    queries, keys, vals, qrot, krot = project(place, x_second, attn, cosine, sine, sqk, half, 1)
    half = attend(meta, queries, keys, vals, kpos_rows, docs, 2, ())
    far_core = swap(half[0][local : 2 * local], "mp", 1)
    for_x = jnp.concatenate([half[0][:local], far_core])
    by_x = swap(for_x, "mp", 2)
    half = [after(half[0], for_x), half[1]]
    attended, inverse_mass = attend(meta, queries, keys, vals, kpos_rows, docs, 0, half)
    by_core = swap(attended[3 * local :], "mp", 1)
    heads_in = [(attended, width, 2 * local, 0), (by_core, width, 0, 0), (by_x, width, 0, 0), (by_x, width, local, 0)]
    branch, h_own = own_call(
        attn_body,
        "attn_out",
        heads_in + [(tokens, D, 0, 0)],
        [one],
        out_parts,
        [(local, D, F32), (local, D, BF16)],
        0,
        2 * local * D * D,
    )

    chunks = range(local // BLOCK)
    h_far = [swap(h_own[c * BLOCK : (c + 1) * BLOCK], "mp", 2) for c in chunks]
    *saved_own, sum_own = ffn_forward(h_own, weights, sup, sgate, F32)
    saved_far, sum_far, last = [], [], sum_own
    for c in chunks:
        *saved, last = ffn_forward(after(h_far[c], last), weights, sup, sgate, BF16)
        saved_far.append(saved)
        sum_far.append(swap(last, "mp", 2))
    done, gm_own, gm_far, by_two = (), [], [], 0.0
    for c in chunks:
        *done, gm, by = turn(c, after(sum_own, last), sum_far[c], branch, tokens, cotangent, one, two, done)
        gm_own.append(gm)
        gm_far.append(swap(gm, "mp", 2))
        by_two = by_two + by
    result, keep_two = done
    gu, gg, bu, bg, gh_own = ffn_backward(
        [after(gm_own[0], gm_far[0])] + gm_own[1:], weights, [saved_own], sup, sgate, F32
    )
    gm_next = [after(gm, gh_own) for gm in gm_far]
    gu_far, gg_far, bu_far, bg_far, gh_far = ffn_backward(gm_next, weights, saved_far, sup, sgate, BF16)
    gus, ggs, bu, bg = [gu, gu_far], [gg, gg_far], bu + bu_far, bg + bg_far
    gh_over = swap(gh_far, "mp", 2)
    grad_mlp = weight_grads(
        [h_own] + h_far,
        gm_own + gm_far,
        gus,
        ggs,
        [saved_own[1]] + [saved[1] for saved in saved_far],
        weights.shape,
    )
    grad_mlp, gh_over = lax.optimization_barrier((grad_mlp, gh_over))
    grad_mlp = lax.psum_scatter(
        grad_mlp.reshape(-1, part), ("dp", "mp"), scatter_dimension=0, tiled=True, axis_index_groups=chip_groups()
    ).astype(F32)
    grad_up, grad_gate, grad_down = jnp.split(grad_mlp, 3, axis=0)

    grad_attn, grad_x, att0, att1, att2, att3, by_one = own_call(
        attn_back_body,
        "attn_back_out",
        [(gh_own, D, 0, 0), (gh_over, D, 0, 0), (keep_two, D, 0, 0), (branch, D, 0, 0), (tokens, D, 0, 0)],
        [one],
        out_parts,
        [(local, D, BF16), (local, D, F32)] + [(local, width, BF16)] * 4,
        1,
        2 * local * D * D,
    )
    back_x = swap(jnp.concatenate([att2, att3]), "mp", 2)
    back_core = swap(jnp.concatenate([att1, back_x[local:]]), "mp", 1)
    g_att = jnp.concatenate([back_x[:local], back_core[local:], att0, back_core[:local]])
    outs = [dot(grad_attn, a[s : s + local], 0, 0) for a, _, s, _ in heads_in]
    core_out = swap(jnp.concatenate([outs[1], outs[3]], axis=1).astype(BF16), "mp", 1)
    core_out, g_att = lax.optimization_barrier((core_out, g_att))
    over_out = swap((outs[2] + core_out[:, width:].astype(F32)).astype(BF16), "mp", 2)
    out_sum = outs[0] + core_out[:, :width].astype(F32)
    grads, g_sqk = attend_back(
        meta, queries, qrot, attended, inverse_mass, g_att, keys, vals, krot, kpos_cols, cosine, sine, sqk, docs
    )
    if lax.axis_size("dp") == 8:
        both = jnp.stack([m, lax.axis_index("dp").astype(jnp.int32) & 1])
        half_sum, sent = attn_grads(both, x_first, x_second, grads, out_sum, over_out)
        half_sum = half_sum + swap(sent, "dp", 1).astype(F32)
    else:
        sent = dot(x_first, grads[: 2 * local], 0, 0) + dot(x_second, grads[2 * local :], 0, 0)
        half_sum = jnp.concatenate([sent, out_sum + over_out.astype(F32)], axis=1)
    mlp_squares = jnp.sum(grad_mlp * grad_mlp)
    second_tokens = to_tokens(after(grads, sent), 1, attn, BF16)
    to_core = swap(second_tokens, "mp", 1)
    partial = to_tokens(after(grads, second_tokens), 0, attn, F32)
    for_x = (partial[local:] + to_core[local:].astype(F32)).astype(BF16)
    to_x = swap(for_x, "mp", 2)

    def placed(array, index):
        slots = lax.broadcasted_iota(jnp.int32, (4, 1), 0)
        return jnp.where(slots == index, array[None], 0.0)

    def quarters(by):
        return placed(by[0, 0], m & 2) + placed(by[1, 0], (m & 2) + 1)

    bu, bg, g_sqk, by_one, by_two, _ = lax.optimization_barrier((bu, bg, g_sqk, by_one, by_two, second_tokens))
    rows = [quarters(bu), quarters(bg), placed(g_sqk[0], m), by_one[0], by_two[0]]
    rows = [row.reshape(devices, -1) for row in rows]
    small = jnp.sum(to_all(after(jnp.concatenate(rows, axis=1), for_x)), axis=0)
    cuts, start = [], 0
    for row in rows:
        cuts.append(small[start : start + row.shape[1]])
        start += row.shape[1]
    g_sup, g_sgate, g_sqk, g_alpha_one, g_alpha_two = cuts

    def squared(*arrays):
        return sum(jnp.sum(array * array) for array in arrays)

    grad_attn = scatter_z(after(half_sum, for_x))
    squares = mlp_squares + squared(grad_attn, small)
    g_qkv = [grad_attn[:, i * width : (i + 1) * width] for i in range(3)]
    grad_down, grad_out = turned(after(grad_down, squares)), turned(after(grad_attn, squares)[:, 3 * width :])
    to_x = after(to_x, squares)
    grad_tokens = grad_x + partial[:local] + to_core[:local].astype(F32) + to_x.astype(F32)
    pieces = tuple(g_qkv) + (grad_out, grad_up, grad_gate, grad_down)
    pieces = pieces + (g_sqk, g_sup, g_sgate, g_alpha_one, g_alpha_two)
    squares = jnp.sum(to_all(jnp.broadcast_to(squares, (devices, 128))), axis=0)
    grad_norm = jnp.sqrt(squares[0])
    mean_alphas = jnp.stack([jnp.mean(alpha_one), jnp.mean(alpha_two)])
    return (result, grad_tokens) + pieces + (grad_norm, mean_alphas)


def solution(mesh):
    both_axes = P(("dp", "mp"))
    rows = P(("dp", "mp"), None)
    in_specs = (
        (rows, rows, P("dp", None), P("dp", None))
        + (P("dp", "mp"),) * 3
        + (P("mp", "dp"),)
        + (P("dp", "mp"),) * 2
        + (P("mp", "dp"),)
        + (both_axes,) * 5
    )
    out_specs = (
        (rows, rows)
        + (P("dp", "mp"),) * 3
        + (P("mp", "dp"),)
        + (P("dp", "mp"),) * 2
        + (P("mp", "dp"),)
        + (both_axes,) * 5
        + (P(), P())
    )
    return jax.shard_map(shards, mesh=mesh, in_specs=in_specs, out_specs=out_specs, check_vma=False)
```

```python
import functools

import jax
import jax.numpy as jnp
from jax import lax
from jax.experimental import pallas as pl
from jax.experimental.layout import Layout, with_layout_constraint
from jax.experimental.pallas import tpu as pltpu
from jax.sharding import PartitionSpec as P

D = 1024
HEADS = 16
HEAD = D // HEADS
EPS = 1e-06
NEG = -1e30
BLOCK = 256
F32 = jnp.float32
BF16 = jnp.bfloat16


def mean_rows(tensor):
    return jnp.mean(tensor, axis=-1, keepdims=True)


def normed(tensor):
    factor = lax.rsqrt(mean_rows(tensor * tensor) + EPS)
    return tensor * factor, factor


def normed_back(incoming, unit, factor):
    return factor * (incoming - unit * mean_rows(incoming * unit))


def dot(left, right, left_dim=1, right_dim=0):
    return lax.dot_general(
        left, right, (((left_dim,), (right_dim,)), ((), ())), preferred_element_type=F32
    )


RING = (0, 2, 4, 6, 7, 5, 3, 1)


def swap(array, axis, bit):
    size = lax.axis_size(axis)
    return lax.ppermute(array, axis, [(i, i ^ bit) for i in range(size)])


def to_z(array, step):
    return lax.ppermute(
        array, "dp", [(z * 2 + y, ((z + step) % 4) * 2 + y) for z in range(4) for y in range(2)]
    )


def around(array, step):
    return lax.ppermute(array, "dp", [(RING[p], RING[(p + step) % 8]) for p in range(8)])


def after(array, *others):
    if not others:
        return array
    return lax.optimization_barrier((array,) + others)[0]


def gather(shard, before):
    if lax.axis_size("dp") != 8:
        full = lax.all_gather(shard, "dp", axis=0, tiled=True)
        return full, [(full,)] * 4
    d = lax.axis_index("dp")
    rows, width = shard.shape
    place = jnp.where((d & 1) == 0, d >> 1, 7 - (d >> 1))

    def put(full, part, step):
        q = (place + step) & 7
        index = jnp.where(q < 4, 2 * q, 2 * (7 - q) + 1)
        return lax.dynamic_update_slice(full, part, (index * rows, jnp.int32(0)))

    full = put(jnp.zeros((8 * rows, width), shard.dtype), shard, 0)
    ahead, behind, arrived = shard, shard, []
    for step in (1, 2, 3, 4):
        if step > 1:
            ahead, behind = lax.optimization_barrier((ahead, behind) + tuple(before[step - 1]))[:2]
        ahead = around(ahead, 1)
        full = put(full, ahead, -step)
        if step < 4:
            behind = around(behind, -1)
            full = put(full, behind, step)
        arrived.append((ahead, behind))
    return full, arrived


def chip_groups():
    return [
        [d * 4 + 2 * x + core for d in range(lax.axis_size("dp")) for core in range(2)]
        for x in range(2)
    ]


def scatter_z(half):
    if lax.axis_size("dp") != 8:
        return lax.psum_scatter(half.astype(F32), "dp", scatter_dimension=0, tiled=True)
    z = lax.axis_index("dp") >> 1
    total = lax.dynamic_index_in_dim(half, z, axis=0, keepdims=False)
    for step in (1, 2, 3):
        part = lax.dynamic_index_in_dim(half, (z + step) & 3, axis=0, keepdims=False)
        total = total + to_z(part.astype(BF16), step).astype(F32)
    return total


def turned(array):
    return with_layout_constraint(array, Layout(major_to_minor=(0, 1))).T


def to_all(rows):
    return lax.all_to_all(rows, ("dp", "mp"), 0, 0, tiled=True)


def rotate_half(tensor):
    width = tensor.shape[-1]
    lane = lax.broadcasted_iota(jnp.int32, tensor.shape, 1)
    ahead = pltpu.roll(tensor, width - HEAD // 2, 1)
    behind = pltpu.roll(tensor, HEAD // 2, 1)
    return jnp.where((lane & (HEAD - 1)) < HEAD // 2, -ahead, behind)


def head_mean(tensor):
    width = tensor.shape[-1]
    row = lax.broadcasted_iota(jnp.int32, (width, width), 0) // HEAD
    col = lax.broadcasted_iota(jnp.int32, (width, width), 1) // HEAD
    ones = jnp.where(row == col, 1.0 / HEAD, 0.0).astype(BF16)
    high = tensor.astype(BF16)
    rest = (tensor - high.astype(F32)).astype(BF16)
    return dot(high, ones) + dot(rest, ones)


def wide(table):
    return jnp.concatenate([table, table], axis=1)


def project_body(m_ref, x_ref, w_ref, cos_ref, sin_ref, sqk_ref, *refs):
    q_ref, k_ref, v_ref, qr_ref, kr_ref = refs[-5:]
    rows = x_ref[...]
    cosine, sine = wide(cos_ref[...]), wide(sin_ref[...])
    scale = sqk_ref[0:1, :]
    width = q_ref.shape[1]
    raws = [dot(rows, w_ref[:, i * width : (i + 1) * width]) for i in range(3)]
    v_ref[...] = raws[2].astype(BF16)
    for raw, out_ref, rot_ref in ((raws[0], q_ref, qr_ref), (raws[1], k_ref, kr_ref)):
        turned = raw * cosine + rotate_half(raw) * sine
        rot_ref[...] = turned
        unit = turned * lax.rsqrt(head_mean(turned * turned) + EPS)
        out_ref[...] = (unit * scale).astype(BF16)


def project(place, x_rows, weight, cosine, sine, sqk, previous, first):
    rows, width = x_rows.shape[0], weight.shape[1] // 4
    total = cosine.shape[0]
    per = total // 4 // BLOCK

    def row_block(i, m):
        return ((m[0] ^ (first + 2 * (i // per))) * per + i % per, 0)

    any_spec = pl.BlockSpec(memory_space=pl.ANY)
    table = pl.BlockSpec((BLOCK, cosine.shape[1]), row_block)
    out = pl.BlockSpec((BLOCK, width), row_block)
    shapes = [jax.ShapeDtypeStruct((total, width), t) for t in (BF16, BF16, BF16, F32, F32)]
    extra = list(previous) if previous is not None else []
    return pl.pallas_call(
        project_body,
        out_shape=shapes,
        grid_spec=pltpu.PrefetchScalarGridSpec(
            num_scalar_prefetch=1,
            grid=(rows // BLOCK,),
            in_specs=[
                pl.BlockSpec((BLOCK, x_rows.shape[1]), lambda i, m: (i, 0)),
                pl.BlockSpec((x_rows.shape[1], 3 * width), lambda i, m: (0, 0)),
                table,
                table,
                pl.BlockSpec((1, width), lambda i, m: (0, 0)),
            ]
            + [any_spec] * len(extra),
            out_specs=[out] * 5,
        ),
        input_output_aliases={6 + i: i for i in range(len(extra))},
        cost_estimate=pl.CostEstimate(
            flops=6 * rows * D * width, bytes_accessed=8 * rows * D, transcendentals=rows
        ),
        name="project",
    )(place, x_rows, weight, cosine, sine, sqk, *extra)


def head_lanes(array, head):
    lane = lax.broadcasted_iota(jnp.int32, array.shape, 1)
    return jnp.where(lane // HEAD == head, array, jnp.zeros_like(array))


def stack_heads(array):
    heads = array.shape[1] // HEAD
    return jnp.concatenate([head_lanes(array, h) for h in range(heads)], axis=0)


def doc_start(meta_ref, docs, slots):
    start = jnp.zeros_like(slots)
    end = 0
    for i in range(docs):
        length = meta_ref[1 + i]
        end = end + length
        start = start + jnp.where(slots >= end, length, 0)
    return start


def slot_place(rel):
    return (rel >> 1) + 2 * (rel & 1)


def block_at(block):
    return pl.ds(pl.multiple_of(block * BLOCK, BLOCK), BLOCK)


def split_heads(source_ref, split_ref):
    def one(block, carry):
        split_ref[block] = stack_heads(source_ref[block_at(block), :])
        return carry

    lax.fori_loop(0, source_ref.shape[0] // BLOCK, one, 0)


def attend_body(docs, first, meta_ref, q_ref, k_ref, v_ref, kpos_ref, *refs):
    o_ref, inv_ref, acc_ref, sum_ref, vs_ref = refs[-5:]
    per = k_ref.shape[0] // 4 // BLOCK
    index = pl.program_id(0)
    step = ((first + index // per) ^ meta_ref[0]) * per + index % per
    heads = q_ref.shape[1] // HEAD
    base = step * BLOCK
    low = doc_start(meta_ref, docs, base) // BLOCK

    @pl.when(index == 0)
    def _():
        split_heads(v_ref, vs_ref)

    scaled = q_ref[...] * jnp.bfloat16(HEAD**-0.5)
    queries = [head_lanes(scaled, h) for h in range(heads)]
    rows = lax.broadcasted_iota(jnp.int32, (BLOCK, BLOCK), 0) + base
    starts = doc_start(meta_ref, docs, rows)
    acc_ref[...] = jnp.zeros_like(acc_ref)
    sum_ref[...] = jnp.zeros_like(sum_ref)

    def visit(blocks, allowed):
        expos = []
        sums = [0.0] * heads
        for block, mask in zip(blocks, allowed):
            keys = k_ref[block_at(block), :]
            bias = jnp.where(mask, 0.0, NEG)
            for h in range(heads):
                expo = jnp.exp(dot(queries[h], keys, 1, 1) + bias)
                sums[h] = sums[h] + expo[:, :128] + expo[:, 128:]
                expos.append(expo.astype(BF16))
        for h in range(heads):
            sum_ref[h * BLOCK : (h + 1) * BLOCK, :] += sums[h]
        vals = jnp.concatenate([vs_ref[block] for block in blocks], axis=0)
        acc_ref[...] += dot(jnp.concatenate(expos, axis=1), vals)

    def one(block, carry):
        cols = lax.broadcasted_iota(jnp.int32, (BLOCK, BLOCK), 1) + block * BLOCK
        same = kpos_ref[0:1, block_at(block)] >= starts
        visit([block], [(same & (cols <= rows)) | (cols == rows)])
        return carry

    lax.fori_loop(low, step + 1, one, 0)
    lane = lax.broadcasted_iota(jnp.int32, (BLOCK, q_ref.shape[1]), 1) // HEAD
    inverse = jnp.zeros((BLOCK, q_ref.shape[1]), F32)
    for h in range(heads):
        mass = jnp.sum(sum_ref[h * BLOCK : (h + 1) * BLOCK, :], axis=1, keepdims=True)
        inverse = jnp.where(lane == h, 1.0 / mass, inverse)
    inv_ref[...] = inverse
    o_ref[...] = (acc_ref[...] * inverse).astype(BF16)


def attend(meta, queries, keys, vals, kpos, docs, first, previous):
    total, width = queries.shape
    per = total // 4 // BLOCK
    heads = width // HEAD
    whole = pl.BlockSpec((total, width), lambda i, m: (0, 0))

    def natural(i, m):
        return (((first + i // per) ^ m[0]) * per + i % per, 0)

    block = pl.BlockSpec((BLOCK, width), natural)
    out = pl.BlockSpec((BLOCK, width), lambda i, m: ((first ^ 2) * per + i, 0))
    extra = list(previous)
    return pl.pallas_call(
        functools.partial(attend_body, docs, first),
        out_shape=[
            jax.ShapeDtypeStruct((total, width), BF16),
            jax.ShapeDtypeStruct((total, width), F32),
        ],
        grid_spec=pltpu.PrefetchScalarGridSpec(
            num_scalar_prefetch=1,
            grid=(2 * per,),
            in_specs=[block, whole, whole, pl.BlockSpec((1, total), lambda i, m: (0, 0))]
            + [pl.BlockSpec(memory_space=pl.ANY)] * len(extra),
            out_specs=[out, block],
            scratch_shapes=[
                pltpu.VMEM((BLOCK, width), F32),
                pltpu.VMEM((heads * BLOCK, 128), F32),
                pltpu.VMEM((total // BLOCK, heads * BLOCK, width), BF16),
            ],
        ),
        input_output_aliases={5 + i: i for i in range(len(extra))},
        cost_estimate=pl.CostEstimate(
            flops=8_000_000_000, bytes_accessed=8 * total * width, transcendentals=3_000_000
        ),
        name="attend",
    )(meta, queries, keys, vals, kpos, *extra)


def finish(grad, turned, cosine, sine, scale):
    factor = lax.rsqrt(head_mean(turned * turned) + EPS)
    unit = turned * factor
    by_scale = jnp.sum(grad * unit, axis=0, keepdims=True)
    scaled = grad * scale
    back = factor * (scaled - unit * head_mean(scaled * unit))
    raw = back * cosine - rotate_half(back) * sine
    return raw.astype(BF16), by_scale


def back_body(
    docs,
    meta_ref,
    q_ref,
    qr_ref,
    o_ref,
    inv_ref,
    do_ref,
    k_ref,
    v_ref,
    kr_ref,
    kpos_ref,
    cos_ref,
    sin_ref,
    sqk_ref,
    g_ref,
    gs_ref,
    dq_ref,
    dk_ref,
    dv_ref,
    ks_ref,
):
    step = pl.program_id(0)
    width = q_ref.shape[1]
    heads = width // HEAD
    per = k_ref.shape[0] // 4 // BLOCK
    base = step * BLOCK
    low = doc_start(meta_ref, docs, base) // BLOCK

    @pl.when(step == 0)
    def _():
        dk_ref[...] = jnp.zeros_like(dk_ref)
        dv_ref[...] = jnp.zeros_like(dv_ref)
        gs_ref[...] = jnp.zeros_like(gs_ref)
        split_heads(k_ref, ks_ref)

    dq_ref[...] = jnp.zeros_like(dq_ref)
    scaled = q_ref[...] * jnp.bfloat16(HEAD**-0.5)
    queries = [head_lanes(scaled, h) for h in range(heads)]
    all_queries = jnp.concatenate(queries, axis=0)
    upward = do_ref[...].astype(F32) * inv_ref[...]
    ups = [head_lanes(upward.astype(BF16), h) for h in range(heads)]
    all_ups = jnp.concatenate(ups, axis=0)
    picks = lax.broadcasted_iota(jnp.int32, (8, width), 0)
    lanes = lax.broadcasted_iota(jnp.int32, (8, width), 1) // HEAD
    delta = lax.dot_general(
        jnp.where(picks == lanes, 1.0, 0.0).astype(F32),
        upward * o_ref[...].astype(F32),
        (((1,), (1,)), ((), ())),
        precision=lax.Precision.HIGHEST,
        preferred_element_type=F32,
    )
    cols = lax.broadcasted_iota(jnp.int32, (BLOCK, BLOCK), 1) + base
    starts = doc_start(meta_ref, docs, cols)

    def visit(block, count, allowed):
        rows_at = pl.ds(pl.multiple_of(block * BLOCK, BLOCK), count * BLOCK)
        keys, vals = k_ref[rows_at, :], v_ref[rows_at, :]
        bias = jnp.where(allowed, 0.0, NEG)
        expos, slopes = [], []
        for h in range(heads):
            expo = jnp.exp(dot(keys, queries[h], 1, 1) + bias)
            expos.append(expo.astype(BF16))
            slope = expo * (dot(vals, ups[h], 1, 1) - delta[h : h + 1, :])
            slopes.append(slope.astype(BF16))
        dv_ref[rows_at, :] += dot(jnp.concatenate(expos, axis=1), all_ups)
        dk_ref[rows_at, :] += dot(jnp.concatenate(slopes, axis=1), all_queries)
        pieces = [slope[i * BLOCK : (i + 1) * BLOCK] for i in range(count) for slope in slopes]
        split = jnp.concatenate([ks_ref[block + i] for i in range(count)], axis=0)
        dq_ref[...] += dot(jnp.concatenate(pieces, axis=0), split, 0, 0)

    pairs = (step - low) >> 1

    def pair(i, carry):
        block = low + 2 * i
        keys_at = pl.ds(pl.multiple_of(block * BLOCK, BLOCK), 2 * BLOCK)
        visit(block, 2, wide(kpos_ref[keys_at, :]) >= jnp.concatenate([starts, starts], axis=0))
        return carry

    def one(block, carry):
        rows = lax.broadcasted_iota(jnp.int32, (BLOCK, BLOCK), 0) + block * BLOCK
        same = wide(kpos_ref[block_at(block), :]) >= starts
        visit(block, 1, (same & (rows <= cols)) | (rows == cols))
        return carry

    lax.fori_loop(0, pairs, pair, 0)
    lax.fori_loop(low + 2 * pairs, step + 1, one, 0)

    scale = sqk_ref[0:1, :]
    here = pl.ds(pl.multiple_of(base, BLOCK), BLOCK)
    raw, by_scale = finish(
        dq_ref[...] * (HEAD**-0.5),
        qr_ref[...],
        wide(cos_ref[here, :]),
        wide(sin_ref[here, :]),
        scale,
    )
    slot = slot_place(meta_ref[0] ^ (step // per)) * per + step % per
    g_ref[pl.ds(pl.multiple_of(slot * BLOCK, BLOCK), BLOCK), :width] = raw
    gs_ref[0:1, :] += by_scale

    @pl.when(step == pl.num_programs(0) - 1)
    def _():
        def one(block, carry):
            at = pl.ds(pl.multiple_of(block * BLOCK, BLOCK), BLOCK)
            slot = slot_place(meta_ref[0] ^ (block // per)) * per + block % per
            to = pl.ds(pl.multiple_of(slot * BLOCK, BLOCK), BLOCK)
            raw, by_scale = finish(
                dk_ref[at, :], kr_ref[at, :], wide(cos_ref[at, :]), wide(sin_ref[at, :]), scale
            )
            g_ref[to, width : 2 * width] = raw
            gs_ref[0:1, :] += by_scale
            g_ref[to, 2 * width :] = dv_ref[at, :].astype(BF16)
            return carry

        lax.fori_loop(0, pl.num_programs(0), one, 0)


def attend_back(meta, queries, qrot, out, inverse, grad, keys, vals, krot, kpos, cosine, sine, sqk, docs):
    total, width = queries.shape
    per = total // 4 // BLOCK

    def rel(i, m):
        return ((m[0] ^ (i // per) ^ 2) * per + i % per, 0)

    whole = pl.BlockSpec((total, width), lambda i, m: (0, 0))
    half = pl.BlockSpec((total, 128), lambda i, m: (0, 0))
    block = pl.BlockSpec((BLOCK, width), lambda i, m: (i, 0))
    moved = pl.BlockSpec((BLOCK, width), rel)
    return pl.pallas_call(
        functools.partial(back_body, docs),
        out_shape=[
            jax.ShapeDtypeStruct((total, 3 * width), BF16),
            jax.ShapeDtypeStruct((8, width), F32),
        ],
        grid_spec=pltpu.PrefetchScalarGridSpec(
            num_scalar_prefetch=1,
            grid=(total // BLOCK,),
            in_specs=[block, block, moved, block, moved, whole, whole, whole, half, half, half]
            + [pl.BlockSpec((1, width), lambda i, m: (0, 0))],
            out_specs=[
                pl.BlockSpec((total, 3 * width), lambda i, m: (0, 0)),
                pl.BlockSpec((8, width), lambda i, m: (0, 0)),
            ],
            scratch_shapes=[
                pltpu.VMEM((BLOCK, width), F32),
                pltpu.VMEM((total, width), F32),
                pltpu.VMEM((total, width), F32),
                pltpu.VMEM((total // BLOCK, width // HEAD * BLOCK, width), BF16),
            ],
        ),
        cost_estimate=pl.CostEstimate(
            flops=40_000_000_000, bytes_accessed=12 * total * width, transcendentals=6_000_000
        ),
        name="attend_back",
    )(meta, queries, qrot, out, inverse, grad, keys, vals, krot, kpos, cosine, sine, sqk)


TILE = 256


def weight_tile(weight_ref, part, index):
    return weight_ref[:, part, index].reshape(D, TILE)


def weight_spec(weights):
    return pl.BlockSpec(weights.shape[:4] + (TILE,), lambda t: (0, 0, 0, 0, t))


def forward_body(
    h_ref, w_ref, sup_ref, sgate_ref, gate_ref, act_ref, by_up_ref, by_gate_ref, out_ref, acc_ref
):
    t = pl.program_id(0)
    rows = h_ref[...]
    acts = []
    for part in range(2):
        sup, sgate = sup_ref[part, 0:1, :], sgate_ref[part, 0:1, :]
        scaled = sup * dot(rows, weight_tile(w_ref, part, 0))
        gate_proj = dot(rows, weight_tile(w_ref, part, 1))
        outer = sgate * gate_proj
        sigma = jax.nn.sigmoid(outer)
        silu = outer * sigma
        acts.append((scaled * silu).astype(BF16))
        gate_ref[part] = gate_proj.astype(BF16)
        act_ref[part] = acts[part]
        by_up_ref[part] = (sup * silu).astype(BF16)
        by_gate_ref[part] = ((sgate * scaled) * (sigma + silu * (1.0 - sigma))).astype(BF16)
    total = dot(
        jnp.concatenate(acts, axis=1),
        jnp.concatenate([weight_tile(w_ref, part, 2) for part in range(2)], axis=1),
        1,
        1,
    )
    add_up(t, total, acc_ref, out_ref)


def add_up(t, total, acc_ref, out_ref):
    @pl.when(t == 0)
    def _():
        acc_ref[...] = total

    @pl.when((t > 0) & (t < pl.num_programs(0) - 1))
    def _():
        acc_ref[...] += total

    @pl.when(t == pl.num_programs(0) - 1)
    def _():
        out_ref[...] = (acc_ref[...] + total).astype(out_ref.dtype)


def ffn_specs(count):
    whole = pl.BlockSpec((count, D), lambda t: (0, 0))
    tile = pl.BlockSpec((2, count, TILE), lambda t: (0, 0, t))
    scale = pl.BlockSpec((2, 1, TILE), lambda t: (0, 0, t))
    return whole, tile, scale


def ffn_forward(rows, weights, sup, sgate, kind):
    count, hidden = rows.shape[0], sup.shape[2]
    whole, tile, scale = ffn_specs(count)
    return pl.pallas_call(
        forward_body,
        out_shape=[jax.ShapeDtypeStruct((2, count, hidden), BF16)] * 4
        + [jax.ShapeDtypeStruct((count, D), kind)],
        grid=(hidden // TILE,),
        in_specs=[whole, weight_spec(weights), scale, scale],
        out_specs=[tile] * 4 + [whole],
        scratch_shapes=[pltpu.VMEM((count, D), F32)],
        cost_estimate=pl.CostEstimate(
            flops=12 * count * D * hidden,
            bytes_accessed=12 * D * hidden + 12 * count * hidden,
            transcendentals=2 * count * hidden,
        ),
        name="ffn_forward",
    )(rows, weights, sup, sgate)


def backward_body(pieces, groups, *refs):
    rows = jnp.concatenate([ref[...] for ref in refs[:pieces]], axis=0)
    w_ref, kept = refs[pieces], refs[pieces + 1 : pieces + 1 + 4 * groups]
    sup_ref, sgate_ref, gu_ref, gg_ref, bu_ref, bg_ref, out_ref, acc_ref = refs[pieces + 1 + 4 * groups :]
    t = pl.program_id(0)

    def saved(index, part):
        return jnp.concatenate([kept[4 * g + index][part] for g in range(groups)], axis=0).astype(F32)

    lefts, rights = [], []
    for part in range(2):
        g_act = dot(rows, weight_tile(w_ref, part, 2))
        g_up = (g_act * saved(2, part)).astype(BF16)
        g_gate = g_act * saved(3, part)
        up_sum = jnp.sum(g_act * saved(1, part), axis=0, keepdims=True)
        gate_sum = jnp.sum(g_gate * saved(0, part), axis=0, keepdims=True)
        g_gate = g_gate.astype(BF16)
        bu_ref[part, 0:1, :] = up_sum / sup_ref[part, 0:1, :]
        bg_ref[part, 0:1, :] = gate_sum / sgate_ref[part, 0:1, :]
        gu_ref[part] = g_up
        gg_ref[part] = g_gate
        lefts += [g_up, g_gate]
        rights += [weight_tile(w_ref, part, 0), weight_tile(w_ref, part, 1)]
    total = dot(jnp.concatenate(lefts, axis=1), jnp.concatenate(rights, axis=1), 1, 1)
    add_up(t, total, acc_ref, out_ref)


def ffn_backward(grads, weights, saved, sup, sgate, kind):
    count, hidden = sum(g.shape[0] for g in grads), sup.shape[2]
    whole, tile, scale = ffn_specs(count)
    sums = pl.BlockSpec((2, 8, TILE), lambda t: (0, 0, t))
    return pl.pallas_call(
        functools.partial(backward_body, len(grads), len(saved)),
        out_shape=[jax.ShapeDtypeStruct((2, count, hidden), BF16)] * 2
        + [jax.ShapeDtypeStruct((2, 8, hidden), F32)] * 2
        + [jax.ShapeDtypeStruct((count, D), kind)],
        grid=(hidden // TILE,),
        in_specs=[pl.BlockSpec(g.shape, lambda t: (0, 0)) for g in grads]
        + [weight_spec(weights)]
        + [pl.BlockSpec((2, k.shape[1], TILE), lambda t: (0, 0, t)) for group in saved for k in group]
        + [scale, scale],
        out_specs=[tile, tile, sums, sums, whole],
        scratch_shapes=[pltpu.VMEM((count, D), F32)],
        cost_estimate=pl.CostEstimate(
            flops=12 * count * D * hidden,
            bytes_accessed=12 * D * hidden + 24 * count * hidden,
            transcendentals=0,
        ),
        name="ffn_backward",
    )(*grads, weights, *[k for group in saved for k in group], sup, sgate)


def weight_body(counts, *refs):
    h_count, m_count, g_count, a_count = counts
    take = iter(refs)
    hs = [next(take) for _ in range(h_count)]
    ms = [next(take) for _ in range(m_count)]
    ups, gates, acts = [[next(take) for _ in range(n)] for n in (g_count, g_count, a_count)]
    out_ref, ht_ref, mt_ref = refs[-3:]

    @pl.when(pl.program_id(0) == 0)
    def _():
        for pieces, to_ref in ((hs, ht_ref), (ms, mt_ref)):
            start = 0
            for ref in pieces:
                to_ref[:, start : start + ref.shape[0]] = ref[...].T
                start += ref.shape[0]

    for index, (left_ref, rights) in enumerate(((ht_ref, ups), (ht_ref, gates), (mt_ref, acts))):
        for part in range(2):
            right = jnp.concatenate([ref[part] for ref in rights], axis=0)
            total = dot(left_ref[...], right).astype(BF16)
            out_ref[:, part, index] = total.reshape(out_ref.shape[0], out_ref.shape[3], TILE)


def weight_grads(hs, ms, ups, gates, acts, shape):
    hidden = ups[0].shape[2]
    count = sum(h.shape[0] for h in hs)

    def whole(array):
        return pl.BlockSpec(array.shape, lambda t: (0, 0))

    def tile(array):
        return pl.BlockSpec((2, array.shape[1], TILE), lambda t: (0, 0, t))

    lefts, rights = list(hs) + list(ms), list(ups) + list(gates) + list(acts)
    return pl.pallas_call(
        functools.partial(weight_body, (len(hs), len(ms), len(ups), len(acts))),
        out_shape=jax.ShapeDtypeStruct(shape, BF16),
        grid=(hidden // TILE,),
        in_specs=[whole(a) for a in lefts] + [tile(a) for a in rights],
        out_specs=pl.BlockSpec(shape[:4] + (TILE,), lambda t: (0, 0, 0, 0, t)),
        scratch_shapes=[pltpu.VMEM((D, count), BF16)] * 2,
        cost_estimate=pl.CostEstimate(
            flops=12 * count * D * hidden,
            bytes_accessed=12 * D * hidden + 12 * count * hidden,
            transcendentals=0,
        ),
        name="weight_grads",
    )(*lefts, *rights)


def attn_grad_body(m_ref, xf_ref, xs_ref, g_ref, out_ref, over_ref, mine_ref, sent_ref, xt_ref, sum_ref):
    t = pl.program_id(0)
    rows = xf_ref.shape[0]
    y = m_ref[1]

    @pl.when(t == 0)
    def _():
        def one(block, carry):
            for start, ref in ((0, xf_ref), (rows, xs_ref)):
                at = pl.ds(pl.multiple_of(start + block * BLOCK, BLOCK), BLOCK)
                xt_ref[:, at] = ref[block_at(block), :].T
            return carry

        lax.fori_loop(0, rows // BLOCK, one, 0)

    @pl.when(t < 3)
    def _():
        sum_ref[...] = dot(xt_ref[...], g_ref[...]).reshape(sum_ref.shape)

    @pl.when(t == 3)
    def _():
        sum_ref[...] = (out_ref[...] + over_ref[...].astype(F32)).reshape(sum_ref.shape)

    mine_ref[...] = sum_ref[:, y]
    sent_ref[...] = sum_ref[:, 1 - y].astype(BF16)


def attn_grads(place, x_first, x_second, grads, out_sum, over_out):
    width = out_sum.shape[1]
    rows = D // lax.axis_size("dp")

    def whole(array):
        return pl.BlockSpec(array.shape, lambda t, m: (0, 0))

    half = (D // rows // 2, rows, width)
    out = pl.BlockSpec(half, lambda t, m: (0, 0, t))
    return pl.pallas_call(
        attn_grad_body,
        out_shape=[
            jax.ShapeDtypeStruct(half[:2] + (4 * width,), F32),
            jax.ShapeDtypeStruct(half[:2] + (4 * width,), BF16),
        ],
        grid_spec=pltpu.PrefetchScalarGridSpec(
            num_scalar_prefetch=1,
            grid=(4,),
            in_specs=[
                whole(x_first),
                whole(x_second),
                pl.BlockSpec((grads.shape[0], width), lambda t, m: (0, jnp.minimum(t, 2))),
                whole(out_sum),
                whole(over_out),
            ],
            out_specs=[out, out],
            scratch_shapes=[
                pltpu.VMEM((D, grads.shape[0]), BF16),
                pltpu.VMEM((half[0], 2) + half[1:], F32),
            ],
        ),
        cost_estimate=pl.CostEstimate(
            flops=2 * D * grads.size, bytes_accessed=4 * grads.size, transcendentals=0
        ),
        name="attn_grads",
    )(place, x_first, x_second, grads, out_sum, over_out)


def to_tokens(grads, half, weight, kind):
    rows, width = grads.shape[0] // 2, grads.shape[1]
    step = rows // 2
    row = weight.shape[0]

    def body(g_ref, w_ref, out_ref):
        out_ref[...] = dot(g_ref[...], w_ref[...], 1, 1).astype(kind)

    return pl.pallas_call(
        body,
        out_shape=jax.ShapeDtypeStruct((rows, row), kind),
        grid=(2,),
        in_specs=[
            pl.BlockSpec((step, width), lambda i: (2 * half + i, 0)),
            pl.BlockSpec((row, width), lambda i: (0, 0)),
        ],
        out_specs=pl.BlockSpec((step, row), lambda i: (i, 0)),
        cost_estimate=pl.CostEstimate(
            flops=2 * rows * width * row, bytes_accessed=6 * rows * row, transcendentals=0
        ),
        name="to_tokens",
    )(grads, weight)


def own_call(body, name, rows_in, vectors, wholes, outs, sums, flops):
    count = outs[0][0]
    blocks = count // BLOCK

    def rows_spec(width, skip, column):
        return pl.BlockSpec((BLOCK, width), lambda i: (skip // BLOCK + i, column))

    in_specs = [rows_spec(w, s, c) for _, w, s, c in rows_in]
    in_specs += [pl.BlockSpec((1, v.shape[1]), lambda i: (0, 0)) for v in vectors]
    in_specs += [pl.BlockSpec((D, w), lambda i, c=c: (0, c)) for _, w, c in wholes]
    shapes = [jax.ShapeDtypeStruct((count, w), t) for count, w, t in outs]
    shapes += [jax.ShapeDtypeStruct((8, D), F32)] * sums
    out_specs = [pl.BlockSpec((BLOCK, w), lambda i: (i, 0)) for _, w, _ in outs]
    out_specs += [pl.BlockSpec((8, D), lambda i: (0, 0))] * sums
    return pl.pallas_call(
        body,
        out_shape=shapes,
        grid=(blocks,),
        in_specs=in_specs,
        out_specs=out_specs,
        cost_estimate=pl.CostEstimate(
            flops=flops, bytes_accessed=20 * count * D, transcendentals=count
        ),
        name=name,
    )(*[a for a, *_ in rows_in], *vectors, *[a for a, *_ in wholes])


def first_update(branch, x_rows, alpha):
    h_attn, attn_factor = normed(branch)
    hidden, one_factor = normed(x_rows + alpha * (h_attn - x_rows))
    return h_attn, attn_factor, hidden, one_factor


def attn_body(a0, a1, a2, a3, x_ref, alpha_ref, w0, w1, w2, w3, branch_ref, low_ref):
    branch = dot(a0[...], w0[...], 1, 1) + dot(a1[...], w1[...], 1, 1)
    branch = branch + dot(a2[...], w2[...], 1, 1) + dot(a3[...], w3[...], 1, 1)
    branch_ref[...] = branch
    hidden = first_update(branch, x_ref[...].astype(F32), alpha_ref[0:1, :])[2]
    low_ref[...] = hidden.astype(BF16)


def turn_body(own_ref, far_ref, branch_ref, x_ref, cot_ref, one_ref, two_ref, *refs):
    out_ref, keep_ref, gm_ref, sum_ref = refs[-4:]
    hidden = first_update(branch_ref[...], x_ref[...].astype(F32), one_ref[0:1, :])[2]
    alpha = two_ref[0:1, :]
    h_mlp, mlp_factor = normed(own_ref[...] + far_ref[...].astype(F32))
    step = h_mlp - hidden
    result, two_factor = normed(hidden + alpha * step)
    out_ref[...] = result.astype(BF16)
    grad_two = normed_back(cot_ref[...].astype(F32), result, two_factor)
    keep_ref[...] = grad_two * (1.0 - alpha)
    gm_ref[...] = normed_back(grad_two * alpha, h_mlp, mlp_factor).astype(BF16)

    @pl.when(pl.program_id(0) == 0)
    def _():
        sum_ref[...] = jnp.zeros_like(sum_ref)

    sum_ref[0:1, :] += jnp.sum(grad_two * step, axis=0, keepdims=True)


def turn(chunk, own, far, branch, x_rows, cotangent, one, two, previous):
    count = branch.shape[0]
    rows = pl.BlockSpec((BLOCK // 2, D), lambda i: (2 * chunk + i, 0))
    first = pl.BlockSpec((BLOCK // 2, D), lambda i: (i, 0))
    vector = pl.BlockSpec((1, D), lambda i: (0, 0))
    total = pl.BlockSpec((8, D), lambda i: (0, 0))
    extra = list(previous)
    return pl.pallas_call(
        turn_body,
        out_shape=[
            jax.ShapeDtypeStruct((count, D), BF16),
            jax.ShapeDtypeStruct((count, D), F32),
            jax.ShapeDtypeStruct((BLOCK, D), BF16),
            jax.ShapeDtypeStruct((8, D), F32),
        ],
        grid=(2,),
        in_specs=[rows, first, rows, rows, rows, vector, vector]
        + [pl.BlockSpec(memory_space=pl.ANY)] * len(extra),
        out_specs=[rows, rows, first, total],
        input_output_aliases={7 + i: i for i in range(len(extra))},
        cost_estimate=pl.CostEstimate(
            flops=60 * BLOCK * D, bytes_accessed=20 * BLOCK * D, transcendentals=BLOCK
        ),
        name="turn",
    )(own, far, branch, x_rows, cotangent, one, two, *extra)


def attn_back_body(
    own_ref, far_ref, keep_ref, branch_ref, x_ref, one_ref, w0, w1, w2, w3, ga_ref, gt_ref, o0, o1, o2, o3, sum_ref
):
    x_rows, alpha = x_ref[...].astype(F32), one_ref[0:1, :]
    h_attn, attn_factor, hidden, one_factor = first_update(branch_ref[...], x_rows, alpha)
    incoming = keep_ref[...] + own_ref[...] + far_ref[...].astype(F32)
    grad_one = normed_back(incoming, hidden, one_factor)
    gt_ref[...] = grad_one * (1.0 - alpha)
    grad_attn = normed_back(grad_one * alpha, h_attn, attn_factor).astype(BF16)
    ga_ref[...] = grad_attn
    for weight_ref, out_ref in ((w0, o0), (w1, o1), (w2, o2), (w3, o3)):
        out_ref[...] = dot(grad_attn, weight_ref[...]).astype(BF16)

    @pl.when(pl.program_id(0) == 0)
    def _():
        sum_ref[...] = jnp.zeros_like(sum_ref)

    sum_ref[0:1, :] += jnp.sum(grad_one * (h_attn - x_rows), axis=0, keepdims=True)


def shards(
    tokens,
    cotangent,
    lengths,
    key_mask,
    w_query,
    w_key,
    w_value,
    w_out,
    w_up,
    w_gate,
    w_down,
    s_qk,
    s_up,
    s_gate,
    alpha_attn,
    alpha_mlp,
):
    m = lax.axis_index("mp").astype(jnp.int32)
    devices = lax.axis_size("dp") * lax.axis_size("mp")
    local = tokens.shape[0]
    row_len = key_mask.shape[1]
    docs = lengths.shape[1]
    part = w_up.shape[1]
    width = w_query.shape[1]

    place = m.reshape(1)
    meta = jnp.concatenate([place, lengths[0]])
    slot_ids = jnp.arange(row_len, dtype=jnp.int32)
    steps_even = jnp.arange(0, HEAD, 2).astype(F32)
    frequencies = jnp.power(jnp.float32(10000.0), -steps_even / HEAD)
    frequencies = jnp.tile(frequencies, 4)[None, :]

    def turn_by(steps):
        angles = steps.astype(F32)[:, None] * frequencies
        return jnp.cos(angles), jnp.sin(angles)

    coarse_cos, coarse_sin = (t[:, None] for t in turn_by(jnp.arange(0, row_len, 64)))
    fine_cos, fine_sin = (t[None] for t in turn_by(jnp.arange(64)))
    slot_cos = (coarse_cos * fine_cos - coarse_sin * fine_sin).reshape(row_len, -1)
    slot_sin = (coarse_sin * fine_cos + coarse_cos * fine_sin).reshape(row_len, -1)
    first_slots = jnp.cumsum(lengths[0]) - lengths[0]
    doc_cos, doc_sin = turn_by(first_slots)
    start_cos, start_sin = doc_cos[0:1], doc_sin[0:1]
    for i in range(1, docs):
        later = (slot_ids >= first_slots[i])[:, None]
        start_cos = jnp.where(later, doc_cos[i : i + 1], start_cos)
        start_sin = jnp.where(later, doc_sin[i : i + 1], start_sin)
    cosine = slot_cos * start_cos + slot_sin * start_sin
    sine = slot_sin * start_cos - slot_cos * start_sin
    x_halves = [swap(tokens[i * local // 2 : (i + 1) * local // 2], "mp", 2) for i in range(2)]
    vector = jnp.concatenate([s_up, s_gate, s_qk, alpha_attn, alpha_mlp])[None]
    every = to_all(jnp.broadcast_to(vector, (devices, vector.shape[1])))
    attn, arrived = gather(
        jnp.concatenate([w_query, w_key, w_value, w_out.T], axis=1),
        [(), (), (), (x_halves[0], x_halves[1], every)],
    )
    x_first = jnp.concatenate([tokens, x_halves[0], after(x_halves[1], *arrived[2])], axis=0)
    x_second = swap(x_first, "mp", 1)
    shard = jnp.concatenate([w_up, w_gate, w_down.T], axis=0)
    shard = with_layout_constraint(after(shard, *arrived[2]), Layout(major_to_minor=(0, 1)))
    weights = lax.all_gather(
        shard, ("dp", "mp"), axis=0, tiled=True, axis_index_groups=chip_groups()
    ).reshape(-1, 2, 3, shard.shape[0] // 3, part)
    cuts, start = [], 0
    for piece in (s_up, s_gate, s_qk, alpha_attn, alpha_mlp):
        cuts.append(every[:, start : start + piece.shape[0]].reshape(-1))
        start += piece.shape[0]
    sup_all, sgate_all, sqk_all, alpha_one, alpha_two = cuts

    def quarter(array, index):
        size = array.shape[0] // 4
        return lax.dynamic_slice_in_dim(array, index * size, size)

    def row(array):
        return array[None]

    sqk = row(quarter(sqk_all, m))
    low = m & 2
    sup = jnp.stack([row(quarter(sup_all, low)), row(quarter(sup_all, low + 1))])
    sgate = jnp.stack([row(quarter(sgate_all, low)), row(quarter(sgate_all, low + 1))])
    one, two = row(alpha_one), row(alpha_two)
    out_mine = attn[:, 3 * width :]
    out_core = swap(out_mine, "mp", 1)
    out_over = swap(out_mine, "mp", 2)
    out_cross = swap(out_over, "mp", 1)
    out_parts = [(w, width, 0) for w in (out_mine, out_core, out_over, out_cross)]

    kpos = jnp.where(key_mask[0] == 1, slot_ids, -1)
    kpos_rows = kpos[None, :]
    kpos_cols = jnp.broadcast_to(kpos[:, None], (row_len, 128))
    x_second, kpos_cols = lax.optimization_barrier((x_second, kpos_cols))

    half = project(place, x_first, attn, cosine, sine, sqk, None, 0)
    queries, keys, vals, qrot, krot = project(place, x_second, attn, cosine, sine, sqk, half, 1)
    half = attend(meta, queries, keys, vals, kpos_rows, docs, 2, ())
    far_core = swap(half[0][local : 2 * local], "mp", 1)
    for_x = jnp.concatenate([half[0][:local], far_core])
    by_x = swap(for_x, "mp", 2)
    half = [after(half[0], for_x), half[1]]
    attended, inverse_mass = attend(meta, queries, keys, vals, kpos_rows, docs, 0, half)
    by_core = swap(attended[3 * local :], "mp", 1)
    heads_in = [(attended, width, 2 * local, 0), (by_core, width, 0, 0), (by_x, width, 0, 0), (by_x, width, local, 0)]
    branch, h_own = own_call(
        attn_body,
        "attn_out",
        heads_in + [(tokens, D, 0, 0)],
        [one],
        out_parts,
        [(local, D, F32), (local, D, BF16)],
        0,
        2 * local * D * D,
    )

    chunks = range(local // BLOCK)
    h_far = [swap(h_own[c * BLOCK : (c + 1) * BLOCK], "mp", 2) for c in chunks]
    *saved_own, sum_own = ffn_forward(h_own, weights, sup, sgate, F32)
    saved_far, sum_far, last = [], [], sum_own
    for c in chunks:
        *saved, last = ffn_forward(after(h_far[c], last), weights, sup, sgate, BF16)
        saved_far.append(saved)
        sum_far.append(swap(last, "mp", 2))
    done, gm_own, gm_far, by_two = (), [], [], 0.0
    for c in chunks:
        *done, gm, by = turn(c, after(sum_own, last), sum_far[c], branch, tokens, cotangent, one, two, done)
        gm_own.append(gm)
        gm_far.append(swap(gm, "mp", 2))
        by_two = by_two + by
    result, keep_two = done
    gu, gg, bu, bg, gh_own = ffn_backward(
        [after(gm_own[0], gm_far[0])] + gm_own[1:], weights, [saved_own], sup, sgate, F32
    )
    gm_next = [after(gm, gh_own) for gm in gm_far]
    gu_far, gg_far, bu_far, bg_far, gh_far = ffn_backward(gm_next, weights, saved_far, sup, sgate, BF16)
    gus, ggs, bu, bg = [gu, gu_far], [gg, gg_far], bu + bu_far, bg + bg_far
    gh_over = swap(gh_far, "mp", 2)
    grad_mlp = weight_grads(
        [h_own] + h_far,
        gm_own + gm_far,
        gus,
        ggs,
        [saved_own[1]] + [saved[1] for saved in saved_far],
        weights.shape,
    )
    grad_mlp, gh_over = lax.optimization_barrier((grad_mlp, gh_over))
    grad_mlp = lax.psum_scatter(
        grad_mlp.reshape(-1, part), ("dp", "mp"), scatter_dimension=0, tiled=True, axis_index_groups=chip_groups()
    ).astype(F32)
    grad_up, grad_gate, grad_down = jnp.split(grad_mlp, 3, axis=0)

    grad_attn, grad_x, att0, att1, att2, att3, by_one = own_call(
        attn_back_body,
        "attn_back_out",
        [(gh_own, D, 0, 0), (gh_over, D, 0, 0), (keep_two, D, 0, 0), (branch, D, 0, 0), (tokens, D, 0, 0)],
        [one],
        out_parts,
        [(local, D, BF16), (local, D, F32)] + [(local, width, BF16)] * 4,
        1,
        2 * local * D * D,
    )
    back_x = swap(jnp.concatenate([att2, att3]), "mp", 2)
    back_core = swap(jnp.concatenate([att1, back_x[local:]]), "mp", 1)
    g_att = jnp.concatenate([back_x[:local], back_core[local:], att0, back_core[:local]])
    outs = [dot(grad_attn, a[s : s + local], 0, 0) for a, _, s, _ in heads_in]
    core_out = swap(jnp.concatenate([outs[1], outs[3]], axis=1).astype(BF16), "mp", 1)
    core_out, g_att = lax.optimization_barrier((core_out, g_att))
    over_out = swap((outs[2] + core_out[:, width:].astype(F32)).astype(BF16), "mp", 2)
    out_sum = outs[0] + core_out[:, :width].astype(F32)
    grads, g_sqk = attend_back(
        meta, queries, qrot, attended, inverse_mass, g_att, keys, vals, krot, kpos_cols, cosine, sine, sqk, docs
    )
    if lax.axis_size("dp") == 8:
        both = jnp.stack([m, lax.axis_index("dp").astype(jnp.int32) & 1])
        half_sum, sent = attn_grads(both, x_first, x_second, grads, out_sum, over_out)
        half_sum = half_sum + swap(sent, "dp", 1).astype(F32)
    else:
        sent = dot(x_first, grads[: 2 * local], 0, 0) + dot(x_second, grads[2 * local :], 0, 0)
        half_sum = jnp.concatenate([sent, out_sum + over_out.astype(F32)], axis=1)
    mlp_squares = jnp.sum(grad_mlp * grad_mlp)
    second_tokens = to_tokens(after(grads, sent), 1, attn, BF16)
    to_core = swap(second_tokens, "mp", 1)
    partial = to_tokens(after(grads, second_tokens), 0, attn, F32)
    for_x = (partial[local:] + to_core[local:].astype(F32)).astype(BF16)
    to_x = swap(for_x, "mp", 2)

    def placed(array, index):
        slots = lax.broadcasted_iota(jnp.int32, (4, 1), 0)
        return jnp.where(slots == index, array[None], 0.0)

    def quarters(by):
        return placed(by[0, 0], m & 2) + placed(by[1, 0], (m & 2) + 1)

    bu, bg, g_sqk, by_one, by_two, _ = lax.optimization_barrier((bu, bg, g_sqk, by_one, by_two, second_tokens))
    rows = [quarters(bu), quarters(bg), placed(g_sqk[0], m), by_one[0], by_two[0]]
    rows = [row.reshape(devices, -1) for row in rows]
    small = jnp.sum(to_all(after(jnp.concatenate(rows, axis=1), for_x)), axis=0)
    cuts, start = [], 0
    for row in rows:
        cuts.append(small[start : start + row.shape[1]])
        start += row.shape[1]
    g_sup, g_sgate, g_sqk, g_alpha_one, g_alpha_two = cuts

    def squared(*arrays):
        return sum(jnp.sum(array * array) for array in arrays)

    grad_attn = scatter_z(after(half_sum, for_x))
    squares = mlp_squares + squared(grad_attn, small)
    g_qkv = [grad_attn[:, i * width : (i + 1) * width] for i in range(3)]
    grad_down, grad_out = turned(after(grad_down, squares)), turned(after(grad_attn, squares)[:, 3 * width :])
    to_x = after(to_x, squares)
    grad_tokens = grad_x + partial[:local] + to_core[:local].astype(F32) + to_x.astype(F32)
    pieces = tuple(g_qkv) + (grad_out, grad_up, grad_gate, grad_down)
    pieces = pieces + (g_sqk, g_sup, g_sgate, g_alpha_one, g_alpha_two)
    squares = jnp.sum(to_all(jnp.broadcast_to(squares, (devices, 128))), axis=0)
    grad_norm = jnp.sqrt(squares[0])
    mean_alphas = jnp.stack([jnp.mean(alpha_one), jnp.mean(alpha_two)])
    return (result, grad_tokens) + pieces + (grad_norm, mean_alphas)


def solution(mesh):
    both_axes = P(("dp", "mp"))
    rows = P(("dp", "mp"), None)
    in_specs = (
        (rows, rows, P("dp", None), P("dp", None))
        + (P("dp", "mp"),) * 3
        + (P("mp", "dp"),)
        + (P("dp", "mp"),) * 2
        + (P("mp", "dp"),)
        + (both_axes,) * 5
    )
    out_specs = (
        (rows, rows)
        + (P("dp", "mp"),) * 3
        + (P("mp", "dp"),)
        + (P("dp", "mp"),) * 2
        + (P("mp", "dp"),)
        + (both_axes,) * 5
        + (P(), P())
    )
    return jax.shard_map(shards, mesh=mesh, in_specs=in_specs, out_specs=out_specs, check_vma=False)
```
